32 devices in a mesh: groups: 2 (over y), seq: 4 (over z), head: 2 (over x), sub: 2 (over core).
Axes of the slice: x: 2, y: 2, z: 4, core: 2. Of those that a mesh axis runs over, the one named last changes fastest.
Arguments:
- queries: bfloat16 [2048, 2048], P(('groups', 'seq'), ('head', 'sub')), parts along dimension 0, may hold values from -8 to 8, as said below
- key_rows: bfloat16 [2048, 2048], P(('groups', 'seq'), ('head', 'sub')), parts along dimension 0, may hold values from -5 to 5
- values: bfloat16 [2048, 2048], P(('groups', 'seq'), ('head', 'sub')), parts along dimension 0, may hold values from -18 to 18
- grad_out: bfloat16 [2048, 2048], P(('groups', 'seq'), ('head', 'sub')), parts along dimension 0, may hold values from -9 to 9
- window_width: int32 [32], P(('groups', 'head', 'sub')), parts along dimension 0, may hold values from 0 to 1, as said below
- global_blocks: int32 [4], P('groups'), parts along dimension 0, may hold values from 0 to 7, as said below
- random_blocks: int32 [32, 8, 3], P(('groups', 'head', 'sub'), 'seq'), parts along dimension 0, may hold values from 0 to 7, as said below
Outputs:
- attn_out: bfloat16 [2048, 2048], P(('groups', 'seq'), ('head', 'sub')), parts along dimension 0
- grad_query: bfloat16 [2048, 2048], P(('groups', 'seq'), ('head', 'sub')), parts along dimension 0
- grad_key: bfloat16 [2048, 2048], P(('groups', 'seq'), ('head', 'sub')), parts along dimension 0
- grad_value: bfloat16 [2048, 2048], P(('groups', 'seq'), ('head', 'sub')), parts along dimension 0
The draws below stay inside these ranges and needn't reach their ends.
There are 2 independent parts, one for each index of `groups`. The reference program is written for one: setup_inputs(seed, part) draws one part's arguments, and reference() takes and returns one part's arrays. A program takes and returns all parts, laid end to end along the dimension named above; each array names one. Nothing has to cross between parts.
Inputs may be any that keep to these rules, and one draw needn't show every extreme that they name: queries of the hidden draw lie within the same range. `window_width`: in each group of 4 heads (h // 4 equal) some head has width 1. `global_blocks`: the 2 indices are distinct. `random_blocks`: for one group of 4 heads (h // 4 equal) and one run of 2 query blocks (b // 2 equal), at most 6 of the 24 entries name key blocks c with the same c // 2, and exactly 6 do for one value of c // 2.
All inputs are finite; a program needn't handle non-finite values.
Results may differ from the reference program's by a relative error of at most 0.028.
Values may be sent and summed in bfloat16 or wider, within the bound.
A program may use at most 128 MiB of HBM per device.

```python
import math
import jax
import jax.numpy as jnp
from jax import lax

HEADS = 16
HD = 128
BLK = 128
WMAX = 1
NG = 2
NR = 3
QB = 2
HEADS_DEV = 4
NBLK = 8
SEQ = 1024
NL = 8
REQ = 24
CAP = 6
N_SEQ = 4


def draw_queries(key, part):
    shape_all = (NBLK, BLK, HEADS * HD)
    base = jnp.clip(2.0 * jax.random.normal(jax.random.fold_in(key, 1), shape_all, jnp.float32), -8.0, 8.0)
    return base.reshape(SEQ, HEADS * HD).astype(jnp.bfloat16)


def draw_key_rows(key, part):
    shape_all = (NBLK, BLK, HEADS * HD)
    base = jnp.clip(jax.random.normal(jax.random.fold_in(key, 2), shape_all, jnp.float32), -5.0, 5.0)
    return base.reshape(SEQ, HEADS * HD).astype(jnp.bfloat16)


def draw_window_width(key, part):
    first_key, second_key = jax.random.split(jax.random.fold_in(key, 3))
    widths = jax.random.randint(first_key, (HEADS,), 0, WMAX + 1)
    group_total = HEADS // HEADS_DEV
    chosen = jax.random.randint(second_key, (group_total,), 0, HEADS_DEV)
    position = jnp.arange(HEADS)
    forced = position % HEADS_DEV == jnp.repeat(chosen, HEADS_DEV)
    return jnp.where(forced, WMAX, widths).astype(jnp.int32)


def draw_global_blocks(key, part):
    return jax.random.permutation(jax.random.fold_in(key, 4), NBLK)[:NG].astype(jnp.int32)


def draw_random_blocks(key, part):
    group_total = HEADS // HEADS_DEV
    key_table = jax.random.split(jax.random.fold_in(key, 5), group_total * N_SEQ)

    def one_device(device_key):
        subkeys = jax.random.split(device_key, 4)
        ordering = jax.random.permutation(subkeys[0], N_SEQ)
        remaining = jax.random.permutation(subkeys[1], (N_SEQ - 1) * CAP)[:REQ - CAP] // CAP + 1
        targets = jnp.concatenate([jnp.full((CAP,), ordering[0], jnp.int32), ordering[remaining].astype(jnp.int32)])
        targets = targets[jax.random.permutation(subkeys[2], REQ)]
        local_pick = jax.random.randint(subkeys[3], (REQ,), 0, QB)
        return (targets * QB + local_pick).astype(jnp.int32).reshape(HEADS_DEV, QB, NR)
    tiled = jax.vmap(one_device)(key_table).reshape(group_total, N_SEQ, HEADS_DEV, QB, NR)
    return tiled.transpose(0, 2, 1, 3, 4).reshape(HEADS, NBLK, NR)


def shard_levels(stream_key, extent, pieces, smallest, largest):
    def one(dim, shards_of):
        heights = jax.random.uniform(jax.random.fold_in(jax.random.fold_in(stream_key, 6), dim), (shards_of,), jnp.float32, smallest / len(pieces), largest / len(pieces))
        return jnp.repeat(jnp.exp(heights), extent[dim] // shards_of).reshape((-1,) + (1,) * (len(extent) - dim - 1))

    level = one(*pieces[0])
    for cut in pieces[1:]:
        level = level * one(*cut)
    return level


def scatter_about(own_key, dims, scale, most, cuts=(), kind=jnp.bfloat16):
    level = shard_levels(own_key, dims, cuts, -0.22, 0.18) if cuts else 1.0
    drawn = jax.random.normal(own_key, dims, jnp.float32) * scale * level
    return jnp.minimum(jnp.maximum(drawn, -most), most).astype(kind)


def setup_inputs(seed: int = 0, part: int = 0) -> dict:
    streams_of = jax.random.split(jax.random.key(seed), 8)
    part_splits = jax.random.split(jax.random.fold_in(streams_of[7], part), 8)
    return {
        "queries": draw_queries(jax.random.fold_in(jax.random.fold_in(streams_of[7], part), 71), part),
        "key_rows": draw_key_rows(jax.random.fold_in(jax.random.fold_in(streams_of[7], part), 71), part),
        "values": scatter_about(part_splits[2], (SEQ, HEADS * HD), 3.0, 18.0, ((0, 4), (1, 4))),
        "grad_out": scatter_about(part_splits[3], (SEQ, HEADS * HD), 1.5, 9.0, ((0, 4), (1, 4))),
        "window_width": draw_window_width(jax.random.fold_in(jax.random.fold_in(streams_of[7], part), 71), part),
        "global_blocks": draw_global_blocks(jax.random.fold_in(jax.random.fold_in(streams_of[7], part), 71), part),
        "random_blocks": draw_random_blocks(jax.random.fold_in(jax.random.fold_in(streams_of[7], part), 71), part),
    }


def reference(queries, key_rows, values, grad_out, window_width, global_blocks, random_blocks):
    span = 2 * WMAX + 1
    fixed_count = span + NG
    logit_scale = 1.0 / math.sqrt(HD)
    peak_precision = lax.Precision.HIGHEST

    def head_major(tensor):
        return tensor.reshape(NBLK, BLK, HEADS, HD).transpose(2, 0, 1, 3)

    def token_major(tensor):
        return tensor.transpose(1, 2, 0, 3).reshape(SEQ, HEADS * HD)
    block_ids = jnp.arange(NBLK, dtype=jnp.int32)
    offsets = jnp.arange(span, dtype=jnp.int32) - WMAX
    reach = block_ids[:, None] + offsets[None, :]
    in_range = (reach >= 0) & (reach < NBLK)
    reach_clip = jnp.clip(reach, 0, NBLK - 1).astype(jnp.int32)
    fixed_index = jnp.concatenate([reach_clip, jnp.broadcast_to(global_blocks[None, :], (NBLK, NG)).astype(jnp.int32)], axis=1)
    row_global = jnp.any(block_ids[:, None] == global_blocks[None, :], axis=1)

    def one_head(operands):
        query_h, key_h, value_h, grad_h, width_h, random_h = operands
        list_index = jnp.concatenate([fixed_index, random_h.astype(jnp.int32)], axis=1)
        valid = jnp.concatenate([in_range & (jnp.abs(offsets)[None, :] <= width_h), jnp.ones((NBLK, NG + NR), jnp.bool_)], axis=1)
        key_sequence = key_h[list_index].reshape(NBLK, NL * BLK, HD).astype(jnp.float32)
        value_sequence = value_h[list_index].reshape(NBLK, NL * BLK, HD).astype(jnp.float32)
        list_mask = jnp.repeat(valid, BLK, axis=1)[:, None, :]
        broad_query = query_h.astype(jnp.float32)
        broad_gradient = grad_h.astype(jnp.float32)
        score_matrix = jnp.einsum('fts,fzs->ftz', broad_query, key_sequence, precision=peak_precision) * logit_scale
        score_matrix = jnp.where(list_mask, score_matrix, -jnp.inf)
        row_max = lax.optimization_barrier(jnp.max(score_matrix, axis=-1))
        weights = jnp.exp(score_matrix - row_max[..., None])
        totals = lax.optimization_barrier(jnp.sum(weights, axis=-1))
        weight_reduced = lax.optimization_barrier(weights.astype(jnp.bfloat16)).astype(jnp.float32)
        accumulated_total = jnp.einsum('zou,zuc->zoc', weight_reduced, value_sequence, precision=peak_precision)
        sparse_out = (accumulated_total / totals[..., None]).astype(jnp.bfloat16)
        sparse_lse = row_max + jnp.log(totals)
        glob_query = query_h[global_blocks].reshape(NG * BLK, HD)
        glob_grad = grad_h[global_blocks].reshape(NG * BLK, HD)
        all_keys = key_h.reshape(SEQ, HD)
        all_values = value_h.reshape(SEQ, HD)
        glob_scores = jnp.dot(glob_query, all_keys.T, preferred_element_type=jnp.float32) * logit_scale
        glob_max = lax.optimization_barrier(jnp.max(glob_scores, axis=-1))
        glob_weights = jnp.exp(glob_scores - glob_max[:, None])
        glob_total = lax.optimization_barrier(jnp.sum(glob_weights, axis=-1))
        glob_sum = jnp.dot(glob_weights.astype(jnp.bfloat16), all_values, preferred_element_type=jnp.float32)
        glob_out = (glob_sum / glob_total[:, None]).astype(jnp.bfloat16)
        glob_lse = glob_max + jnp.log(glob_total)
        out_head = sparse_out.at[global_blocks].set(glob_out.reshape(NG, BLK, HD))
        delta = lax.optimization_barrier(jnp.sum(broad_gradient * out_head.astype(jnp.float32), axis=-1))
        row_lse = jnp.where(row_global[:, None], jnp.inf, sparse_lse)
        probs = jnp.where(list_mask, jnp.exp(score_matrix - row_lse[..., None]), 0.0)
        probability_reduced = lax.optimization_barrier(probs.astype(jnp.bfloat16)).astype(jnp.float32)
        probability_gradient = jnp.einsum('fts,fzs->ftz', broad_gradient, value_sequence, precision=peak_precision)
        score_gradient = lax.optimization_barrier((probs * (probability_gradient - delta[..., None])).astype(jnp.bfloat16)).astype(jnp.float32)
        gradient_row_values = jnp.einsum('zou,zuc->zoc', score_gradient, key_sequence, precision=peak_precision) * logit_scale
        key_contributions = jnp.einsum('uxe,uxf->uef', score_gradient, broad_query, precision=peak_precision) * logit_scale
        value_contributions = jnp.einsum('uxe,uxf->uef', probability_reduced, broad_gradient, precision=peak_precision)
        terms = jnp.concatenate([key_contributions, value_contributions], axis=-1).reshape(NBLK, NL, BLK, 2 * HD)
        pair_grads = jnp.zeros((NBLK, BLK, 2 * HD), jnp.float32).at[list_index[:, :fixed_count]].add(terms[:, :fixed_count])
        rounded = lax.optimization_barrier(terms[:, fixed_count:].astype(jnp.bfloat16)).astype(jnp.float32)
        pair_grads = pair_grads.at[list_index[:, fixed_count:]].add(rounded)
        glob_probs = jnp.exp(glob_scores - glob_lse[:, None])
        glob_delta = lax.optimization_barrier(jnp.sum(glob_grad.astype(jnp.float32) * glob_out.astype(jnp.float32), axis=-1))
        glob_grad_probs = jnp.dot(glob_grad, all_values.T, preferred_element_type=jnp.float32)
        glob_grad_scores = (glob_probs * (glob_grad_probs - glob_delta[:, None])).astype(jnp.bfloat16)
        glob_rows = jnp.dot(glob_grad_scores, all_keys, preferred_element_type=jnp.float32) * logit_scale
        key_from_glob = jnp.dot(glob_grad_scores.T, glob_query, preferred_element_type=jnp.float32) * logit_scale
        value_from_glob = jnp.dot(glob_probs.astype(jnp.bfloat16).T, glob_grad, preferred_element_type=jnp.float32)
        pair_grads = pair_grads + jnp.concatenate([key_from_glob, value_from_glob], axis=-1).reshape(NBLK, BLK, 2 * HD)
        gradient_row_values = gradient_row_values.at[global_blocks].add(glob_rows.reshape(NG, BLK, HD))
        return (out_head, gradient_row_values.astype(jnp.bfloat16), pair_grads[..., :HD].astype(jnp.bfloat16), pair_grads[..., HD:].astype(jnp.bfloat16))
    results = lax.map(one_head, (head_major(queries), head_major(key_rows), head_major(values), head_major(grad_out), window_width, random_blocks))
    return (token_major(results[0]), token_major(results[1]), token_major(results[2]), token_major(results[3]))
```

```python
import functools
import math

import jax
import jax.numpy as jnp
from jax import lax
from jax.experimental import pallas as pl
from jax.experimental.pallas import tpu as pltpu
from jax.sharding import PartitionSpec as P

BLK = 128
WMAX = 1


def extended(cells, sides, width):
    for axis, dim in sides:
        count = lax.axis_size(axis)
        ends = count - 1
        head = lax.slice_in_dim(cells, 0, width, axis=dim)
        tail = lax.slice_in_dim(cells, cells.shape[dim] - width, cells.shape[dim], axis=dim)
        cells = jnp.concatenate(
            [
                lax.ppermute(tail, axis, [(i, (i + 1) % count) for i in range(ends)]),
                cells,
                lax.ppermute(head, axis, [((i + 1) % count, i) for i in range(ends)]),
            ],
            axis=dim,
        )
    return cells


def from_behind(block, axis, distance):
    devices = range(lax.axis_size(axis))
    route = [(i - distance, i) for i in devices if i - distance in devices]
    return lax.ppermute(block, axis, route)


def head_major(tensor, head_count, head_width):
    block_count = tensor.shape[0] // BLK
    return tensor.reshape(block_count, BLK, head_count, head_width).transpose(2, 0, 1, 3)


def token_major(tensor):
    head_count, block_count, row_count, head_width = tensor.shape
    return tensor.transpose(1, 2, 0, 3).reshape(block_count * row_count, head_count * head_width)


def on_device(queries, key_rows, values, grad_out, window_width, global_blocks, random_blocks):
    head_count = window_width.shape[0]
    tokens = queries.shape[0]
    head_width = queries.shape[1] // head_count
    blocks = tokens // BLK
    span = 2 * WMAX + 1
    globals_count = global_blocks.shape[0]
    randoms = random_blocks.shape[2]
    shards = lax.axis_size("seq")
    my_index = lax.axis_index("seq")
    logit_scale = 1.0 / math.sqrt(head_width)
    group = 2
    group_count = blocks // group
    pair_width = 2 * head_width
    query_heads = head_major(queries, head_count, head_width)
    grad_heads = head_major(grad_out, head_count, head_width)
    packed = jnp.concatenate([key_rows, values], axis=1)
    padded = extended(packed, (("seq", 0),), WMAX * BLK)
    pair_heads = (
        padded.reshape(blocks + 2 * WMAX, BLK, 2, head_count, head_width)
        .transpose(3, 0, 1, 2, 4)
        .reshape(head_count, blocks + 2 * WMAX, BLK, pair_width)
    )
    local_pairs = pair_heads[:, WMAX : WMAX + blocks]
    owners = global_blocks // blocks
    local_spot = global_blocks % blocks
    stacked = jnp.concatenate([queries, key_rows, values, grad_out], axis=1)
    own_rows = jnp.stack(
        [
            lax.dynamic_slice_in_dim(stacked, local_spot[glob_index] * BLK, BLK, 0)
            for glob_index in range(globals_count)
        ]
    )
    owned_mask = (owners == my_index)[:, None, None]
    masked_rows = jnp.where(owned_mask, own_rows, jnp.zeros((), jnp.bfloat16))
    panels = lax.psum(masked_rows, "seq").astype(jnp.float32).astype(jnp.bfloat16)
    panel_heads = panels.reshape(globals_count, BLK, 4, head_count, head_width).transpose(
        2, 3, 0, 1, 4
    )
    glob_query = panel_heads[0]
    glob_grad = panel_heads[3]
    glob_pairs = jnp.concatenate([panel_heads[1], panel_heads[2]], axis=-1)
    requests = random_blocks.reshape(-1)
    request_count = requests.shape[0]
    capacity = max(2, -(-request_count // shards))
    targets = requests // blocks
    request_head = jnp.arange(request_count, dtype=jnp.int32) // (blocks * randoms)
    codes = request_head * blocks + requests % blocks
    positions = jnp.arange(request_count, dtype=jnp.int32)
    earlier = (targets[:, None] == targets[None, :]) & (positions[None, :] < positions[:, None])
    ranks = jnp.sum(earlier.astype(jnp.int32), axis=1)
    slots = targets * capacity + ranks
    outgoing = jnp.full((shards * capacity,), -1, jnp.int32).at[slots].set(codes)
    incoming = lax.all_to_all(
        outgoing.reshape(shards, capacity), "seq", split_axis=0, concat_axis=0, tiled=True
    ).reshape(-1)
    code_hits = (
        incoming[:, None] == jnp.arange(head_count * blocks, dtype=jnp.int32)[None, :]
    ).astype(jnp.bfloat16)
    flat_pairs = local_pairs.reshape(head_count * blocks, BLK, pair_width)
    reply = jnp.einsum(
        "sc,cid->sid", code_hits, flat_pairs, preferred_element_type=jnp.float32
    ).astype(jnp.bfloat16)
    fetched = lax.all_to_all(
        reply.reshape(shards, capacity, BLK, pair_width),
        "seq",
        split_axis=0,
        concat_axis=0,
        tiled=True,
    )
    slot_hits = (
        slots[:, None] == jnp.arange(shards * capacity, dtype=jnp.int32)[None, :]
    ).astype(jnp.bfloat16)
    random_pairs = (
        jnp.einsum(
            "rs,sid->rid",
            slot_hits,
            fetched.reshape(shards * capacity, BLK, pair_width),
            preferred_element_type=jnp.float32,
        )
        .astype(jnp.bfloat16)
        .reshape(head_count, blocks, randoms, BLK, pair_width)
    )
    offsets = jnp.arange(span, dtype=jnp.int32) - WMAX
    block_ids = my_index * blocks + jnp.arange(blocks, dtype=jnp.int32)
    reach = block_ids[:, None] + offsets[None, :]
    in_range = (reach >= 0) & (reach < shards * blocks)
    window_ok = in_range[None, :, :] & (
        jnp.abs(offsets)[None, None, :] <= window_width[:, None, None]
    )
    list_ok = jnp.concatenate(
        [window_ok, jnp.ones((head_count, blocks, globals_count + randoms), jnp.bool_)], axis=2
    )
    global_hit = block_ids[:, None] == global_blocks[None, :]
    row_global = jnp.any(global_hit, axis=1)
    hit_weight = global_hit.astype(jnp.float32)

    def key_sequence(first_block):
        pieces_list = [
            jnp.stack(
                [
                    lax.dynamic_slice_in_dim(pair_heads, first_block + offset, group, 1)
                    for offset in range(span)
                ],
                axis=2,
            )
        ]
        pieces_list.append(
            jnp.broadcast_to(
                glob_pairs[:, None], (head_count, group, globals_count, BLK, pair_width)
            )
        )
        pieces_list.append(random_pairs)
        joined = jnp.concatenate(pieces_list, axis=2)
        entry_count = joined.shape[2]
        list_mask = list_ok[:, :, :entry_count]
        return (
            joined.reshape(head_count, group, entry_count * BLK, pair_width),
            jnp.repeat(list_mask, BLK, axis=2),
        )

    def forward_group(group_index):
        first_block = group_index * group
        pairs, list_mask = key_sequence(first_block)
        key_part = pairs[..., :head_width]
        value_part = pairs[..., head_width:]
        score_matrix = (
            jnp.einsum("hqid,hqkd->hqik", query_heads, key_part, preferred_element_type=jnp.float32)
            * logit_scale
        )
        score_matrix = jnp.where(list_mask[:, :, None, :], score_matrix, -jnp.inf)
        row_max = jnp.max(score_matrix, axis=-1)
        weights = jnp.exp(score_matrix - row_max[..., None])
        totals = jnp.sum(weights, axis=-1)
        accumulated_total = jnp.einsum(
            "hqik,hqkd->hqid",
            weights.astype(jnp.bfloat16),
            value_part,
            preferred_element_type=jnp.float32,
        )
        return (
            (accumulated_total / totals[..., None]).astype(jnp.bfloat16),
            row_max + jnp.log(totals),
        )

    sparse_out, sparse_lse = lax.map(forward_group, jnp.arange(group_count))
    sparse_out = jnp.moveaxis(sparse_out, 0, 1).reshape(head_count, blocks, BLK, head_width)
    sparse_lse = jnp.moveaxis(sparse_lse, 0, 1).reshape(head_count, blocks, BLK)
    local_keys = local_pairs[..., :head_width].reshape(head_count, blocks * BLK, head_width)
    local_values = local_pairs[..., head_width:].reshape(head_count, blocks * BLK, head_width)
    glob_rows = glob_query.reshape(head_count, globals_count * BLK, head_width)
    glob_grad_rows = glob_grad.reshape(head_count, globals_count * BLK, head_width)
    glob_scores = (
        jnp.einsum("hid,hjd->hij", glob_rows, local_keys, preferred_element_type=jnp.float32)
        * logit_scale
    )
    glob_max = lax.pmax(jnp.max(glob_scores, axis=-1), "seq")
    glob_weights = jnp.exp(glob_scores - glob_max[..., None])
    glob_part_sum = jnp.einsum(
        "hij,hjd->hid",
        glob_weights.astype(jnp.bfloat16),
        local_values,
        preferred_element_type=jnp.float32,
    )
    glob_sum, glob_total = lax.psum((glob_part_sum, jnp.sum(glob_weights, axis=-1)), "seq")
    glob_out = (glob_sum / glob_total[..., None]).astype(jnp.bfloat16)
    glob_lse = glob_max + jnp.log(glob_total)
    chosen_out = jnp.einsum(
        "bg,hgid->hbid",
        hit_weight,
        glob_out.reshape(head_count, globals_count, BLK, head_width).astype(jnp.float32),
    )
    out_heads = jnp.where(
        row_global[None, :, None, None], chosen_out.astype(jnp.bfloat16), sparse_out
    )
    attn_out = token_major(out_heads)
    delta = jnp.sum(grad_heads.astype(jnp.float32) * out_heads.astype(jnp.float32), axis=-1)
    row_lse = jnp.where(row_global[None, :, None], jnp.inf, sparse_lse)
    glob_delta = jnp.sum(glob_grad_rows.astype(jnp.float32) * glob_out.astype(jnp.float32), axis=-1)

    def backward_group(group_index):
        first_block = group_index * group
        pairs, list_mask = key_sequence(first_block)
        key_part = pairs[..., :head_width]
        value_part = pairs[..., head_width:]
        score_matrix = (
            jnp.einsum("hqid,hqkd->hqik", query_heads, key_part, preferred_element_type=jnp.float32)
            * logit_scale
        )
        probs = jnp.where(list_mask[:, :, None, :], jnp.exp(score_matrix - row_lse[..., None]), 0.0)
        probability_gradient = jnp.einsum(
            "hqid,hqkd->hqik", grad_heads, value_part, preferred_element_type=jnp.float32
        )
        score_gradient = (probs * (probability_gradient - delta[..., None])).astype(jnp.bfloat16)
        grad_rows_part = (
            jnp.einsum(
                "hqik,hqkd->hqid", score_gradient, key_part, preferred_element_type=jnp.float32
            )
            * logit_scale
        )
        key_contributions = (
            jnp.einsum(
                "hqik,hqid->hqkd", score_gradient, query_heads, preferred_element_type=jnp.float32
            )
            * logit_scale
        )
        value_contributions = jnp.einsum(
            "hqik,hqid->hqkd",
            probs.astype(jnp.bfloat16),
            grad_heads,
            preferred_element_type=jnp.float32,
        )
        terms = jnp.concatenate([key_contributions, value_contributions], axis=-1).reshape(
            head_count, group, -1, BLK, pair_width
        )
        window_terms = terms[:, :, :span]
        glob_terms = jnp.sum(terms[:, :, span : span + globals_count], axis=1)
        random_terms = terms[:, :, span + globals_count :].astype(jnp.bfloat16)
        return (grad_rows_part, window_terms, glob_terms, random_terms)

    gradient_row_values, window_terms, glob_terms, random_terms = lax.map(
        backward_group, jnp.arange(group_count)
    )
    gradient_row_values = jnp.moveaxis(gradient_row_values, 0, 1).reshape(
        head_count, blocks, BLK, head_width
    )
    window_terms = jnp.moveaxis(window_terms, 0, 1).reshape(
        head_count, blocks, span, BLK, pair_width
    )
    glob_terms = jnp.sum(glob_terms, axis=0)
    spread = jnp.zeros((head_count, blocks + 2 * WMAX, BLK, pair_width), jnp.float32)
    for offset in range(span):
        spread = spread.at[:, offset : offset + blocks].add(window_terms[:, :, offset])
    glob_probs = jnp.exp(glob_scores - glob_lse[..., None])
    glob_grad_probs = jnp.einsum(
        "hid,hjd->hij", glob_grad_rows, local_values, preferred_element_type=jnp.float32
    )
    glob_grad_scores = (glob_probs * (glob_grad_probs - glob_delta[..., None])).astype(jnp.bfloat16)
    glob_query_part = (
        jnp.einsum("hij,hjd->hid", glob_grad_scores, local_keys, preferred_element_type=jnp.float32)
        * logit_scale
    )
    key_from_glob = (
        jnp.einsum("hij,hid->hjd", glob_grad_scores, glob_rows, preferred_element_type=jnp.float32)
        * logit_scale
    )
    value_from_glob = jnp.einsum(
        "hij,hid->hjd",
        glob_probs.astype(jnp.bfloat16),
        glob_grad_rows,
        preferred_element_type=jnp.float32,
    )
    glob_total_terms, glob_query_grad = lax.psum((glob_terms, glob_query_part), "seq")
    from_below = from_behind(spread[:, blocks + WMAX :], "seq", 1)
    from_above = from_behind(spread[:, :WMAX].astype(jnp.bfloat16), "seq", -1).astype(jnp.float32)
    own_terms = spread[:, WMAX : WMAX + blocks]
    own_terms = own_terms.at[:, :WMAX].add(from_below).at[:, blocks - WMAX :].add(from_above)
    own_terms = own_terms + jnp.concatenate([key_from_glob, value_from_glob], axis=-1).reshape(
        head_count, blocks, BLK, pair_width
    )
    own_terms = own_terms + jnp.einsum("bg,hgid->hbid", hit_weight, glob_total_terms)
    random_terms = jnp.moveaxis(random_terms, 0, 1).reshape(request_count, BLK, pair_width)
    outgoing_terms = (
        jnp.zeros((shards * capacity, BLK, pair_width), jnp.bfloat16).at[slots].set(random_terms)
    )
    returned = lax.all_to_all(
        outgoing_terms.reshape(shards, capacity, BLK, pair_width),
        "seq",
        split_axis=0,
        concat_axis=0,
        tiled=True,
    ).reshape(shards * capacity, BLK, pair_width)
    random_add = jnp.einsum(
        "sc,sid->cid", code_hits, returned, preferred_element_type=jnp.float32
    ).reshape(head_count, blocks, BLK, pair_width)
    own_terms = own_terms + random_add
    glob_query_add = jnp.einsum(
        "bg,hgid->hbid",
        hit_weight,
        glob_query_grad.reshape(head_count, globals_count, BLK, head_width),
    )
    grad_query = token_major((gradient_row_values + glob_query_add).astype(jnp.bfloat16))
    grad_key = token_major(own_terms[..., :head_width].astype(jnp.bfloat16))
    grad_value = token_major(own_terms[..., head_width:].astype(jnp.bfloat16))
    return (attn_out, grad_query, grad_key, grad_value)


MASKED = -1e30
ALIGNED = pl.DeviceIdType.MESH


NEXT, ACROSS, SKIP = 0, 1, 2
EARLY = (0, 1, 2, 3)
INNER_SENDS = ((0, SKIP), (1, SKIP), (0, NEXT), (1, NEXT), (2, SKIP), (3, SKIP), (2, NEXT), (3, NEXT))
OUTER_SENDS = ((0, ACROSS), (1, ACROSS), (0, SKIP), (1, SKIP), (0, NEXT), (1, NEXT), (2, ACROSS), (3, ACROSS), (2, SKIP), (3, SKIP), (2, NEXT), (3, NEXT))
TURNS = ((ACROSS, ACROSS), None, (NEXT, SKIP), (SKIP, NEXT))
LAST = ((ACROSS, SKIP), (SKIP, ACROSS), (NEXT, NEXT))


def rows_dot(left, right):
    return lax.dot_general(left, right, (((1,), (1,)), ((), ())), preferred_element_type=jnp.float32)


def one_head_kernel(
    shards,
    blocks,
    width_in,
    global_in,
    random_in,
    q_in,
    k_in,
    v_in,
    g_in,
    o_out,
    dq_out,
    dk_out,
    dv_out,
    width_ref,
    global_ref,
    random_ref,
    q_all,
    k_all,
    v_all,
    g_all,
    bias_own,
    bias_all,
    o_all,
    dq_all,
    dk_all,
    dv_all,
    dk_sum,
    dv_sum,
    small_sem,
    in_send,
    in_recv,
    in_local,
    bias_send,
    bias_recv,
    out_send,
    out_recv,
    out_local,
):
    me = lax.axis_index("seq")
    rows = blocks * BLK
    key_blocks = shards * blocks
    hd = q_all.shape[1]
    logit_scale = 1.0 / math.sqrt(hd)
    inner = ((me + 1) // 2) % 2
    partner = (me + 1 - 2 * (me % 2), 3 - me, (me + 2) % 4)

    def pick(pair, table):
        first, second = table[pair[0]], table[pair[1]]
        return first + (second - first) * inner

    def cols(index):
        return pl.ds(pl.multiple_of(index * hd, hd), hd)

    def span(index):
        return pl.ds(pl.multiple_of(index * rows, rows), rows)

    inputs = ((k_in, k_all), (v_in, v_all), (q_in, q_all), (g_in, g_all))
    outputs = ((o_all, o_out), (dq_all, dq_out), (dk_all, dk_out), (dv_all, dv_out))

    def send_in(slot, step, target):
        source, landing = inputs[slot]
        return pltpu.make_async_remote_copy(
            src_ref=source.at[:, cols(target)],
            dst_ref=landing.at[span(me), :],
            send_sem=in_send.at[slot, step],
            recv_sem=in_recv.at[slot, step],
            device_id={"seq": target},
            device_id_type=ALIGNED,
        )

    def send_bias(step, target):
        return pltpu.make_async_remote_copy(
            src_ref=bias_own.at[target],
            dst_ref=bias_all.at[me],
            send_sem=bias_send.at[step],
            recv_sem=bias_recv.at[step],
            device_id={"seq": target},
            device_id_type=ALIGNED,
        )

    def send_out(slot, step, target):
        source, landing = outputs[slot]
        return pltpu.make_async_remote_copy(
            src_ref=source.at[span(target), :],
            dst_ref=landing.at[:, cols(me)],
            send_sem=out_send.at[slot, step],
            recv_sem=out_recv.at[slot, step],
            device_id={"seq": target},
            device_id_type=ALIGNED,
        )

    small = [
        pltpu.make_async_copy(source, landing, small_sem.at[index])
        for index, (source, landing) in enumerate(
            ((width_in, width_ref), (global_in, global_ref), (random_in, random_ref))
        )
    ]
    local_in = [
        pltpu.make_async_copy(source.at[:, cols(me)], landing.at[span(me), :], in_local.at[slot])
        for slot, (source, landing) in enumerate(inputs)
    ]
    local_out = [
        pltpu.make_async_copy(source.at[span(me), :], landing.at[:, cols(me)], out_local.at[slot])
        for slot, (source, landing) in enumerate(outputs)
    ]

    barrier = pltpu.get_barrier_semaphore()

    def greet(device):
        pl.semaphore_signal(barrier, inc=1, device_id={"seq": device}, device_id_type=ALIGNED)

    greet(3 - me)
    for copy in small:
        copy.start()

    @pl.when(inner == 1)
    def _():
        pl.semaphore_wait(barrier, 1)
        for slot in EARLY:
            send_in(slot, ACROSS, partner[ACROSS]).start()
        greet(0)
        greet(3)

    for copy in local_in:
        copy.start()
    for copy in small:
        copy.wait()

    lane = lax.broadcasted_iota(jnp.int32, (1, BLK), 1)
    spot_ids = jnp.zeros_like(lane)
    for spot in range(1, blocks):
        spot_ids += jnp.where(lane >= spot * key_blocks, 1, 0)
    key_ids = lane - spot_ids * key_blocks
    block_ids = me * blocks + spot_ids
    distance = jnp.abs(key_ids - block_ids)
    listed = jnp.zeros(lane.shape, jnp.float32)
    row_global = jnp.zeros(lane.shape, jnp.float32)
    for index in range(global_ref.shape[0]):
        listed += jnp.where(key_ids == global_ref[index], 1.0, 0.0)
        row_global = jnp.maximum(row_global, jnp.where(block_ids == global_ref[index], 1.0, 0.0))
    for head in range(shards):
        hits = listed + jnp.where(distance <= jnp.minimum(width_ref[head], WMAX), 1.0, 0.0)
        for index in range(random_ref.shape[0]):
            named = jnp.zeros_like(lane)
            for spot in range(blocks):
                named = jnp.where(spot_ids == spot, random_ref[index, spot, head], named)
            hits += jnp.where(key_ids == named, 1.0, 0.0)
        hits = row_global + (1.0 - row_global) * hits
        bias_own[head] = jnp.where(
            hits > 0.5, jnp.log(jnp.maximum(hits, 1.0)) * (1.0 / math.log(2.0)), MASKED
        )

    @pl.when(inner == 0)
    def _():
        pl.semaphore_wait(barrier, 3)
        greet(1)
        greet(2)
        for step, target in enumerate(partner):
            send_bias(step, target).start()
        for slot, step in OUTER_SENDS:
            send_in(slot, step, partner[step]).start()

    @pl.when(inner == 1)
    def _():
        pl.semaphore_wait(barrier, 2)
        for step, target in enumerate(partner):
            send_bias(step, target).start()
        for slot, step in INNER_SENDS:
            send_in(slot, step, partner[step]).start()

    bias_all[me] = bias_own[me]

    sub_ids = lax.broadcasted_iota(jnp.int32, (key_blocks, BLK), 0)
    lane_ids = lax.broadcasted_iota(jnp.int32, (key_blocks, BLK), 1)

    for slot in (0, 1):
        local_in[slot].wait()
        for step in range(shards - 1):
            send_in(slot, step, partner[step]).wait_recv()
    keys = k_all[...]
    vals = v_all[...]
    keys_t = keys.T
    vals_t = vals.T
    for turn, pair in enumerate(TURNS):
        if pair is None:
            chunk = me
            local_in[2].wait()
            local_in[3].wait()
        else:
            chunk, step = pick(pair, partner), pick(pair, (NEXT, ACROSS, SKIP))
            send_in(2, step, chunk).wait_recv()
            send_in(3, step, chunk).wait_recv()
            send_bias(step, chunk).wait_recv()
        q = q_all[span(chunk), :]
        g = g_all[span(chunk), :]
        row = jnp.broadcast_to(bias_all[chunk], lane_ids.shape)
        spread = [
            jnp.broadcast_to(
                jnp.sum(
                    jnp.where(lane_ids == sub_ids + spot * key_blocks, row, 0.0),
                    axis=1,
                    keepdims=True,
                ),
                lane_ids.shape,
            )
            for spot in range(blocks)
        ]
        bias = jnp.concatenate(
            [
                jnp.concatenate(
                    [
                        jnp.broadcast_to(spread[spot][key : key + 1, :], (BLK, BLK))
                        for spot in range(blocks)
                    ],
                    axis=1,
                )
                for key in range(key_blocks)
            ],
            axis=0,
        )
        scores = rows_dot(keys, q) * (logit_scale / math.log(2.0)) + bias
        top = jnp.max(scores, axis=0, keepdims=True)
        weights = jnp.exp2(scores - top)
        inverse = 1.0 / jnp.sum(weights, axis=0, keepdims=True)
        out_t = (
            jnp.dot(vals_t, weights.astype(jnp.bfloat16), preferred_element_type=jnp.float32)
            * inverse
        )
        out_rows = out_t.T.astype(jnp.bfloat16)
        o_all[span(chunk), :] = out_rows
        delta = jnp.sum(
            (g.astype(jnp.float32) * out_rows.astype(jnp.float32)).T, axis=0, keepdims=True
        )
        probs = weights * inverse
        grads = (probs * (rows_dot(vals, g) - delta)).astype(jnp.bfloat16)
        dq_t = jnp.dot(keys_t, grads, preferred_element_type=jnp.float32) * logit_scale
        dq_all[span(chunk), :] = dq_t.T.astype(jnp.bfloat16)
        for slot in (0, 1):
            if pair is None:
                local_out[slot].start()
            else:
                send_out(slot, step, chunk).start()
        dv_part = jnp.dot(probs.astype(jnp.bfloat16), g, preferred_element_type=jnp.float32)
        dk_part = jnp.dot(grads, q, preferred_element_type=jnp.float32)
        if turn == 0:
            dv_sum[...] = dv_part
            dk_sum[...] = dk_part
        elif turn < shards - 1:
            dv_sum[...] += dv_part
            dk_sum[...] += dk_part
        else:
            dv_all[...] = (dv_sum[...] + dv_part).astype(jnp.bfloat16)
            dk_all[...] = ((dk_sum[...] + dk_part) * logit_scale).astype(jnp.bfloat16)
    for pair in LAST:
        target, step = pick(pair, partner), pick(pair, (NEXT, ACROSS, SKIP))
        for slot in (2, 3):
            send_out(slot, step, target).start()
    for slot in (2, 3):
        local_out[slot].start()
    for copy in local_out:
        copy.wait()
    for step, target in enumerate(partner):
        for slot in range(4):
            send_in(slot, step, target).wait_send()
        send_bias(step, target).wait_send()
    for step, target in enumerate(partner):
        for slot in range(4):
            send_out(slot, step, target).wait()


def deliver_kernel(*refs):
    copies = [
        pltpu.make_async_copy(refs[slot], refs[slot + 4], refs[8].at[slot]) for slot in range(4)
    ]
    for copy in copies:
        copy.start()
    for copy in copies:
        copy.wait()


def one_head(queries, key_rows, values, grad_out, window_width, global_blocks, random_blocks):
    shards = lax.axis_size("seq")
    tokens, columns = queries.shape
    hd = columns // shards
    blocks = tokens // BLK
    whole = shards * tokens
    bf16 = jnp.bfloat16
    shape = jax.ShapeDtypeStruct((tokens, columns), bf16)
    anywhere = pl.BlockSpec(memory_space=pl.ANY)
    dma = pltpu.SemaphoreType.DMA
    lists = (window_width, global_blocks, random_blocks.transpose(2, 1, 0))
    landed = pl.pallas_call(
        functools.partial(one_head_kernel, shards, blocks),
        out_shape=(shape,) * 4,
        in_specs=[anywhere] * 7,
        out_specs=(anywhere,) * 4,
        scratch_shapes=[pltpu.SMEM(array.shape, jnp.int32) for array in lists]
        + [pltpu.VMEM((whole, hd), bf16)] * 4
        + [pltpu.VMEM((shards, 1, BLK), jnp.float32)] * 2
        + [pltpu.VMEM((whole, hd), bf16)] * 4
        + [pltpu.VMEM((whole, hd), jnp.float32)] * 2
        + [
            dma((3,)),
            dma((4, shards - 1)),
            dma((4, shards - 1)),
            dma((4,)),
            dma((shards - 1,)),
            dma((shards - 1,)),
            dma((4, shards - 1)),
            dma((4, shards - 1)),
            dma((4,)),
        ],
        compiler_params=pltpu.CompilerParams(
            collective_id=0, has_side_effects=True, vmem_limit_bytes=48 * 1024 * 1024
        ),
    )(
        *(
            pltpu.with_memory_space_constraint(array, pltpu.HBM)
            for array in (*lists, queries, key_rows, values, grad_out)
        )
    )
    return pl.pallas_call(
        deliver_kernel,
        out_shape=(shape,) * 4,
        in_specs=[anywhere] * 4,
        out_specs=(anywhere,) * 4,
        scratch_shapes=[dma((4,))],
        compiler_params=pltpu.CompilerParams(vmem_limit_bytes=8 * 1024 * 1024),
    )(*landed)


def dispatch(queries, key_rows, values, grad_out, window_width, global_blocks, random_blocks):
    shards = lax.axis_size("seq")
    if shards == 4 and window_width.shape[0] == shards and queries.shape[1] == shards * BLK:
        chosen = one_head
    else:
        chosen = on_device
    return chosen(
        queries, key_rows, values, grad_out, window_width, global_blocks, random_blocks
    )


def solution(mesh):
    in_specs = (
        P(("groups", "seq"), ("head", "sub")),
        P(("groups", "seq"), ("head", "sub")),
        P(("groups", "seq"), ("head", "sub")),
        P(("groups", "seq"), ("head", "sub")),
        P(("groups", "head", "sub")),
        P("groups"),
        P(("groups", "head", "sub"), "seq", None),
    )
    out_specs = (
        P(("groups", "seq"), ("head", "sub")),
        P(("groups", "seq"), ("head", "sub")),
        P(("groups", "seq"), ("head", "sub")),
        P(("groups", "seq"), ("head", "sub")),
    )
    return jax.shard_map(
        dispatch, mesh=mesh, in_specs=in_specs, out_specs=out_specs, check_vma=False
    )
```

```python
import functools
import math

import jax
import jax.numpy as jnp
from jax import lax
from jax.experimental import pallas as pl
from jax.experimental.pallas import tpu as pltpu
from jax.sharding import PartitionSpec as P

BLK = 128
WMAX = 1


def extended(cells, sides, width):
    for axis, dim in sides:
        count = lax.axis_size(axis)
        ends = count - 1
        head = lax.slice_in_dim(cells, 0, width, axis=dim)
        tail = lax.slice_in_dim(cells, cells.shape[dim] - width, cells.shape[dim], axis=dim)
        cells = jnp.concatenate(
            [
                lax.ppermute(tail, axis, [(i, (i + 1) % count) for i in range(ends)]),
                cells,
                lax.ppermute(head, axis, [((i + 1) % count, i) for i in range(ends)]),
            ],
            axis=dim,
        )
    return cells


def from_behind(block, axis, distance):
    devices = range(lax.axis_size(axis))
    route = [(i - distance, i) for i in devices if i - distance in devices]
    return lax.ppermute(block, axis, route)


def head_major(tensor, head_count, head_width):
    block_count = tensor.shape[0] // BLK
    return tensor.reshape(block_count, BLK, head_count, head_width).transpose(2, 0, 1, 3)


def token_major(tensor):
    head_count, block_count, row_count, head_width = tensor.shape
    return tensor.transpose(1, 2, 0, 3).reshape(block_count * row_count, head_count * head_width)


def on_device(queries, key_rows, values, grad_out, window_width, global_blocks, random_blocks):
    head_count = window_width.shape[0]
    tokens = queries.shape[0]
    head_width = queries.shape[1] // head_count
    blocks = tokens // BLK
    span = 2 * WMAX + 1
    globals_count = global_blocks.shape[0]
    randoms = random_blocks.shape[2]
    shards = lax.axis_size("seq")
    my_index = lax.axis_index("seq")
    logit_scale = 1.0 / math.sqrt(head_width)
    group = 2
    group_count = blocks // group
    pair_width = 2 * head_width
    query_heads = head_major(queries, head_count, head_width)
    grad_heads = head_major(grad_out, head_count, head_width)
    packed = jnp.concatenate([key_rows, values], axis=1)
    padded = extended(packed, (("seq", 0),), WMAX * BLK)
    pair_heads = (
        padded.reshape(blocks + 2 * WMAX, BLK, 2, head_count, head_width)
        .transpose(3, 0, 1, 2, 4)
        .reshape(head_count, blocks + 2 * WMAX, BLK, pair_width)
    )
    local_pairs = pair_heads[:, WMAX : WMAX + blocks]
    owners = global_blocks // blocks
    local_spot = global_blocks % blocks
    stacked = jnp.concatenate([queries, key_rows, values, grad_out], axis=1)
    own_rows = jnp.stack(
        [
            lax.dynamic_slice_in_dim(stacked, local_spot[glob_index] * BLK, BLK, 0)
            for glob_index in range(globals_count)
        ]
    )
    owned_mask = (owners == my_index)[:, None, None]
    masked_rows = jnp.where(owned_mask, own_rows, jnp.zeros((), jnp.bfloat16))
    panels = lax.psum(masked_rows, "seq").astype(jnp.float32).astype(jnp.bfloat16)
    panel_heads = panels.reshape(globals_count, BLK, 4, head_count, head_width).transpose(
        2, 3, 0, 1, 4
    )
    glob_query = panel_heads[0]
    glob_grad = panel_heads[3]
    glob_pairs = jnp.concatenate([panel_heads[1], panel_heads[2]], axis=-1)
    requests = random_blocks.reshape(-1)
    request_count = requests.shape[0]
    capacity = max(2, -(-request_count // shards))
    targets = requests // blocks
    request_head = jnp.arange(request_count, dtype=jnp.int32) // (blocks * randoms)
    codes = request_head * blocks + requests % blocks
    positions = jnp.arange(request_count, dtype=jnp.int32)
    earlier = (targets[:, None] == targets[None, :]) & (positions[None, :] < positions[:, None])
    ranks = jnp.sum(earlier.astype(jnp.int32), axis=1)
    slots = targets * capacity + ranks
    outgoing = jnp.full((shards * capacity,), -1, jnp.int32).at[slots].set(codes)
    incoming = lax.all_to_all(
        outgoing.reshape(shards, capacity), "seq", split_axis=0, concat_axis=0, tiled=True
    ).reshape(-1)
    code_hits = (
        incoming[:, None] == jnp.arange(head_count * blocks, dtype=jnp.int32)[None, :]
    ).astype(jnp.bfloat16)
    flat_pairs = local_pairs.reshape(head_count * blocks, BLK, pair_width)
    reply = jnp.einsum(
        "sc,cid->sid", code_hits, flat_pairs, preferred_element_type=jnp.float32
    ).astype(jnp.bfloat16)
    fetched = lax.all_to_all(
        reply.reshape(shards, capacity, BLK, pair_width),
        "seq",
        split_axis=0,
        concat_axis=0,
        tiled=True,
    )
    slot_hits = (
        slots[:, None] == jnp.arange(shards * capacity, dtype=jnp.int32)[None, :]
    ).astype(jnp.bfloat16)
    random_pairs = (
        jnp.einsum(
            "rs,sid->rid",
            slot_hits,
            fetched.reshape(shards * capacity, BLK, pair_width),
            preferred_element_type=jnp.float32,
        )
        .astype(jnp.bfloat16)
        .reshape(head_count, blocks, randoms, BLK, pair_width)
    )
    offsets = jnp.arange(span, dtype=jnp.int32) - WMAX
    block_ids = my_index * blocks + jnp.arange(blocks, dtype=jnp.int32)
    reach = block_ids[:, None] + offsets[None, :]
    in_range = (reach >= 0) & (reach < shards * blocks)
    window_ok = in_range[None, :, :] & (
        jnp.abs(offsets)[None, None, :] <= window_width[:, None, None]
    )
    list_ok = jnp.concatenate(
        [window_ok, jnp.ones((head_count, blocks, globals_count + randoms), jnp.bool_)], axis=2
    )
    global_hit = block_ids[:, None] == global_blocks[None, :]
    row_global = jnp.any(global_hit, axis=1)
    hit_weight = global_hit.astype(jnp.float32)

    def key_sequence(first_block):
        pieces_list = [
            jnp.stack(
                [
                    lax.dynamic_slice_in_dim(pair_heads, first_block + offset, group, 1)
                    for offset in range(span)
                ],
                axis=2,
            )
        ]
        pieces_list.append(
            jnp.broadcast_to(
                glob_pairs[:, None], (head_count, group, globals_count, BLK, pair_width)
            )
        )
        pieces_list.append(random_pairs)
        joined = jnp.concatenate(pieces_list, axis=2)
        entry_count = joined.shape[2]
        list_mask = list_ok[:, :, :entry_count]
        return (
            joined.reshape(head_count, group, entry_count * BLK, pair_width),
            jnp.repeat(list_mask, BLK, axis=2),
        )

    def forward_group(group_index):
        first_block = group_index * group
        pairs, list_mask = key_sequence(first_block)
        key_part = pairs[..., :head_width]
        value_part = pairs[..., head_width:]
        score_matrix = (
            jnp.einsum("hqid,hqkd->hqik", query_heads, key_part, preferred_element_type=jnp.float32)
            * logit_scale
        )
        score_matrix = jnp.where(list_mask[:, :, None, :], score_matrix, -jnp.inf)
        row_max = jnp.max(score_matrix, axis=-1)
        weights = jnp.exp(score_matrix - row_max[..., None])
        totals = jnp.sum(weights, axis=-1)
        accumulated_total = jnp.einsum(
            "hqik,hqkd->hqid",
            weights.astype(jnp.bfloat16),
            value_part,
            preferred_element_type=jnp.float32,
        )
        return (
            (accumulated_total / totals[..., None]).astype(jnp.bfloat16),
            row_max + jnp.log(totals),
        )

    sparse_out, sparse_lse = lax.map(forward_group, jnp.arange(group_count))
    sparse_out = jnp.moveaxis(sparse_out, 0, 1).reshape(head_count, blocks, BLK, head_width)
    sparse_lse = jnp.moveaxis(sparse_lse, 0, 1).reshape(head_count, blocks, BLK)
    local_keys = local_pairs[..., :head_width].reshape(head_count, blocks * BLK, head_width)
    local_values = local_pairs[..., head_width:].reshape(head_count, blocks * BLK, head_width)
    glob_rows = glob_query.reshape(head_count, globals_count * BLK, head_width)
    glob_grad_rows = glob_grad.reshape(head_count, globals_count * BLK, head_width)
    glob_scores = (
        jnp.einsum("hid,hjd->hij", glob_rows, local_keys, preferred_element_type=jnp.float32)
        * logit_scale
    )
    glob_max = lax.pmax(jnp.max(glob_scores, axis=-1), "seq")
    glob_weights = jnp.exp(glob_scores - glob_max[..., None])
    glob_part_sum = jnp.einsum(
        "hij,hjd->hid",
        glob_weights.astype(jnp.bfloat16),
        local_values,
        preferred_element_type=jnp.float32,
    )
    glob_sum, glob_total = lax.psum((glob_part_sum, jnp.sum(glob_weights, axis=-1)), "seq")
    glob_out = (glob_sum / glob_total[..., None]).astype(jnp.bfloat16)
    glob_lse = glob_max + jnp.log(glob_total)
    chosen_out = jnp.einsum(
        "bg,hgid->hbid",
        hit_weight,
        glob_out.reshape(head_count, globals_count, BLK, head_width).astype(jnp.float32),
    )
    out_heads = jnp.where(
        row_global[None, :, None, None], chosen_out.astype(jnp.bfloat16), sparse_out
    )
    attn_out = token_major(out_heads)
    delta = jnp.sum(grad_heads.astype(jnp.float32) * out_heads.astype(jnp.float32), axis=-1)
    row_lse = jnp.where(row_global[None, :, None], jnp.inf, sparse_lse)
    glob_delta = jnp.sum(glob_grad_rows.astype(jnp.float32) * glob_out.astype(jnp.float32), axis=-1)

    def backward_group(group_index):
        first_block = group_index * group
        pairs, list_mask = key_sequence(first_block)
        key_part = pairs[..., :head_width]
        value_part = pairs[..., head_width:]
        score_matrix = (
            jnp.einsum("hqid,hqkd->hqik", query_heads, key_part, preferred_element_type=jnp.float32)
            * logit_scale
        )
        probs = jnp.where(list_mask[:, :, None, :], jnp.exp(score_matrix - row_lse[..., None]), 0.0)
        probability_gradient = jnp.einsum(
            "hqid,hqkd->hqik", grad_heads, value_part, preferred_element_type=jnp.float32
        )
        score_gradient = (probs * (probability_gradient - delta[..., None])).astype(jnp.bfloat16)
        grad_rows_part = (
            jnp.einsum(
                "hqik,hqkd->hqid", score_gradient, key_part, preferred_element_type=jnp.float32
            )
            * logit_scale
        )
        key_contributions = (
            jnp.einsum(
                "hqik,hqid->hqkd", score_gradient, query_heads, preferred_element_type=jnp.float32
            )
            * logit_scale
        )
        value_contributions = jnp.einsum(
            "hqik,hqid->hqkd",
            probs.astype(jnp.bfloat16),
            grad_heads,
            preferred_element_type=jnp.float32,
        )
        terms = jnp.concatenate([key_contributions, value_contributions], axis=-1).reshape(
            head_count, group, -1, BLK, pair_width
        )
        window_terms = terms[:, :, :span]
        glob_terms = jnp.sum(terms[:, :, span : span + globals_count], axis=1)
        random_terms = terms[:, :, span + globals_count :].astype(jnp.bfloat16)
        return (grad_rows_part, window_terms, glob_terms, random_terms)

    gradient_row_values, window_terms, glob_terms, random_terms = lax.map(
        backward_group, jnp.arange(group_count)
    )
    gradient_row_values = jnp.moveaxis(gradient_row_values, 0, 1).reshape(
        head_count, blocks, BLK, head_width
    )
    window_terms = jnp.moveaxis(window_terms, 0, 1).reshape(
        head_count, blocks, span, BLK, pair_width
    )
    glob_terms = jnp.sum(glob_terms, axis=0)
    spread = jnp.zeros((head_count, blocks + 2 * WMAX, BLK, pair_width), jnp.float32)
    for offset in range(span):
        spread = spread.at[:, offset : offset + blocks].add(window_terms[:, :, offset])
    glob_probs = jnp.exp(glob_scores - glob_lse[..., None])
    glob_grad_probs = jnp.einsum(
        "hid,hjd->hij", glob_grad_rows, local_values, preferred_element_type=jnp.float32
    )
    glob_grad_scores = (glob_probs * (glob_grad_probs - glob_delta[..., None])).astype(jnp.bfloat16)
    glob_query_part = (
        jnp.einsum("hij,hjd->hid", glob_grad_scores, local_keys, preferred_element_type=jnp.float32)
        * logit_scale
    )
    key_from_glob = (
        jnp.einsum("hij,hid->hjd", glob_grad_scores, glob_rows, preferred_element_type=jnp.float32)
        * logit_scale
    )
    value_from_glob = jnp.einsum(
        "hij,hid->hjd",
        glob_probs.astype(jnp.bfloat16),
        glob_grad_rows,
        preferred_element_type=jnp.float32,
    )
    glob_total_terms, glob_query_grad = lax.psum((glob_terms, glob_query_part), "seq")
    from_below = from_behind(spread[:, blocks + WMAX :], "seq", 1)
    from_above = from_behind(spread[:, :WMAX].astype(jnp.bfloat16), "seq", -1).astype(jnp.float32)
    own_terms = spread[:, WMAX : WMAX + blocks]
    own_terms = own_terms.at[:, :WMAX].add(from_below).at[:, blocks - WMAX :].add(from_above)
    own_terms = own_terms + jnp.concatenate([key_from_glob, value_from_glob], axis=-1).reshape(
        head_count, blocks, BLK, pair_width
    )
    own_terms = own_terms + jnp.einsum("bg,hgid->hbid", hit_weight, glob_total_terms)
    random_terms = jnp.moveaxis(random_terms, 0, 1).reshape(request_count, BLK, pair_width)
    outgoing_terms = (
        jnp.zeros((shards * capacity, BLK, pair_width), jnp.bfloat16).at[slots].set(random_terms)
    )
    returned = lax.all_to_all(
        outgoing_terms.reshape(shards, capacity, BLK, pair_width),
        "seq",
        split_axis=0,
        concat_axis=0,
        tiled=True,
    ).reshape(shards * capacity, BLK, pair_width)
    random_add = jnp.einsum(
        "sc,sid->cid", code_hits, returned, preferred_element_type=jnp.float32
    ).reshape(head_count, blocks, BLK, pair_width)
    own_terms = own_terms + random_add
    glob_query_add = jnp.einsum(
        "bg,hgid->hbid",
        hit_weight,
        glob_query_grad.reshape(head_count, globals_count, BLK, head_width),
    )
    grad_query = token_major((gradient_row_values + glob_query_add).astype(jnp.bfloat16))
    grad_key = token_major(own_terms[..., :head_width].astype(jnp.bfloat16))
    grad_value = token_major(own_terms[..., head_width:].astype(jnp.bfloat16))
    return (attn_out, grad_query, grad_key, grad_value)


MASKED = -1e30
ALIGNED = pl.DeviceIdType.MESH


NEXT, ACROSS, SKIP = 0, 1, 2
IN_PIECES = (((0, 2), (2, 2)), ((0, 1), (1, 1), (2, 2)), ((0, 2), (2, 2)))
EARLY = ((0, 1), (1, 1), (2, 2))
OUTER_IN = ((0, 1, ACROSS), (1, 1, ACROSS), (0, 2, SKIP), (0, 2, NEXT), (2, 2, ACROSS), (2, 2, SKIP), (2, 2, NEXT))
INNER_IN = ((0, 2, SKIP), (0, 2, NEXT), (2, 2, SKIP), (2, 2, NEXT))
TURNS = ((ACROSS, ACROSS), None, (NEXT, SKIP), (SKIP, NEXT))
OUTER_OUT = (((0, 2, ACROSS),), (), ((0, 2, NEXT),), ((2, 2, ACROSS), (2, 2, NEXT), (0, 4, SKIP)))
INNER_OUT = ((), (), ((0, 2, SKIP),), ((2, 2, SKIP), (0, 4, ACROSS), (0, 4, NEXT)))


def rows_dot(left, right):
    return lax.dot_general(left, right, (((1,), (1,)), ((), ())), preferred_element_type=jnp.float32)


def one_head_kernel(
    shards,
    blocks,
    width_in,
    global_in,
    random_in,
    k_in,
    v_in,
    q_in,
    g_in,
    out,
    width_ref,
    global_ref,
    random_ref,
    stage,
    in_all,
    bias_own,
    bias_all,
    out_all,
    dk_sum,
    dv_sum,
    small_sem,
    stage_sem,
    in_send,
    in_recv,
    in_local,
    bias_send,
    bias_recv,
    out_send,
    out_recv,
    out_local,
):
    me = lax.axis_index("seq")
    rows = blocks * BLK
    key_blocks = shards * blocks
    hd = in_all.shape[2]
    logit_scale = 1.0 / math.sqrt(hd)
    inner = ((me + 1) // 2) % 2
    partner = (me + 1 - 2 * (me % 2), 3 - me, (me + 2) % 4)
    arrays = (k_in, v_in, q_in, g_in)

    def pick(pair, table):
        first, second = table[pair[0]], table[pair[1]]
        return first + (second - first) * inner

    def cols(index):
        return pl.ds(pl.multiple_of(index * hd, hd), hd)

    def span(index):
        return pl.ds(pl.multiple_of(index * rows, rows), rows)

    def send_in(first, count, step, target):
        if count == 1:
            source, landing = arrays[first].at[:, cols(target)], in_all.at[first, span(me), :]
        else:
            source = stage.at[pl.ds(first, count), :, cols(target)]
            landing = in_all.at[pl.ds(first, count), span(me), :]
        return pltpu.make_async_remote_copy(
            src_ref=source,
            dst_ref=landing,
            send_sem=in_send.at[first, step],
            recv_sem=in_recv.at[first, step],
            device_id={"seq": target},
            device_id_type=ALIGNED,
        )

    def send_bias(step, target):
        return pltpu.make_async_remote_copy(
            src_ref=bias_own.at[target],
            dst_ref=bias_all.at[me],
            send_sem=bias_send.at[step],
            recv_sem=bias_recv.at[step],
            device_id={"seq": target},
            device_id_type=ALIGNED,
        )

    def send_out(first, count, step):
        return pltpu.make_async_remote_copy(
            src_ref=out_all.at[pl.ds(first, count), span(partner[step]), :],
            dst_ref=out.at[pl.ds(first, count), :, cols(me)],
            send_sem=out_send.at[first, step],
            recv_sem=out_recv.at[first, step],
            device_id={"seq": partner[step]},
            device_id_type=ALIGNED,
        )

    def start_outs(turn):
        for role, table in enumerate((OUTER_OUT, INNER_OUT)):

            @pl.when(inner == role)
            def _():
                for first, count, step in table[turn]:
                    send_out(first, count, step).start()

    def finish_outs():
        sent = [[piece for pieces in table for piece in pieces] for table in (OUTER_OUT, INNER_OUT)]
        for role in range(2):

            @pl.when(inner == role)
            def _():
                for piece in sent[role]:
                    send_out(*piece).wait_send()
                for step in (NEXT, SKIP, ACROSS):
                    for piece in sent[role if step == ACROSS else 1 - role]:
                        if piece[2] == step:
                            send_out(*piece).wait_recv()

    small = [
        pltpu.make_async_copy(source, landing, small_sem.at[index])
        for index, (source, landing) in enumerate(
            ((width_in, width_ref), (global_in, global_ref), (random_in, random_ref))
        )
    ]
    staged = [
        pltpu.make_async_copy(array, stage.at[slot], stage_sem.at[slot])
        for slot, array in enumerate(arrays)
    ]
    local_in = [
        pltpu.make_async_copy(
            array.at[:, cols(me)], in_all.at[slot, span(me), :], in_local.at[slot]
        )
        for slot, array in enumerate(arrays)
    ]
    local_out = [
        pltpu.make_async_copy(
            out_all.at[pl.ds(2 * half, 2), span(me), :],
            out.at[pl.ds(2 * half, 2), :, cols(me)],
            out_local.at[half],
        )
        for half in range(2)
    ]

    barrier = pltpu.get_barrier_semaphore()

    def greet(device):
        pl.semaphore_signal(barrier, inc=1, device_id={"seq": device}, device_id_type=ALIGNED)

    greet(3 - me)

    @pl.when(inner == 1)
    def _():
        pl.semaphore_wait(barrier, 1)
        for first, count in EARLY:
            if count == 1:
                send_in(first, count, ACROSS, partner[ACROSS]).start()
        greet(0)
        greet(3)

    for copy in staged:
        copy.start()
    for copy in small:
        copy.start()
    for copy in local_in:
        copy.start()
    for copy in staged:
        copy.wait()

    @pl.when(inner == 1)
    def _():
        for first, count in EARLY:
            if count > 1:
                send_in(first, count, ACROSS, partner[ACROSS]).start()

    for copy in small:
        copy.wait()

    lane = lax.broadcasted_iota(jnp.int32, (1, BLK), 1)
    spot_ids = jnp.zeros_like(lane)
    for spot in range(1, blocks):
        spot_ids += jnp.where(lane >= spot * key_blocks, 1, 0)
    key_ids = lane - spot_ids * key_blocks
    block_ids = me * blocks + spot_ids
    distance = jnp.abs(key_ids - block_ids)
    listed = jnp.zeros(lane.shape, jnp.float32)
    row_global = jnp.zeros(lane.shape, jnp.float32)
    for index in range(global_ref.shape[0]):
        listed += jnp.where(key_ids == global_ref[index], 1.0, 0.0)
        row_global = jnp.maximum(row_global, jnp.where(block_ids == global_ref[index], 1.0, 0.0))
    for head in range(shards):
        hits = listed + jnp.where(distance <= jnp.minimum(width_ref[head], WMAX), 1.0, 0.0)
        for index in range(random_ref.shape[0]):
            named = jnp.zeros_like(lane)
            for spot in range(blocks):
                named = jnp.where(spot_ids == spot, random_ref[index, spot, head], named)
            hits += jnp.where(key_ids == named, 1.0, 0.0)
        hits = row_global + (1.0 - row_global) * hits
        bias_own[head] = jnp.where(
            hits > 0.5, jnp.log(jnp.maximum(hits, 1.0)) * (1.0 / math.log(2.0)), MASKED
        )

    @pl.when(inner == 0)
    def _():
        pl.semaphore_wait(barrier, 3)
        greet(1)
        greet(2)
        for step, target in enumerate(partner):
            send_bias(step, target).start()
        for first, count, step in OUTER_IN:
            send_in(first, count, step, partner[step]).start()

    @pl.when(inner == 1)
    def _():
        pl.semaphore_wait(barrier, 2)
        for step, target in enumerate(partner):
            send_bias(step, target).start()
        for first, count, step in INNER_IN:
            send_in(first, count, step, partner[step]).start()

    bias_all[me] = bias_own[me]

    sub_ids = lax.broadcasted_iota(jnp.int32, (key_blocks, BLK), 0)
    lane_ids = lax.broadcasted_iota(jnp.int32, (key_blocks, BLK), 1)

    for slot in (0, 1):
        local_in[slot].wait()
    for step, target in enumerate(partner):
        for first, count in IN_PIECES[step]:
            if first < 2:
                send_in(first, count, step, target).wait_recv()
    keys = in_all[0]
    vals = in_all[1]
    keys_t = keys.T
    vals_t = vals.T
    for turn, pair in enumerate(TURNS):
        if pair is None:
            chunk = me
            local_in[2].wait()
            local_in[3].wait()
        else:
            chunk, step = pick(pair, partner), pick(pair, (NEXT, ACROSS, SKIP))
            send_in(2, 2, step, chunk).wait_recv()
            send_bias(step, chunk).wait_recv()
        q = in_all[2, span(chunk), :]
        g = in_all[3, span(chunk), :]
        row = jnp.broadcast_to(bias_all[chunk], lane_ids.shape)
        spread = [
            jnp.broadcast_to(
                jnp.sum(
                    jnp.where(lane_ids == sub_ids + spot * key_blocks, row, 0.0),
                    axis=1,
                    keepdims=True,
                ),
                lane_ids.shape,
            )
            for spot in range(blocks)
        ]
        bias = jnp.concatenate(
            [
                jnp.concatenate(
                    [
                        jnp.broadcast_to(spread[spot][key : key + 1, :], (BLK, BLK))
                        for spot in range(blocks)
                    ],
                    axis=1,
                )
                for key in range(key_blocks)
            ],
            axis=0,
        )
        scores = rows_dot(keys, q) * (logit_scale / math.log(2.0)) + bias
        top = jnp.max(scores, axis=0, keepdims=True)
        weights = jnp.exp2(scores - top)
        inverse = 1.0 / jnp.sum(weights, axis=0, keepdims=True)
        out_t = (
            jnp.dot(vals_t, weights.astype(jnp.bfloat16), preferred_element_type=jnp.float32)
            * inverse
        )
        out_rows = out_t.T.astype(jnp.bfloat16)
        out_all[0, span(chunk), :] = out_rows
        delta = jnp.sum(
            (g.astype(jnp.float32) * out_rows.astype(jnp.float32)).T, axis=0, keepdims=True
        )
        probs = weights * inverse
        grads = (probs * (rows_dot(vals, g) - delta)).astype(jnp.bfloat16)
        dq_t = jnp.dot(keys_t, grads, preferred_element_type=jnp.float32) * logit_scale
        out_all[1, span(chunk), :] = dq_t.T.astype(jnp.bfloat16)
        if pair is None:
            local_out[0].start()
        if turn < shards - 1:
            start_outs(turn)
        dv_part = jnp.dot(probs.astype(jnp.bfloat16), g, preferred_element_type=jnp.float32)
        dk_part = jnp.dot(grads, q, preferred_element_type=jnp.float32)
        if turn == 0:
            dv_sum[...] = dv_part
            dk_sum[...] = dk_part
        elif turn < shards - 1:
            dv_sum[...] += dv_part
            dk_sum[...] += dk_part
        else:
            out_all[3] = (dv_sum[...] + dv_part).astype(jnp.bfloat16)
            out_all[2] = ((dk_sum[...] + dk_part) * logit_scale).astype(jnp.bfloat16)
    start_outs(shards - 1)
    local_out[1].start()
    for copy in local_out:
        copy.wait()
    for step, target in enumerate(partner):
        for first, count in IN_PIECES[step]:
            send_in(first, count, step, target).wait_send()
        send_bias(step, target).wait_send()
    finish_outs()


def deliver_kernel(landed, *refs):
    copies = [
        pltpu.make_async_copy(landed.at[slot], refs[slot], refs[4].at[slot]) for slot in range(4)
    ]
    for copy in copies:
        copy.start()
    for copy in copies:
        copy.wait()


def one_head(queries, key_rows, values, grad_out, window_width, global_blocks, random_blocks):
    shards = lax.axis_size("seq")
    tokens, columns = queries.shape
    hd = columns // shards
    blocks = tokens // BLK
    whole = shards * tokens
    bf16 = jnp.bfloat16
    anywhere = pl.BlockSpec(memory_space=pl.ANY)
    dma = pltpu.SemaphoreType.DMA
    lists = (window_width, global_blocks, random_blocks.transpose(2, 1, 0))
    landed = pl.pallas_call(
        functools.partial(one_head_kernel, shards, blocks),
        out_shape=jax.ShapeDtypeStruct((4, tokens, columns), bf16),
        in_specs=[anywhere] * 7,
        out_specs=anywhere,
        scratch_shapes=[pltpu.SMEM(array.shape, jnp.int32) for array in lists]
        + [pltpu.VMEM((4, tokens, columns), bf16), pltpu.VMEM((4, whole, hd), bf16)]
        + [pltpu.VMEM((shards, 1, BLK), jnp.float32)] * 2
        + [pltpu.VMEM((4, whole, hd), bf16)]
        + [pltpu.VMEM((whole, hd), jnp.float32)] * 2
        + [
            dma((3,)),
            dma((4,)),
            dma((4, shards - 1)),
            dma((4, shards - 1)),
            dma((4,)),
            dma((shards - 1,)),
            dma((shards - 1,)),
            dma((4, shards - 1)),
            dma((4, shards - 1)),
            dma((2,)),
        ],
        compiler_params=pltpu.CompilerParams(
            collective_id=0, has_side_effects=True, vmem_limit_bytes=48 * 1024 * 1024
        ),
    )(
        *(
            pltpu.with_memory_space_constraint(array, pltpu.HBM)
            for array in (*lists, key_rows, values, queries, grad_out)
        )
    )
    return pl.pallas_call(
        deliver_kernel,
        out_shape=(jax.ShapeDtypeStruct((tokens, columns), bf16),) * 4,
        in_specs=[anywhere],
        out_specs=(anywhere,) * 4,
        scratch_shapes=[dma((4,))],
        compiler_params=pltpu.CompilerParams(vmem_limit_bytes=8 * 1024 * 1024),
    )(landed)


def dispatch(queries, key_rows, values, grad_out, window_width, global_blocks, random_blocks):
    shards = lax.axis_size("seq")
    if shards == 4 and window_width.shape[0] == shards and queries.shape[1] == shards * BLK:
        chosen = one_head
    else:
        chosen = on_device
    return chosen(
        queries, key_rows, values, grad_out, window_width, global_blocks, random_blocks
    )


def solution(mesh):
    in_specs = (
        P(("groups", "seq"), ("head", "sub")),
        P(("groups", "seq"), ("head", "sub")),
        P(("groups", "seq"), ("head", "sub")),
        P(("groups", "seq"), ("head", "sub")),
        P(("groups", "head", "sub")),
        P("groups"),
        P(("groups", "head", "sub"), "seq", None),
    )
    out_specs = (
        P(("groups", "seq"), ("head", "sub")),
        P(("groups", "seq"), ("head", "sub")),
        P(("groups", "seq"), ("head", "sub")),
        P(("groups", "seq"), ("head", "sub")),
    )
    return jax.shard_map(
        dispatch, mesh=mesh, in_specs=in_specs, out_specs=out_specs, check_vma=False
    )
```

```python
import functools
import math

import jax
import jax.numpy as jnp
from jax import lax
from jax.experimental import pallas as pl
from jax.experimental.pallas import tpu as pltpu
from jax.sharding import PartitionSpec as P

BLK = 128
WMAX = 1


def extended(cells, sides, width):
    for axis, dim in sides:
        count = lax.axis_size(axis)
        ends = count - 1
        head = lax.slice_in_dim(cells, 0, width, axis=dim)
        tail = lax.slice_in_dim(cells, cells.shape[dim] - width, cells.shape[dim], axis=dim)
        cells = jnp.concatenate(
            [
                lax.ppermute(tail, axis, [(i, (i + 1) % count) for i in range(ends)]),
                cells,
                lax.ppermute(head, axis, [((i + 1) % count, i) for i in range(ends)]),
            ],
            axis=dim,
        )
    return cells


def from_behind(block, axis, distance):
    devices = range(lax.axis_size(axis))
    route = [(i - distance, i) for i in devices if i - distance in devices]
    return lax.ppermute(block, axis, route)


def head_major(tensor, head_count, head_width):
    block_count = tensor.shape[0] // BLK
    return tensor.reshape(block_count, BLK, head_count, head_width).transpose(2, 0, 1, 3)


def token_major(tensor):
    head_count, block_count, row_count, head_width = tensor.shape
    return tensor.transpose(1, 2, 0, 3).reshape(block_count * row_count, head_count * head_width)


def on_device(queries, key_rows, values, grad_out, window_width, global_blocks, random_blocks):
    head_count = window_width.shape[0]
    tokens = queries.shape[0]
    head_width = queries.shape[1] // head_count
    blocks = tokens // BLK
    span = 2 * WMAX + 1
    globals_count = global_blocks.shape[0]
    randoms = random_blocks.shape[2]
    shards = lax.axis_size("seq")
    my_index = lax.axis_index("seq")
    logit_scale = 1.0 / math.sqrt(head_width)
    group = 2
    group_count = blocks // group
    pair_width = 2 * head_width
    query_heads = head_major(queries, head_count, head_width)
    grad_heads = head_major(grad_out, head_count, head_width)
    packed = jnp.concatenate([key_rows, values], axis=1)
    padded = extended(packed, (("seq", 0),), WMAX * BLK)
    pair_heads = (
        padded.reshape(blocks + 2 * WMAX, BLK, 2, head_count, head_width)
        .transpose(3, 0, 1, 2, 4)
        .reshape(head_count, blocks + 2 * WMAX, BLK, pair_width)
    )
    local_pairs = pair_heads[:, WMAX : WMAX + blocks]
    owners = global_blocks // blocks
    local_spot = global_blocks % blocks
    stacked = jnp.concatenate([queries, key_rows, values, grad_out], axis=1)
    own_rows = jnp.stack(
        [
            lax.dynamic_slice_in_dim(stacked, local_spot[glob_index] * BLK, BLK, 0)
            for glob_index in range(globals_count)
        ]
    )
    owned_mask = (owners == my_index)[:, None, None]
    masked_rows = jnp.where(owned_mask, own_rows, jnp.zeros((), jnp.bfloat16))
    panels = lax.psum(masked_rows, "seq").astype(jnp.float32).astype(jnp.bfloat16)
    panel_heads = panels.reshape(globals_count, BLK, 4, head_count, head_width).transpose(
        2, 3, 0, 1, 4
    )
    glob_query = panel_heads[0]
    glob_grad = panel_heads[3]
    glob_pairs = jnp.concatenate([panel_heads[1], panel_heads[2]], axis=-1)
    requests = random_blocks.reshape(-1)
    request_count = requests.shape[0]
    capacity = max(2, -(-request_count // shards))
    targets = requests // blocks
    request_head = jnp.arange(request_count, dtype=jnp.int32) // (blocks * randoms)
    codes = request_head * blocks + requests % blocks
    positions = jnp.arange(request_count, dtype=jnp.int32)
    earlier = (targets[:, None] == targets[None, :]) & (positions[None, :] < positions[:, None])
    ranks = jnp.sum(earlier.astype(jnp.int32), axis=1)
    slots = targets * capacity + ranks
    outgoing = jnp.full((shards * capacity,), -1, jnp.int32).at[slots].set(codes)
    incoming = lax.all_to_all(
        outgoing.reshape(shards, capacity), "seq", split_axis=0, concat_axis=0, tiled=True
    ).reshape(-1)
    code_hits = (
        incoming[:, None] == jnp.arange(head_count * blocks, dtype=jnp.int32)[None, :]
    ).astype(jnp.bfloat16)
    flat_pairs = local_pairs.reshape(head_count * blocks, BLK, pair_width)
    reply = jnp.einsum(
        "sc,cid->sid", code_hits, flat_pairs, preferred_element_type=jnp.float32
    ).astype(jnp.bfloat16)
    fetched = lax.all_to_all(
        reply.reshape(shards, capacity, BLK, pair_width),
        "seq",
        split_axis=0,
        concat_axis=0,
        tiled=True,
    )
    slot_hits = (
        slots[:, None] == jnp.arange(shards * capacity, dtype=jnp.int32)[None, :]
    ).astype(jnp.bfloat16)
    random_pairs = (
        jnp.einsum(
            "rs,sid->rid",
            slot_hits,
            fetched.reshape(shards * capacity, BLK, pair_width),
            preferred_element_type=jnp.float32,
        )
        .astype(jnp.bfloat16)
        .reshape(head_count, blocks, randoms, BLK, pair_width)
    )
    offsets = jnp.arange(span, dtype=jnp.int32) - WMAX
    block_ids = my_index * blocks + jnp.arange(blocks, dtype=jnp.int32)
    reach = block_ids[:, None] + offsets[None, :]
    in_range = (reach >= 0) & (reach < shards * blocks)
    window_ok = in_range[None, :, :] & (
        jnp.abs(offsets)[None, None, :] <= window_width[:, None, None]
    )
    list_ok = jnp.concatenate(
        [window_ok, jnp.ones((head_count, blocks, globals_count + randoms), jnp.bool_)], axis=2
    )
    global_hit = block_ids[:, None] == global_blocks[None, :]
    row_global = jnp.any(global_hit, axis=1)
    hit_weight = global_hit.astype(jnp.float32)

    def key_sequence(first_block):
        pieces_list = [
            jnp.stack(
                [
                    lax.dynamic_slice_in_dim(pair_heads, first_block + offset, group, 1)
                    for offset in range(span)
                ],
                axis=2,
            )
        ]
        pieces_list.append(
            jnp.broadcast_to(
                glob_pairs[:, None], (head_count, group, globals_count, BLK, pair_width)
            )
        )
        pieces_list.append(random_pairs)
        joined = jnp.concatenate(pieces_list, axis=2)
        entry_count = joined.shape[2]
        list_mask = list_ok[:, :, :entry_count]
        return (
            joined.reshape(head_count, group, entry_count * BLK, pair_width),
            jnp.repeat(list_mask, BLK, axis=2),
        )

    def forward_group(group_index):
        first_block = group_index * group
        pairs, list_mask = key_sequence(first_block)
        key_part = pairs[..., :head_width]
        value_part = pairs[..., head_width:]
        score_matrix = (
            jnp.einsum("hqid,hqkd->hqik", query_heads, key_part, preferred_element_type=jnp.float32)
            * logit_scale
        )
        score_matrix = jnp.where(list_mask[:, :, None, :], score_matrix, -jnp.inf)
        row_max = jnp.max(score_matrix, axis=-1)
        weights = jnp.exp(score_matrix - row_max[..., None])
        totals = jnp.sum(weights, axis=-1)
        accumulated_total = jnp.einsum(
            "hqik,hqkd->hqid",
            weights.astype(jnp.bfloat16),
            value_part,
            preferred_element_type=jnp.float32,
        )
        return (
            (accumulated_total / totals[..., None]).astype(jnp.bfloat16),
            row_max + jnp.log(totals),
        )

    sparse_out, sparse_lse = lax.map(forward_group, jnp.arange(group_count))
    sparse_out = jnp.moveaxis(sparse_out, 0, 1).reshape(head_count, blocks, BLK, head_width)
    sparse_lse = jnp.moveaxis(sparse_lse, 0, 1).reshape(head_count, blocks, BLK)
    local_keys = local_pairs[..., :head_width].reshape(head_count, blocks * BLK, head_width)
    local_values = local_pairs[..., head_width:].reshape(head_count, blocks * BLK, head_width)
    glob_rows = glob_query.reshape(head_count, globals_count * BLK, head_width)
    glob_grad_rows = glob_grad.reshape(head_count, globals_count * BLK, head_width)
    glob_scores = (
        jnp.einsum("hid,hjd->hij", glob_rows, local_keys, preferred_element_type=jnp.float32)
        * logit_scale
    )
    glob_max = lax.pmax(jnp.max(glob_scores, axis=-1), "seq")
    glob_weights = jnp.exp(glob_scores - glob_max[..., None])
    glob_part_sum = jnp.einsum(
        "hij,hjd->hid",
        glob_weights.astype(jnp.bfloat16),
        local_values,
        preferred_element_type=jnp.float32,
    )
    glob_sum, glob_total = lax.psum((glob_part_sum, jnp.sum(glob_weights, axis=-1)), "seq")
    glob_out = (glob_sum / glob_total[..., None]).astype(jnp.bfloat16)
    glob_lse = glob_max + jnp.log(glob_total)
    chosen_out = jnp.einsum(
        "bg,hgid->hbid",
        hit_weight,
        glob_out.reshape(head_count, globals_count, BLK, head_width).astype(jnp.float32),
    )
    out_heads = jnp.where(
        row_global[None, :, None, None], chosen_out.astype(jnp.bfloat16), sparse_out
    )
    attn_out = token_major(out_heads)
    delta = jnp.sum(grad_heads.astype(jnp.float32) * out_heads.astype(jnp.float32), axis=-1)
    row_lse = jnp.where(row_global[None, :, None], jnp.inf, sparse_lse)
    glob_delta = jnp.sum(glob_grad_rows.astype(jnp.float32) * glob_out.astype(jnp.float32), axis=-1)

    def backward_group(group_index):
        first_block = group_index * group
        pairs, list_mask = key_sequence(first_block)
        key_part = pairs[..., :head_width]
        value_part = pairs[..., head_width:]
        score_matrix = (
            jnp.einsum("hqid,hqkd->hqik", query_heads, key_part, preferred_element_type=jnp.float32)
            * logit_scale
        )
        probs = jnp.where(list_mask[:, :, None, :], jnp.exp(score_matrix - row_lse[..., None]), 0.0)
        probability_gradient = jnp.einsum(
            "hqid,hqkd->hqik", grad_heads, value_part, preferred_element_type=jnp.float32
        )
        score_gradient = (probs * (probability_gradient - delta[..., None])).astype(jnp.bfloat16)
        grad_rows_part = (
            jnp.einsum(
                "hqik,hqkd->hqid", score_gradient, key_part, preferred_element_type=jnp.float32
            )
            * logit_scale
        )
        key_contributions = (
            jnp.einsum(
                "hqik,hqid->hqkd", score_gradient, query_heads, preferred_element_type=jnp.float32
            )
            * logit_scale
        )
        value_contributions = jnp.einsum(
            "hqik,hqid->hqkd",
            probs.astype(jnp.bfloat16),
            grad_heads,
            preferred_element_type=jnp.float32,
        )
        terms = jnp.concatenate([key_contributions, value_contributions], axis=-1).reshape(
            head_count, group, -1, BLK, pair_width
        )
        window_terms = terms[:, :, :span]
        glob_terms = jnp.sum(terms[:, :, span : span + globals_count], axis=1)
        random_terms = terms[:, :, span + globals_count :].astype(jnp.bfloat16)
        return (grad_rows_part, window_terms, glob_terms, random_terms)

    gradient_row_values, window_terms, glob_terms, random_terms = lax.map(
        backward_group, jnp.arange(group_count)
    )
    gradient_row_values = jnp.moveaxis(gradient_row_values, 0, 1).reshape(
        head_count, blocks, BLK, head_width
    )
    window_terms = jnp.moveaxis(window_terms, 0, 1).reshape(
        head_count, blocks, span, BLK, pair_width
    )
    glob_terms = jnp.sum(glob_terms, axis=0)
    spread = jnp.zeros((head_count, blocks + 2 * WMAX, BLK, pair_width), jnp.float32)
    for offset in range(span):
        spread = spread.at[:, offset : offset + blocks].add(window_terms[:, :, offset])
    glob_probs = jnp.exp(glob_scores - glob_lse[..., None])
    glob_grad_probs = jnp.einsum(
        "hid,hjd->hij", glob_grad_rows, local_values, preferred_element_type=jnp.float32
    )
    glob_grad_scores = (glob_probs * (glob_grad_probs - glob_delta[..., None])).astype(jnp.bfloat16)
    glob_query_part = (
        jnp.einsum("hij,hjd->hid", glob_grad_scores, local_keys, preferred_element_type=jnp.float32)
        * logit_scale
    )
    key_from_glob = (
        jnp.einsum("hij,hid->hjd", glob_grad_scores, glob_rows, preferred_element_type=jnp.float32)
        * logit_scale
    )
    value_from_glob = jnp.einsum(
        "hij,hid->hjd",
        glob_probs.astype(jnp.bfloat16),
        glob_grad_rows,
        preferred_element_type=jnp.float32,
    )
    glob_total_terms, glob_query_grad = lax.psum((glob_terms, glob_query_part), "seq")
    from_below = from_behind(spread[:, blocks + WMAX :], "seq", 1)
    from_above = from_behind(spread[:, :WMAX].astype(jnp.bfloat16), "seq", -1).astype(jnp.float32)
    own_terms = spread[:, WMAX : WMAX + blocks]
    own_terms = own_terms.at[:, :WMAX].add(from_below).at[:, blocks - WMAX :].add(from_above)
    own_terms = own_terms + jnp.concatenate([key_from_glob, value_from_glob], axis=-1).reshape(
        head_count, blocks, BLK, pair_width
    )
    own_terms = own_terms + jnp.einsum("bg,hgid->hbid", hit_weight, glob_total_terms)
    random_terms = jnp.moveaxis(random_terms, 0, 1).reshape(request_count, BLK, pair_width)
    outgoing_terms = (
        jnp.zeros((shards * capacity, BLK, pair_width), jnp.bfloat16).at[slots].set(random_terms)
    )
    returned = lax.all_to_all(
        outgoing_terms.reshape(shards, capacity, BLK, pair_width),
        "seq",
        split_axis=0,
        concat_axis=0,
        tiled=True,
    ).reshape(shards * capacity, BLK, pair_width)
    random_add = jnp.einsum(
        "sc,sid->cid", code_hits, returned, preferred_element_type=jnp.float32
    ).reshape(head_count, blocks, BLK, pair_width)
    own_terms = own_terms + random_add
    glob_query_add = jnp.einsum(
        "bg,hgid->hbid",
        hit_weight,
        glob_query_grad.reshape(head_count, globals_count, BLK, head_width),
    )
    grad_query = token_major((gradient_row_values + glob_query_add).astype(jnp.bfloat16))
    grad_key = token_major(own_terms[..., :head_width].astype(jnp.bfloat16))
    grad_value = token_major(own_terms[..., head_width:].astype(jnp.bfloat16))
    return (attn_out, grad_query, grad_key, grad_value)


MASKED = -1e30
ALIGNED = pl.DeviceIdType.MESH


NEXT, ACROSS, SKIP = 0, 1, 2
EARLY = ((0, 1), (1, 1), (2, 2))
OUTER_IN = ((0, 1, ACROSS), (1, 1, ACROSS), (0, 2, SKIP), (0, 2, NEXT), (2, 2, ACROSS), (2, 2, SKIP), (2, 2, NEXT))
INNER_IN = ((0, 2, SKIP), (0, 2, NEXT), (2, 2, SKIP), (2, 2, NEXT))
TURNS = ((ACROSS, ACROSS), None, (NEXT, SKIP), (SKIP, NEXT))
OUTER_OUT = (((0, 2, ACROSS),), (), ((0, 2, NEXT),), ((2, 2, ACROSS), (2, 2, NEXT), (0, 4, SKIP)))
INNER_OUT = ((), (), ((0, 2, SKIP),), ((2, 2, SKIP), (0, 4, ACROSS), (0, 4, NEXT)))


def rows_dot(left, right):
    return lax.dot_general(left, right, (((1,), (1,)), ((), ())), preferred_element_type=jnp.float32)


def one_head_kernel(
    shards,
    blocks,
    width_in,
    global_in,
    random_in,
    k_in,
    v_in,
    q_in,
    g_in,
    out,
    width_ref,
    global_ref,
    random_ref,
    stage,
    in_all,
    bias_own,
    bias_all,
    out_all,
    dk_sum,
    dv_sum,
    small_sem,
    stage_sem,
    pair_recv,
    rest_recv,
    in_send,
    bias_send,
    bias_recv,
    out_send,
    out_recv,
):
    me = lax.axis_index("seq")
    rows = blocks * BLK
    key_blocks = shards * blocks
    hd = in_all.shape[2]
    logit_scale = 1.0 / math.sqrt(hd)
    inner = ((me + 1) // 2) % 2
    partner = (me + 1 - 2 * (me % 2), 3 - me, (me + 2) % 4)
    arrays = (k_in, v_in, q_in, g_in)

    def pick(pair, table):
        first, second = table[pair[0]], table[pair[1]]
        return first + (second - first) * inner

    def cols(index):
        return pl.ds(pl.multiple_of(index * hd, hd), hd)

    def span(index):
        return pl.ds(pl.multiple_of(index * rows, rows), rows)

    def send_in(first, count, step, target):
        if count == 1:
            source, landing = arrays[first].at[:, cols(target)], in_all.at[first, span(me), :]
        else:
            source = stage.at[pl.ds(first, count), :, cols(target)]
            landing = in_all.at[pl.ds(first, count), span(me), :]
        return pltpu.make_async_remote_copy(
            src_ref=source,
            dst_ref=landing,
            send_sem=in_send,
            recv_sem=pair_recv if first < 2 else rest_recv.at[step],
            device_id={"seq": target},
            device_id_type=ALIGNED,
        )

    def send_bias(target):
        return pltpu.make_async_remote_copy(
            src_ref=bias_own.at[target],
            dst_ref=bias_all.at[me],
            send_sem=bias_send,
            recv_sem=bias_recv,
            device_id={"seq": target},
            device_id_type=ALIGNED,
        )

    def send_out(first, count, step):
        return pltpu.make_async_remote_copy(
            src_ref=out_all.at[pl.ds(first, count), span(partner[step]), :],
            dst_ref=out.at[pl.ds(first, count), :, cols(me)],
            send_sem=out_send,
            recv_sem=out_recv,
            device_id={"seq": partner[step]},
            device_id_type=ALIGNED,
        )

    def start_outs(turn):
        for role, table in enumerate((OUTER_OUT, INNER_OUT)):

            @pl.when(inner == role)
            def _():
                for first, count, step in table[turn]:
                    send_out(first, count, step).start()

    def wait_for(bytes_of, semaphore):
        pltpu.make_async_copy(bytes_of, bytes_of, semaphore).wait()

    small = [
        pltpu.make_async_copy(source, landing, small_sem.at[index])
        for index, (source, landing) in enumerate(
            ((width_in, width_ref), (global_in, global_ref), (random_in, random_ref))
        )
    ]
    staged = [
        pltpu.make_async_copy(array, stage.at[slot], stage_sem)
        for slot, array in enumerate(arrays)
    ]
    local_out = [
        pltpu.make_async_copy(
            out_all.at[pl.ds(2 * half, 2), span(me), :],
            out.at[pl.ds(2 * half, 2), :, cols(me)],
            out_recv,
        )
        for half in range(2)
    ]

    barrier = pltpu.get_barrier_semaphore()

    def greet(device):
        pl.semaphore_signal(barrier, inc=1, device_id={"seq": device}, device_id_type=ALIGNED)

    greet(3 - me)

    @pl.when(inner == 1)
    def _():
        pl.semaphore_wait(barrier, 1)
        for first, count in EARLY:
            if count == 1:
                send_in(first, count, ACROSS, partner[ACROSS]).start()
        greet(0)
        greet(3)

    for copy in staged:
        copy.start()
    for copy in small:
        copy.start()
    wait_for(stage, stage_sem)

    @pl.when(inner == 1)
    def _():
        for first, count in EARLY:
            if count > 1:
                send_in(first, count, ACROSS, partner[ACROSS]).start()

    for copy in small:
        copy.wait()

    lane = lax.broadcasted_iota(jnp.int32, (1, BLK), 1)
    spot_ids = jnp.zeros_like(lane)
    for spot in range(1, blocks):
        spot_ids += jnp.where(lane >= spot * key_blocks, 1, 0)
    key_ids = lane - spot_ids * key_blocks
    block_ids = me * blocks + spot_ids
    distance = jnp.abs(key_ids - block_ids)
    listed = jnp.zeros(lane.shape, jnp.float32)
    row_global = jnp.zeros(lane.shape, jnp.float32)
    for index in range(global_ref.shape[0]):
        listed += jnp.where(key_ids == global_ref[index], 1.0, 0.0)
        row_global = jnp.maximum(row_global, jnp.where(block_ids == global_ref[index], 1.0, 0.0))
    for head in range(shards):
        hits = listed + jnp.where(distance <= jnp.minimum(width_ref[head], WMAX), 1.0, 0.0)
        for index in range(random_ref.shape[0]):
            named = jnp.zeros_like(lane)
            for spot in range(blocks):
                named = jnp.where(spot_ids == spot, random_ref[index, spot, head], named)
            hits += jnp.where(key_ids == named, 1.0, 0.0)
        hits = row_global + (1.0 - row_global) * hits
        bias_own[head] = jnp.where(
            hits > 0.5, jnp.log(jnp.maximum(hits, 1.0)) * (1.0 / math.log(2.0)), MASKED
        )

    @pl.when(inner == 0)
    def _():
        pl.semaphore_wait(barrier, 3)
        greet(1)
        greet(2)
        for step, target in enumerate(partner):
            send_bias(target).start()
        for first, count, step in OUTER_IN:
            send_in(first, count, step, partner[step]).start()

    @pl.when(inner == 1)
    def _():
        pl.semaphore_wait(barrier, 2)
        for step, target in enumerate(partner):
            send_bias(target).start()
        for first, count, step in INNER_IN:
            send_in(first, count, step, partner[step]).start()

    bias_all[me] = bias_own[me]

    sub_ids = lax.broadcasted_iota(jnp.int32, (key_blocks, BLK), 0)
    lane_ids = lax.broadcasted_iota(jnp.int32, (key_blocks, BLK), 1)

    for slot in range(4):
        in_all[slot, span(me), :] = stage[slot, :, cols(me)]
    others = pl.ds(0, (shards - 1) * rows)
    wait_for(in_all.at[pl.ds(0, 2), others, :], pair_recv)
    wait_for(bias_all.at[pl.ds(0, shards - 1)], bias_recv)
    keys = in_all[0]
    vals = in_all[1]
    keys_t = keys.T
    vals_t = vals.T
    for turn, pair in enumerate(TURNS):
        if pair is None:
            chunk = me
        else:
            chunk, step = pick(pair, partner), pick(pair, (NEXT, ACROSS, SKIP))
            wait_for(in_all.at[pl.ds(2, 2), span(chunk), :], rest_recv.at[step])
        q = in_all[2, span(chunk), :]
        g = in_all[3, span(chunk), :]
        row = jnp.broadcast_to(bias_all[chunk], lane_ids.shape)
        spread = [
            jnp.broadcast_to(
                jnp.sum(
                    jnp.where(lane_ids == sub_ids + spot * key_blocks, row, 0.0),
                    axis=1,
                    keepdims=True,
                ),
                lane_ids.shape,
            )
            for spot in range(blocks)
        ]
        bias = jnp.concatenate(
            [
                jnp.concatenate(
                    [
                        jnp.broadcast_to(spread[spot][key : key + 1, :], (BLK, BLK))
                        for spot in range(blocks)
                    ],
                    axis=1,
                )
                for key in range(key_blocks)
            ],
            axis=0,
        )
        scores = rows_dot(keys, q) * (logit_scale / math.log(2.0)) + bias
        top = jnp.max(scores, axis=0, keepdims=True)
        weights = jnp.exp2(scores - top)
        inverse = 1.0 / jnp.sum(weights, axis=0, keepdims=True)
        out_t = (
            jnp.dot(vals_t, weights.astype(jnp.bfloat16), preferred_element_type=jnp.float32)
            * inverse
        )
        out_rows = out_t.T.astype(jnp.bfloat16)
        out_all[0, span(chunk), :] = out_rows
        delta = jnp.sum(
            (g.astype(jnp.float32) * out_rows.astype(jnp.float32)).T, axis=0, keepdims=True
        )
        probs = weights * inverse
        grads = (probs * (rows_dot(vals, g) - delta)).astype(jnp.bfloat16)
        dq_t = jnp.dot(keys_t, grads, preferred_element_type=jnp.float32) * logit_scale
        out_all[1, span(chunk), :] = dq_t.T.astype(jnp.bfloat16)
        if pair is None:
            local_out[0].start()
        if turn < shards - 1:
            start_outs(turn)
        dv_part = jnp.dot(probs.astype(jnp.bfloat16), g, preferred_element_type=jnp.float32)
        dk_part = jnp.dot(grads, q, preferred_element_type=jnp.float32)
        if turn == 0:
            dv_sum[...] = dv_part
            dk_sum[...] = dk_part
        elif turn < shards - 1:
            dv_sum[...] += dv_part
            dk_sum[...] += dk_part
        else:
            out_all[3] = (dv_sum[...] + dv_part).astype(jnp.bfloat16)
            out_all[2] = ((dk_sum[...] + dk_part) * logit_scale).astype(jnp.bfloat16)
    start_outs(shards - 1)
    local_out[1].start()
    wait_for(bias_own.at[pl.ds(0, shards - 1)], bias_send)
    wait_for(in_all.at[:, others, :], in_send)
    wait_for(out_all.at[:, others, :], out_send)
    wait_for(out, out_recv)


def deliver_kernel(landed, *refs):
    for slot in range(4):
        pltpu.make_async_copy(landed.at[slot], refs[slot], refs[4]).start()
    pltpu.make_async_copy(landed, landed, refs[4]).wait()


def one_head(queries, key_rows, values, grad_out, window_width, global_blocks, random_blocks):
    shards = lax.axis_size("seq")
    tokens, columns = queries.shape
    hd = columns // shards
    blocks = tokens // BLK
    whole = shards * tokens
    bf16 = jnp.bfloat16
    anywhere = pl.BlockSpec(memory_space=pl.ANY)
    dma = pltpu.SemaphoreType.DMA
    lists = (window_width, global_blocks, random_blocks.transpose(2, 1, 0))
    landed = pl.pallas_call(
        functools.partial(one_head_kernel, shards, blocks),
        out_shape=jax.ShapeDtypeStruct((4, tokens, columns), bf16),
        in_specs=[anywhere] * 7,
        out_specs=anywhere,
        scratch_shapes=[pltpu.SMEM(array.shape, jnp.int32) for array in lists]
        + [pltpu.VMEM((4, tokens, columns), bf16), pltpu.VMEM((4, whole, hd), bf16)]
        + [pltpu.VMEM((shards, 1, BLK), jnp.float32)] * 2
        + [pltpu.VMEM((4, whole, hd), bf16)]
        + [pltpu.VMEM((whole, hd), jnp.float32)] * 2
        + [dma((3,)), dma(()), dma(()), dma((shards - 1,))]
        + [dma(())] * 5,
        compiler_params=pltpu.CompilerParams(
            collective_id=0, has_side_effects=True, vmem_limit_bytes=48 * 1024 * 1024
        ),
    )(
        *(
            pltpu.with_memory_space_constraint(array, pltpu.HBM)
            for array in (*lists, key_rows, values, queries, grad_out)
        )
    )
    return pl.pallas_call(
        deliver_kernel,
        out_shape=(jax.ShapeDtypeStruct((tokens, columns), bf16),) * 4,
        in_specs=[anywhere],
        out_specs=(anywhere,) * 4,
        scratch_shapes=[dma(())],
        compiler_params=pltpu.CompilerParams(vmem_limit_bytes=8 * 1024 * 1024),
    )(landed)


def dispatch(queries, key_rows, values, grad_out, window_width, global_blocks, random_blocks):
    shards = lax.axis_size("seq")
    if shards == 4 and window_width.shape[0] == shards and queries.shape[1] == shards * BLK:
        chosen = one_head
    else:
        chosen = on_device
    return chosen(
        queries, key_rows, values, grad_out, window_width, global_blocks, random_blocks
    )


def solution(mesh):
    in_specs = (
        P(("groups", "seq"), ("head", "sub")),
        P(("groups", "seq"), ("head", "sub")),
        P(("groups", "seq"), ("head", "sub")),
        P(("groups", "seq"), ("head", "sub")),
        P(("groups", "head", "sub")),
        P("groups"),
        P(("groups", "head", "sub"), "seq", None),
    )
    out_specs = (
        P(("groups", "seq"), ("head", "sub")),
        P(("groups", "seq"), ("head", "sub")),
        P(("groups", "seq"), ("head", "sub")),
        P(("groups", "seq"), ("head", "sub")),
    )
    return jax.shard_map(
        dispatch, mesh=mesh, in_specs=in_specs, out_specs=out_specs, check_vma=False
    )
```

```python
import functools
import math

import jax
import jax.numpy as jnp
from jax import lax
from jax.experimental import pallas as pl
from jax.experimental.pallas import tpu as pltpu
from jax.sharding import PartitionSpec as P

BLK = 128
WMAX = 1


def extended(cells, sides, width):
    for axis, dim in sides:
        count = lax.axis_size(axis)
        ends = count - 1
        head = lax.slice_in_dim(cells, 0, width, axis=dim)
        tail = lax.slice_in_dim(cells, cells.shape[dim] - width, cells.shape[dim], axis=dim)
        cells = jnp.concatenate(
            [
                lax.ppermute(tail, axis, [(i, (i + 1) % count) for i in range(ends)]),
                cells,
                lax.ppermute(head, axis, [((i + 1) % count, i) for i in range(ends)]),
            ],
            axis=dim,
        )
    return cells


def from_behind(block, axis, distance):
    devices = range(lax.axis_size(axis))
    route = [(i - distance, i) for i in devices if i - distance in devices]
    return lax.ppermute(block, axis, route)


def head_major(tensor, head_count, head_width):
    block_count = tensor.shape[0] // BLK
    return tensor.reshape(block_count, BLK, head_count, head_width).transpose(2, 0, 1, 3)


def token_major(tensor):
    head_count, block_count, row_count, head_width = tensor.shape
    return tensor.transpose(1, 2, 0, 3).reshape(block_count * row_count, head_count * head_width)


def on_device(queries, key_rows, values, grad_out, window_width, global_blocks, random_blocks):
    head_count = window_width.shape[0]
    tokens = queries.shape[0]
    head_width = queries.shape[1] // head_count
    blocks = tokens // BLK
    span = 2 * WMAX + 1
    globals_count = global_blocks.shape[0]
    randoms = random_blocks.shape[2]
    shards = lax.axis_size("seq")
    my_index = lax.axis_index("seq")
    logit_scale = 1.0 / math.sqrt(head_width)
    group = 2
    group_count = blocks // group
    pair_width = 2 * head_width
    query_heads = head_major(queries, head_count, head_width)
    grad_heads = head_major(grad_out, head_count, head_width)
    packed = jnp.concatenate([key_rows, values], axis=1)
    padded = extended(packed, (("seq", 0),), WMAX * BLK)
    pair_heads = (
        padded.reshape(blocks + 2 * WMAX, BLK, 2, head_count, head_width)
        .transpose(3, 0, 1, 2, 4)
        .reshape(head_count, blocks + 2 * WMAX, BLK, pair_width)
    )
    local_pairs = pair_heads[:, WMAX : WMAX + blocks]
    owners = global_blocks // blocks
    local_spot = global_blocks % blocks
    stacked = jnp.concatenate([queries, key_rows, values, grad_out], axis=1)
    own_rows = jnp.stack(
        [
            lax.dynamic_slice_in_dim(stacked, local_spot[glob_index] * BLK, BLK, 0)
            for glob_index in range(globals_count)
        ]
    )
    owned_mask = (owners == my_index)[:, None, None]
    masked_rows = jnp.where(owned_mask, own_rows, jnp.zeros((), jnp.bfloat16))
    panels = lax.psum(masked_rows, "seq").astype(jnp.float32).astype(jnp.bfloat16)
    panel_heads = panels.reshape(globals_count, BLK, 4, head_count, head_width).transpose(
        2, 3, 0, 1, 4
    )
    glob_query = panel_heads[0]
    glob_grad = panel_heads[3]
    glob_pairs = jnp.concatenate([panel_heads[1], panel_heads[2]], axis=-1)
    requests = random_blocks.reshape(-1)
    request_count = requests.shape[0]
    capacity = max(2, -(-request_count // shards))
    targets = requests // blocks
    request_head = jnp.arange(request_count, dtype=jnp.int32) // (blocks * randoms)
    codes = request_head * blocks + requests % blocks
    positions = jnp.arange(request_count, dtype=jnp.int32)
    earlier = (targets[:, None] == targets[None, :]) & (positions[None, :] < positions[:, None])
    ranks = jnp.sum(earlier.astype(jnp.int32), axis=1)
    slots = targets * capacity + ranks
    outgoing = jnp.full((shards * capacity,), -1, jnp.int32).at[slots].set(codes)
    incoming = lax.all_to_all(
        outgoing.reshape(shards, capacity), "seq", split_axis=0, concat_axis=0, tiled=True
    ).reshape(-1)
    code_hits = (
        incoming[:, None] == jnp.arange(head_count * blocks, dtype=jnp.int32)[None, :]
    ).astype(jnp.bfloat16)
    flat_pairs = local_pairs.reshape(head_count * blocks, BLK, pair_width)
    reply = jnp.einsum(
        "sc,cid->sid", code_hits, flat_pairs, preferred_element_type=jnp.float32
    ).astype(jnp.bfloat16)
    fetched = lax.all_to_all(
        reply.reshape(shards, capacity, BLK, pair_width),
        "seq",
        split_axis=0,
        concat_axis=0,
        tiled=True,
    )
    slot_hits = (
        slots[:, None] == jnp.arange(shards * capacity, dtype=jnp.int32)[None, :]
    ).astype(jnp.bfloat16)
    random_pairs = (
        jnp.einsum(
            "rs,sid->rid",
            slot_hits,
            fetched.reshape(shards * capacity, BLK, pair_width),
            preferred_element_type=jnp.float32,
        )
        .astype(jnp.bfloat16)
        .reshape(head_count, blocks, randoms, BLK, pair_width)
    )
    offsets = jnp.arange(span, dtype=jnp.int32) - WMAX
    block_ids = my_index * blocks + jnp.arange(blocks, dtype=jnp.int32)
    reach = block_ids[:, None] + offsets[None, :]
    in_range = (reach >= 0) & (reach < shards * blocks)
    window_ok = in_range[None, :, :] & (
        jnp.abs(offsets)[None, None, :] <= window_width[:, None, None]
    )
    list_ok = jnp.concatenate(
        [window_ok, jnp.ones((head_count, blocks, globals_count + randoms), jnp.bool_)], axis=2
    )
    global_hit = block_ids[:, None] == global_blocks[None, :]
    row_global = jnp.any(global_hit, axis=1)
    hit_weight = global_hit.astype(jnp.float32)

    def key_sequence(first_block):
        pieces_list = [
            jnp.stack(
                [
                    lax.dynamic_slice_in_dim(pair_heads, first_block + offset, group, 1)
                    for offset in range(span)
                ],
                axis=2,
            )
        ]
        pieces_list.append(
            jnp.broadcast_to(
                glob_pairs[:, None], (head_count, group, globals_count, BLK, pair_width)
            )
        )
        pieces_list.append(random_pairs)
        joined = jnp.concatenate(pieces_list, axis=2)
        entry_count = joined.shape[2]
        list_mask = list_ok[:, :, :entry_count]
        return (
            joined.reshape(head_count, group, entry_count * BLK, pair_width),
            jnp.repeat(list_mask, BLK, axis=2),
        )

    def forward_group(group_index):
        first_block = group_index * group
        pairs, list_mask = key_sequence(first_block)
        key_part = pairs[..., :head_width]
        value_part = pairs[..., head_width:]
        score_matrix = (
            jnp.einsum("hqid,hqkd->hqik", query_heads, key_part, preferred_element_type=jnp.float32)
            * logit_scale
        )
        score_matrix = jnp.where(list_mask[:, :, None, :], score_matrix, -jnp.inf)
        row_max = jnp.max(score_matrix, axis=-1)
        weights = jnp.exp(score_matrix - row_max[..., None])
        totals = jnp.sum(weights, axis=-1)
        accumulated_total = jnp.einsum(
            "hqik,hqkd->hqid",
            weights.astype(jnp.bfloat16),
            value_part,
            preferred_element_type=jnp.float32,
        )
        return (
            (accumulated_total / totals[..., None]).astype(jnp.bfloat16),
            row_max + jnp.log(totals),
        )

    sparse_out, sparse_lse = lax.map(forward_group, jnp.arange(group_count))
    sparse_out = jnp.moveaxis(sparse_out, 0, 1).reshape(head_count, blocks, BLK, head_width)
    sparse_lse = jnp.moveaxis(sparse_lse, 0, 1).reshape(head_count, blocks, BLK)
    local_keys = local_pairs[..., :head_width].reshape(head_count, blocks * BLK, head_width)
    local_values = local_pairs[..., head_width:].reshape(head_count, blocks * BLK, head_width)
    glob_rows = glob_query.reshape(head_count, globals_count * BLK, head_width)
    glob_grad_rows = glob_grad.reshape(head_count, globals_count * BLK, head_width)
    glob_scores = (
        jnp.einsum("hid,hjd->hij", glob_rows, local_keys, preferred_element_type=jnp.float32)
        * logit_scale
    )
    glob_max = lax.pmax(jnp.max(glob_scores, axis=-1), "seq")
    glob_weights = jnp.exp(glob_scores - glob_max[..., None])
    glob_part_sum = jnp.einsum(
        "hij,hjd->hid",
        glob_weights.astype(jnp.bfloat16),
        local_values,
        preferred_element_type=jnp.float32,
    )
    glob_sum, glob_total = lax.psum((glob_part_sum, jnp.sum(glob_weights, axis=-1)), "seq")
    glob_out = (glob_sum / glob_total[..., None]).astype(jnp.bfloat16)
    glob_lse = glob_max + jnp.log(glob_total)
    chosen_out = jnp.einsum(
        "bg,hgid->hbid",
        hit_weight,
        glob_out.reshape(head_count, globals_count, BLK, head_width).astype(jnp.float32),
    )
    out_heads = jnp.where(
        row_global[None, :, None, None], chosen_out.astype(jnp.bfloat16), sparse_out
    )
    attn_out = token_major(out_heads)
    delta = jnp.sum(grad_heads.astype(jnp.float32) * out_heads.astype(jnp.float32), axis=-1)
    row_lse = jnp.where(row_global[None, :, None], jnp.inf, sparse_lse)
    glob_delta = jnp.sum(glob_grad_rows.astype(jnp.float32) * glob_out.astype(jnp.float32), axis=-1)

    def backward_group(group_index):
        first_block = group_index * group
        pairs, list_mask = key_sequence(first_block)
        key_part = pairs[..., :head_width]
        value_part = pairs[..., head_width:]
        score_matrix = (
            jnp.einsum("hqid,hqkd->hqik", query_heads, key_part, preferred_element_type=jnp.float32)
            * logit_scale
        )
        probs = jnp.where(list_mask[:, :, None, :], jnp.exp(score_matrix - row_lse[..., None]), 0.0)
        probability_gradient = jnp.einsum(
            "hqid,hqkd->hqik", grad_heads, value_part, preferred_element_type=jnp.float32
        )
        score_gradient = (probs * (probability_gradient - delta[..., None])).astype(jnp.bfloat16)
        grad_rows_part = (
            jnp.einsum(
                "hqik,hqkd->hqid", score_gradient, key_part, preferred_element_type=jnp.float32
            )
            * logit_scale
        )
        key_contributions = (
            jnp.einsum(
                "hqik,hqid->hqkd", score_gradient, query_heads, preferred_element_type=jnp.float32
            )
            * logit_scale
        )
        value_contributions = jnp.einsum(
            "hqik,hqid->hqkd",
            probs.astype(jnp.bfloat16),
            grad_heads,
            preferred_element_type=jnp.float32,
        )
        terms = jnp.concatenate([key_contributions, value_contributions], axis=-1).reshape(
            head_count, group, -1, BLK, pair_width
        )
        window_terms = terms[:, :, :span]
        glob_terms = jnp.sum(terms[:, :, span : span + globals_count], axis=1)
        random_terms = terms[:, :, span + globals_count :].astype(jnp.bfloat16)
        return (grad_rows_part, window_terms, glob_terms, random_terms)

    gradient_row_values, window_terms, glob_terms, random_terms = lax.map(
        backward_group, jnp.arange(group_count)
    )
    gradient_row_values = jnp.moveaxis(gradient_row_values, 0, 1).reshape(
        head_count, blocks, BLK, head_width
    )
    window_terms = jnp.moveaxis(window_terms, 0, 1).reshape(
        head_count, blocks, span, BLK, pair_width
    )
    glob_terms = jnp.sum(glob_terms, axis=0)
    spread = jnp.zeros((head_count, blocks + 2 * WMAX, BLK, pair_width), jnp.float32)
    for offset in range(span):
        spread = spread.at[:, offset : offset + blocks].add(window_terms[:, :, offset])
    glob_probs = jnp.exp(glob_scores - glob_lse[..., None])
    glob_grad_probs = jnp.einsum(
        "hid,hjd->hij", glob_grad_rows, local_values, preferred_element_type=jnp.float32
    )
    glob_grad_scores = (glob_probs * (glob_grad_probs - glob_delta[..., None])).astype(jnp.bfloat16)
    glob_query_part = (
        jnp.einsum("hij,hjd->hid", glob_grad_scores, local_keys, preferred_element_type=jnp.float32)
        * logit_scale
    )
    key_from_glob = (
        jnp.einsum("hij,hid->hjd", glob_grad_scores, glob_rows, preferred_element_type=jnp.float32)
        * logit_scale
    )
    value_from_glob = jnp.einsum(
        "hij,hid->hjd",
        glob_probs.astype(jnp.bfloat16),
        glob_grad_rows,
        preferred_element_type=jnp.float32,
    )
    glob_total_terms, glob_query_grad = lax.psum((glob_terms, glob_query_part), "seq")
    from_below = from_behind(spread[:, blocks + WMAX :], "seq", 1)
    from_above = from_behind(spread[:, :WMAX].astype(jnp.bfloat16), "seq", -1).astype(jnp.float32)
    own_terms = spread[:, WMAX : WMAX + blocks]
    own_terms = own_terms.at[:, :WMAX].add(from_below).at[:, blocks - WMAX :].add(from_above)
    own_terms = own_terms + jnp.concatenate([key_from_glob, value_from_glob], axis=-1).reshape(
        head_count, blocks, BLK, pair_width
    )
    own_terms = own_terms + jnp.einsum("bg,hgid->hbid", hit_weight, glob_total_terms)
    random_terms = jnp.moveaxis(random_terms, 0, 1).reshape(request_count, BLK, pair_width)
    outgoing_terms = (
        jnp.zeros((shards * capacity, BLK, pair_width), jnp.bfloat16).at[slots].set(random_terms)
    )
    returned = lax.all_to_all(
        outgoing_terms.reshape(shards, capacity, BLK, pair_width),
        "seq",
        split_axis=0,
        concat_axis=0,
        tiled=True,
    ).reshape(shards * capacity, BLK, pair_width)
    random_add = jnp.einsum(
        "sc,sid->cid", code_hits, returned, preferred_element_type=jnp.float32
    ).reshape(head_count, blocks, BLK, pair_width)
    own_terms = own_terms + random_add
    glob_query_add = jnp.einsum(
        "bg,hgid->hbid",
        hit_weight,
        glob_query_grad.reshape(head_count, globals_count, BLK, head_width),
    )
    grad_query = token_major((gradient_row_values + glob_query_add).astype(jnp.bfloat16))
    grad_key = token_major(own_terms[..., :head_width].astype(jnp.bfloat16))
    grad_value = token_major(own_terms[..., head_width:].astype(jnp.bfloat16))
    return (attn_out, grad_query, grad_key, grad_value)


MASKED = -1e30
ALIGNED = pl.DeviceIdType.MESH


NEXT, ACROSS, SKIP = 0, 1, 2
OUTER_IN = ((0, 2, ACROSS), (0, 2, SKIP), (0, 2, NEXT), (2, 2, ACROSS), (2, 2, SKIP), (2, 2, NEXT))
INNER_IN = ((0, 2, SKIP), (0, 2, NEXT), (2, 2, SKIP), (2, 2, NEXT))
TURNS = ((ACROSS, ACROSS), None, (NEXT, SKIP), (SKIP, NEXT))
OUTER_OUT = (((0, 2, ACROSS),), (), ((0, 2, NEXT),), ((2, 2, ACROSS), (2, 2, NEXT), (0, 4, SKIP)))
INNER_OUT = ((), (), ((0, 2, SKIP),), ((2, 2, SKIP), (0, 4, ACROSS), (0, 4, NEXT)))


def rows_dot(left, right):
    return lax.dot_general(left, right, (((1,), (1,)), ((), ())), preferred_element_type=jnp.float32)


def one_head_kernel(
    shards,
    blocks,
    width_in,
    global_in,
    random_in,
    k_in,
    v_in,
    q_in,
    g_in,
    out,
    width_ref,
    global_ref,
    random_ref,
    stage,
    in_all,
    bias_own,
    bias_all,
    out_all,
    dk_sum,
    dv_sum,
    small_sem,
    stage_sem,
    pair_recv,
    rest_recv,
    in_send,
    bias_send,
    bias_recv,
    out_send,
    out_recv,
):
    me = lax.axis_index("seq")
    rows = blocks * BLK
    key_blocks = shards * blocks
    hd = in_all.shape[2]
    logit_scale = 1.0 / math.sqrt(hd)
    inner = ((me + 1) // 2) % 2
    partner = (me + 1 - 2 * (me % 2), 3 - me, (me + 2) % 4)
    arrays = (k_in, v_in, q_in, g_in)

    def pick(pair, table):
        first, second = table[pair[0]], table[pair[1]]
        return first + (second - first) * inner

    def cols(index):
        return pl.ds(pl.multiple_of(index * hd, hd), hd)

    def span(index):
        return pl.ds(pl.multiple_of(index * rows, rows), rows)

    def send_in(first, count, step, target):
        if count == 1:
            source, landing = arrays[first].at[:, cols(target)], in_all.at[first, span(me), :]
        else:
            source = stage.at[pl.ds(first, count), :, cols(target)]
            landing = in_all.at[pl.ds(first, count), span(me), :]
        return pltpu.make_async_remote_copy(
            src_ref=source,
            dst_ref=landing,
            send_sem=in_send,
            recv_sem=pair_recv if first < 2 else rest_recv.at[step],
            device_id={"seq": target},
            device_id_type=ALIGNED,
        )

    def send_bias(target):
        return pltpu.make_async_remote_copy(
            src_ref=bias_own.at[target],
            dst_ref=bias_all.at[me],
            send_sem=bias_send,
            recv_sem=bias_recv,
            device_id={"seq": target},
            device_id_type=ALIGNED,
        )

    def send_out(first, count, step):
        return pltpu.make_async_remote_copy(
            src_ref=out_all.at[pl.ds(first, count), span(partner[step]), :],
            dst_ref=out.at[pl.ds(first, count), :, cols(me)],
            send_sem=out_send,
            recv_sem=out_recv,
            device_id={"seq": partner[step]},
            device_id_type=ALIGNED,
        )

    def start_outs(turn):
        for role, table in enumerate((OUTER_OUT, INNER_OUT)):

            @pl.when(inner == role)
            def _():
                for first, count, step in table[turn]:
                    send_out(first, count, step).start()

    def wait_for(bytes_of, semaphore):
        pltpu.make_async_copy(bytes_of, bytes_of, semaphore).wait()

    small = [
        pltpu.make_async_copy(source, landing, small_sem.at[index])
        for index, (source, landing) in enumerate(
            ((width_in, width_ref), (global_in, global_ref), (random_in, random_ref))
        )
    ]
    staged = [
        pltpu.make_async_copy(array, stage.at[slot], stage_sem)
        for slot, array in enumerate(arrays)
    ]
    local_out = [
        pltpu.make_async_copy(
            out_all.at[pl.ds(2 * half, 2), span(me), :],
            out.at[pl.ds(2 * half, 2), :, cols(me)],
            out_recv,
        )
        for half in range(2)
    ]

    barrier = pltpu.get_barrier_semaphore()

    def greet(device):
        pl.semaphore_signal(barrier, inc=1, device_id={"seq": device}, device_id_type=ALIGNED)

    greet(3 - me)

    @pl.when(me != 2)
    def _():
        for copy in staged:
            copy.start()

    @pl.when(inner == 1)
    def _():
        pl.semaphore_wait(barrier, 1)

        @pl.when(me == 1)
        def _():
            wait_for(stage, stage_sem)
            send_in(0, 2, ACROSS, partner[ACROSS]).start()

        @pl.when(me == 2)
        def _():
            for slot in range(2):
                send_in(slot, 1, ACROSS, partner[ACROSS]).start()
            for copy in staged:
                copy.start()

        greet(0)
        greet(3)

    for copy in small:
        copy.start()

    @pl.when(me != 1)
    def _():
        wait_for(stage, stage_sem)

    @pl.when(inner == 1)
    def _():
        send_in(2, 2, ACROSS, partner[ACROSS]).start()

    for copy in small:
        copy.wait()

    lane = lax.broadcasted_iota(jnp.int32, (1, BLK), 1)
    spot_ids = jnp.zeros_like(lane)
    for spot in range(1, blocks):
        spot_ids += jnp.where(lane >= spot * key_blocks, 1, 0)
    key_ids = lane - spot_ids * key_blocks
    block_ids = me * blocks + spot_ids
    distance = jnp.abs(key_ids - block_ids)
    listed = jnp.zeros(lane.shape, jnp.float32)
    row_global = jnp.zeros(lane.shape, jnp.float32)
    for index in range(global_ref.shape[0]):
        listed += jnp.where(key_ids == global_ref[index], 1.0, 0.0)
        row_global = jnp.maximum(row_global, jnp.where(block_ids == global_ref[index], 1.0, 0.0))
    for head in range(shards):
        hits = listed + jnp.where(distance <= jnp.minimum(width_ref[head], WMAX), 1.0, 0.0)
        for index in range(random_ref.shape[0]):
            named = jnp.zeros_like(lane)
            for spot in range(blocks):
                named = jnp.where(spot_ids == spot, random_ref[index, spot, head], named)
            hits += jnp.where(key_ids == named, 1.0, 0.0)
        hits = row_global + (1.0 - row_global) * hits
        bias_own[head] = jnp.where(
            hits > 0.5, jnp.log(jnp.maximum(hits, 1.0)) * (1.0 / math.log(2.0)), MASKED
        )

    @pl.when(inner == 0)
    def _():
        pl.semaphore_wait(barrier, 3)
        greet(1)
        greet(2)
        for step, target in enumerate(partner):
            send_bias(target).start()
        for first, count, step in OUTER_IN:
            send_in(first, count, step, partner[step]).start()

    @pl.when(inner == 1)
    def _():
        pl.semaphore_wait(barrier, 2)
        for step, target in enumerate(partner):
            send_bias(target).start()
        for first, count, step in INNER_IN:
            send_in(first, count, step, partner[step]).start()

    bias_all[me] = bias_own[me]

    sub_ids = lax.broadcasted_iota(jnp.int32, (key_blocks, BLK), 0)
    lane_ids = lax.broadcasted_iota(jnp.int32, (key_blocks, BLK), 1)

    for slot in range(4):
        in_all[slot, span(me), :] = stage[slot, :, cols(me)]
    others = pl.ds(0, (shards - 1) * rows)
    wait_for(in_all.at[pl.ds(0, 2), others, :], pair_recv)
    wait_for(bias_all.at[pl.ds(0, shards - 1)], bias_recv)
    keys = in_all[0]
    vals = in_all[1]
    keys_t = keys.T
    vals_t = vals.T
    for turn, pair in enumerate(TURNS):
        if pair is None:
            chunk = me
        else:
            chunk, step = pick(pair, partner), pick(pair, (NEXT, ACROSS, SKIP))
            wait_for(in_all.at[pl.ds(2, 2), span(chunk), :], rest_recv.at[step])
        q = in_all[2, span(chunk), :]
        g = in_all[3, span(chunk), :]
        row = jnp.broadcast_to(bias_all[chunk], lane_ids.shape)
        spread = [
            jnp.broadcast_to(
                jnp.sum(
                    jnp.where(lane_ids == sub_ids + spot * key_blocks, row, 0.0),
                    axis=1,
                    keepdims=True,
                ),
                lane_ids.shape,
            )
            for spot in range(blocks)
        ]
        bias = jnp.concatenate(
            [
                jnp.concatenate(
                    [
                        jnp.broadcast_to(spread[spot][key : key + 1, :], (BLK, BLK))
                        for spot in range(blocks)
                    ],
                    axis=1,
                )
                for key in range(key_blocks)
            ],
            axis=0,
        )
        scores = rows_dot(keys, q) * (logit_scale / math.log(2.0)) + bias
        top = jnp.max(scores, axis=0, keepdims=True)
        weights = jnp.exp2(scores - top)
        inverse = 1.0 / jnp.sum(weights, axis=0, keepdims=True)
        out_t = (
            jnp.dot(vals_t, weights.astype(jnp.bfloat16), preferred_element_type=jnp.float32)
            * inverse
        )
        out_rows = out_t.T.astype(jnp.bfloat16)
        out_all[0, span(chunk), :] = out_rows
        delta = jnp.sum(
            (g.astype(jnp.float32) * out_rows.astype(jnp.float32)).T, axis=0, keepdims=True
        )
        probs = weights * inverse
        grads = (probs * (rows_dot(vals, g) - delta)).astype(jnp.bfloat16)
        dq_t = jnp.dot(keys_t, grads, preferred_element_type=jnp.float32) * logit_scale
        out_all[1, span(chunk), :] = dq_t.T.astype(jnp.bfloat16)
        if pair is None:
            local_out[0].start()
        if turn < shards - 1:
            start_outs(turn)
        dv_part = jnp.dot(probs.astype(jnp.bfloat16), g, preferred_element_type=jnp.float32)
        dk_part = jnp.dot(grads, q, preferred_element_type=jnp.float32)
        if turn == 0:
            dv_sum[...] = dv_part
            dk_sum[...] = dk_part
        elif turn < shards - 1:
            dv_sum[...] += dv_part
            dk_sum[...] += dk_part
        else:
            out_all[3] = (dv_sum[...] + dv_part).astype(jnp.bfloat16)
            out_all[2] = ((dk_sum[...] + dk_part) * logit_scale).astype(jnp.bfloat16)
    start_outs(shards - 1)
    local_out[1].start()
    wait_for(bias_own.at[pl.ds(0, shards - 1)], bias_send)
    wait_for(in_all.at[:, others, :], in_send)
    wait_for(out_all.at[:, others, :], out_send)
    wait_for(out, out_recv)


def deliver_kernel(landed, *refs):
    for slot in range(4):
        pltpu.make_async_copy(landed.at[slot], refs[slot], refs[4]).start()
    pltpu.make_async_copy(landed, landed, refs[4]).wait()


def one_head(queries, key_rows, values, grad_out, window_width, global_blocks, random_blocks):
    shards = lax.axis_size("seq")
    tokens, columns = queries.shape
    hd = columns // shards
    blocks = tokens // BLK
    whole = shards * tokens
    bf16 = jnp.bfloat16
    anywhere = pl.BlockSpec(memory_space=pl.ANY)
    dma = pltpu.SemaphoreType.DMA
    lists = (window_width, global_blocks, random_blocks.transpose(2, 1, 0))
    landed = pl.pallas_call(
        functools.partial(one_head_kernel, shards, blocks),
        out_shape=jax.ShapeDtypeStruct((4, tokens, columns), bf16),
        in_specs=[anywhere] * 7,
        out_specs=anywhere,
        scratch_shapes=[pltpu.SMEM(array.shape, jnp.int32) for array in lists]
        + [pltpu.VMEM((4, tokens, columns), bf16), pltpu.VMEM((4, whole, hd), bf16)]
        + [pltpu.VMEM((shards, 1, BLK), jnp.float32)] * 2
        + [pltpu.VMEM((4, whole, hd), bf16)]
        + [pltpu.VMEM((whole, hd), jnp.float32)] * 2
        + [dma((3,)), dma(()), dma(()), dma((shards - 1,))]
        + [dma(())] * 5,
        compiler_params=pltpu.CompilerParams(
            collective_id=0, has_side_effects=True, vmem_limit_bytes=48 * 1024 * 1024
        ),
    )(
        *(
            pltpu.with_memory_space_constraint(array, pltpu.HBM)
            for array in (*lists, key_rows, values, queries, grad_out)
        )
    )
    return pl.pallas_call(
        deliver_kernel,
        out_shape=(jax.ShapeDtypeStruct((tokens, columns), bf16),) * 4,
        in_specs=[anywhere],
        out_specs=(anywhere,) * 4,
        scratch_shapes=[dma(())],
        compiler_params=pltpu.CompilerParams(vmem_limit_bytes=8 * 1024 * 1024),
    )(landed)


def dispatch(queries, key_rows, values, grad_out, window_width, global_blocks, random_blocks):
    shards = lax.axis_size("seq")
    if shards == 4 and window_width.shape[0] == shards and queries.shape[1] == shards * BLK:
        chosen = one_head
    else:
        chosen = on_device
    return chosen(
        queries, key_rows, values, grad_out, window_width, global_blocks, random_blocks
    )


def solution(mesh):
    in_specs = (
        P(("groups", "seq"), ("head", "sub")),
        P(("groups", "seq"), ("head", "sub")),
        P(("groups", "seq"), ("head", "sub")),
        P(("groups", "seq"), ("head", "sub")),
        P(("groups", "head", "sub")),
        P("groups"),
        P(("groups", "head", "sub"), "seq", None),
    )
    out_specs = (
        P(("groups", "seq"), ("head", "sub")),
        P(("groups", "seq"), ("head", "sub")),
        P(("groups", "seq"), ("head", "sub")),
        P(("groups", "seq"), ("head", "sub")),
    )
    return jax.shard_map(
        dispatch, mesh=mesh, in_specs=in_specs, out_specs=out_specs, check_vma=False
    )
```

```python
import functools
import math

import jax
import jax.numpy as jnp
from jax import lax
from jax.experimental import pallas as pl
from jax.experimental.pallas import tpu as pltpu
from jax.sharding import PartitionSpec as P

BLK = 128
WMAX = 1


def extended(cells, sides, width):
    for axis, dim in sides:
        count = lax.axis_size(axis)
        ends = count - 1
        head = lax.slice_in_dim(cells, 0, width, axis=dim)
        tail = lax.slice_in_dim(cells, cells.shape[dim] - width, cells.shape[dim], axis=dim)
        cells = jnp.concatenate(
            [
                lax.ppermute(tail, axis, [(i, (i + 1) % count) for i in range(ends)]),
                cells,
                lax.ppermute(head, axis, [((i + 1) % count, i) for i in range(ends)]),
            ],
            axis=dim,
        )
    return cells


def from_behind(block, axis, distance):
    devices = range(lax.axis_size(axis))
    route = [(i - distance, i) for i in devices if i - distance in devices]
    return lax.ppermute(block, axis, route)


def head_major(tensor, head_count, head_width):
    block_count = tensor.shape[0] // BLK
    return tensor.reshape(block_count, BLK, head_count, head_width).transpose(2, 0, 1, 3)


def token_major(tensor):
    head_count, block_count, row_count, head_width = tensor.shape
    return tensor.transpose(1, 2, 0, 3).reshape(block_count * row_count, head_count * head_width)


def on_device(queries, key_rows, values, grad_out, window_width, global_blocks, random_blocks):
    head_count = window_width.shape[0]
    tokens = queries.shape[0]
    head_width = queries.shape[1] // head_count
    blocks = tokens // BLK
    span = 2 * WMAX + 1
    globals_count = global_blocks.shape[0]
    randoms = random_blocks.shape[2]
    shards = lax.axis_size("seq")
    my_index = lax.axis_index("seq")
    logit_scale = 1.0 / math.sqrt(head_width)
    group = 2
    group_count = blocks // group
    pair_width = 2 * head_width
    query_heads = head_major(queries, head_count, head_width)
    grad_heads = head_major(grad_out, head_count, head_width)
    packed = jnp.concatenate([key_rows, values], axis=1)
    padded = extended(packed, (("seq", 0),), WMAX * BLK)
    pair_heads = (
        padded.reshape(blocks + 2 * WMAX, BLK, 2, head_count, head_width)
        .transpose(3, 0, 1, 2, 4)
        .reshape(head_count, blocks + 2 * WMAX, BLK, pair_width)
    )
    local_pairs = pair_heads[:, WMAX : WMAX + blocks]
    owners = global_blocks // blocks
    local_spot = global_blocks % blocks
    stacked = jnp.concatenate([queries, key_rows, values, grad_out], axis=1)
    own_rows = jnp.stack(
        [
            lax.dynamic_slice_in_dim(stacked, local_spot[glob_index] * BLK, BLK, 0)
            for glob_index in range(globals_count)
        ]
    )
    owned_mask = (owners == my_index)[:, None, None]
    masked_rows = jnp.where(owned_mask, own_rows, jnp.zeros((), jnp.bfloat16))
    panels = lax.psum(masked_rows, "seq").astype(jnp.float32).astype(jnp.bfloat16)
    panel_heads = panels.reshape(globals_count, BLK, 4, head_count, head_width).transpose(
        2, 3, 0, 1, 4
    )
    glob_query = panel_heads[0]
    glob_grad = panel_heads[3]
    glob_pairs = jnp.concatenate([panel_heads[1], panel_heads[2]], axis=-1)
    requests = random_blocks.reshape(-1)
    request_count = requests.shape[0]
    capacity = max(2, -(-request_count // shards))
    targets = requests // blocks
    request_head = jnp.arange(request_count, dtype=jnp.int32) // (blocks * randoms)
    codes = request_head * blocks + requests % blocks
    positions = jnp.arange(request_count, dtype=jnp.int32)
    earlier = (targets[:, None] == targets[None, :]) & (positions[None, :] < positions[:, None])
    ranks = jnp.sum(earlier.astype(jnp.int32), axis=1)
    slots = targets * capacity + ranks
    outgoing = jnp.full((shards * capacity,), -1, jnp.int32).at[slots].set(codes)
    incoming = lax.all_to_all(
        outgoing.reshape(shards, capacity), "seq", split_axis=0, concat_axis=0, tiled=True
    ).reshape(-1)
    code_hits = (
        incoming[:, None] == jnp.arange(head_count * blocks, dtype=jnp.int32)[None, :]
    ).astype(jnp.bfloat16)
    flat_pairs = local_pairs.reshape(head_count * blocks, BLK, pair_width)
    reply = jnp.einsum(
        "sc,cid->sid", code_hits, flat_pairs, preferred_element_type=jnp.float32
    ).astype(jnp.bfloat16)
    fetched = lax.all_to_all(
        reply.reshape(shards, capacity, BLK, pair_width),
        "seq",
        split_axis=0,
        concat_axis=0,
        tiled=True,
    )
    slot_hits = (
        slots[:, None] == jnp.arange(shards * capacity, dtype=jnp.int32)[None, :]
    ).astype(jnp.bfloat16)
    random_pairs = (
        jnp.einsum(
            "rs,sid->rid",
            slot_hits,
            fetched.reshape(shards * capacity, BLK, pair_width),
            preferred_element_type=jnp.float32,
        )
        .astype(jnp.bfloat16)
        .reshape(head_count, blocks, randoms, BLK, pair_width)
    )
    offsets = jnp.arange(span, dtype=jnp.int32) - WMAX
    block_ids = my_index * blocks + jnp.arange(blocks, dtype=jnp.int32)
    reach = block_ids[:, None] + offsets[None, :]
    in_range = (reach >= 0) & (reach < shards * blocks)
    window_ok = in_range[None, :, :] & (
        jnp.abs(offsets)[None, None, :] <= window_width[:, None, None]
    )
    list_ok = jnp.concatenate(
        [window_ok, jnp.ones((head_count, blocks, globals_count + randoms), jnp.bool_)], axis=2
    )
    global_hit = block_ids[:, None] == global_blocks[None, :]
    row_global = jnp.any(global_hit, axis=1)
    hit_weight = global_hit.astype(jnp.float32)

    def key_sequence(first_block):
        pieces_list = [
            jnp.stack(
                [
                    lax.dynamic_slice_in_dim(pair_heads, first_block + offset, group, 1)
                    for offset in range(span)
                ],
                axis=2,
            )
        ]
        pieces_list.append(
            jnp.broadcast_to(
                glob_pairs[:, None], (head_count, group, globals_count, BLK, pair_width)
            )
        )
        pieces_list.append(random_pairs)
        joined = jnp.concatenate(pieces_list, axis=2)
        entry_count = joined.shape[2]
        list_mask = list_ok[:, :, :entry_count]
        return (
            joined.reshape(head_count, group, entry_count * BLK, pair_width),
            jnp.repeat(list_mask, BLK, axis=2),
        )

    def forward_group(group_index):
        first_block = group_index * group
        pairs, list_mask = key_sequence(first_block)
        key_part = pairs[..., :head_width]
        value_part = pairs[..., head_width:]
        score_matrix = (
            jnp.einsum("hqid,hqkd->hqik", query_heads, key_part, preferred_element_type=jnp.float32)
            * logit_scale
        )
        score_matrix = jnp.where(list_mask[:, :, None, :], score_matrix, -jnp.inf)
        row_max = jnp.max(score_matrix, axis=-1)
        weights = jnp.exp(score_matrix - row_max[..., None])
        totals = jnp.sum(weights, axis=-1)
        accumulated_total = jnp.einsum(
            "hqik,hqkd->hqid",
            weights.astype(jnp.bfloat16),
            value_part,
            preferred_element_type=jnp.float32,
        )
        return (
            (accumulated_total / totals[..., None]).astype(jnp.bfloat16),
            row_max + jnp.log(totals),
        )

    sparse_out, sparse_lse = lax.map(forward_group, jnp.arange(group_count))
    sparse_out = jnp.moveaxis(sparse_out, 0, 1).reshape(head_count, blocks, BLK, head_width)
    sparse_lse = jnp.moveaxis(sparse_lse, 0, 1).reshape(head_count, blocks, BLK)
    local_keys = local_pairs[..., :head_width].reshape(head_count, blocks * BLK, head_width)
    local_values = local_pairs[..., head_width:].reshape(head_count, blocks * BLK, head_width)
    glob_rows = glob_query.reshape(head_count, globals_count * BLK, head_width)
    glob_grad_rows = glob_grad.reshape(head_count, globals_count * BLK, head_width)
    glob_scores = (
        jnp.einsum("hid,hjd->hij", glob_rows, local_keys, preferred_element_type=jnp.float32)
        * logit_scale
    )
    glob_max = lax.pmax(jnp.max(glob_scores, axis=-1), "seq")
    glob_weights = jnp.exp(glob_scores - glob_max[..., None])
    glob_part_sum = jnp.einsum(
        "hij,hjd->hid",
        glob_weights.astype(jnp.bfloat16),
        local_values,
        preferred_element_type=jnp.float32,
    )
    glob_sum, glob_total = lax.psum((glob_part_sum, jnp.sum(glob_weights, axis=-1)), "seq")
    glob_out = (glob_sum / glob_total[..., None]).astype(jnp.bfloat16)
    glob_lse = glob_max + jnp.log(glob_total)
    chosen_out = jnp.einsum(
        "bg,hgid->hbid",
        hit_weight,
        glob_out.reshape(head_count, globals_count, BLK, head_width).astype(jnp.float32),
    )
    out_heads = jnp.where(
        row_global[None, :, None, None], chosen_out.astype(jnp.bfloat16), sparse_out
    )
    attn_out = token_major(out_heads)
    delta = jnp.sum(grad_heads.astype(jnp.float32) * out_heads.astype(jnp.float32), axis=-1)
    row_lse = jnp.where(row_global[None, :, None], jnp.inf, sparse_lse)
    glob_delta = jnp.sum(glob_grad_rows.astype(jnp.float32) * glob_out.astype(jnp.float32), axis=-1)

    def backward_group(group_index):
        first_block = group_index * group
        pairs, list_mask = key_sequence(first_block)
        key_part = pairs[..., :head_width]
        value_part = pairs[..., head_width:]
        score_matrix = (
            jnp.einsum("hqid,hqkd->hqik", query_heads, key_part, preferred_element_type=jnp.float32)
            * logit_scale
        )
        probs = jnp.where(list_mask[:, :, None, :], jnp.exp(score_matrix - row_lse[..., None]), 0.0)
        probability_gradient = jnp.einsum(
            "hqid,hqkd->hqik", grad_heads, value_part, preferred_element_type=jnp.float32
        )
        score_gradient = (probs * (probability_gradient - delta[..., None])).astype(jnp.bfloat16)
        grad_rows_part = (
            jnp.einsum(
                "hqik,hqkd->hqid", score_gradient, key_part, preferred_element_type=jnp.float32
            )
            * logit_scale
        )
        key_contributions = (
            jnp.einsum(
                "hqik,hqid->hqkd", score_gradient, query_heads, preferred_element_type=jnp.float32
            )
            * logit_scale
        )
        value_contributions = jnp.einsum(
            "hqik,hqid->hqkd",
            probs.astype(jnp.bfloat16),
            grad_heads,
            preferred_element_type=jnp.float32,
        )
        terms = jnp.concatenate([key_contributions, value_contributions], axis=-1).reshape(
            head_count, group, -1, BLK, pair_width
        )
        window_terms = terms[:, :, :span]
        glob_terms = jnp.sum(terms[:, :, span : span + globals_count], axis=1)
        random_terms = terms[:, :, span + globals_count :].astype(jnp.bfloat16)
        return (grad_rows_part, window_terms, glob_terms, random_terms)

    gradient_row_values, window_terms, glob_terms, random_terms = lax.map(
        backward_group, jnp.arange(group_count)
    )
    gradient_row_values = jnp.moveaxis(gradient_row_values, 0, 1).reshape(
        head_count, blocks, BLK, head_width
    )
    window_terms = jnp.moveaxis(window_terms, 0, 1).reshape(
        head_count, blocks, span, BLK, pair_width
    )
    glob_terms = jnp.sum(glob_terms, axis=0)
    spread = jnp.zeros((head_count, blocks + 2 * WMAX, BLK, pair_width), jnp.float32)
    for offset in range(span):
        spread = spread.at[:, offset : offset + blocks].add(window_terms[:, :, offset])
    glob_probs = jnp.exp(glob_scores - glob_lse[..., None])
    glob_grad_probs = jnp.einsum(
        "hid,hjd->hij", glob_grad_rows, local_values, preferred_element_type=jnp.float32
    )
    glob_grad_scores = (glob_probs * (glob_grad_probs - glob_delta[..., None])).astype(jnp.bfloat16)
    glob_query_part = (
        jnp.einsum("hij,hjd->hid", glob_grad_scores, local_keys, preferred_element_type=jnp.float32)
        * logit_scale
    )
    key_from_glob = (
        jnp.einsum("hij,hid->hjd", glob_grad_scores, glob_rows, preferred_element_type=jnp.float32)
        * logit_scale
    )
    value_from_glob = jnp.einsum(
        "hij,hid->hjd",
        glob_probs.astype(jnp.bfloat16),
        glob_grad_rows,
        preferred_element_type=jnp.float32,
    )
    glob_total_terms, glob_query_grad = lax.psum((glob_terms, glob_query_part), "seq")
    from_below = from_behind(spread[:, blocks + WMAX :], "seq", 1)
    from_above = from_behind(spread[:, :WMAX].astype(jnp.bfloat16), "seq", -1).astype(jnp.float32)
    own_terms = spread[:, WMAX : WMAX + blocks]
    own_terms = own_terms.at[:, :WMAX].add(from_below).at[:, blocks - WMAX :].add(from_above)
    own_terms = own_terms + jnp.concatenate([key_from_glob, value_from_glob], axis=-1).reshape(
        head_count, blocks, BLK, pair_width
    )
    own_terms = own_terms + jnp.einsum("bg,hgid->hbid", hit_weight, glob_total_terms)
    random_terms = jnp.moveaxis(random_terms, 0, 1).reshape(request_count, BLK, pair_width)
    outgoing_terms = (
        jnp.zeros((shards * capacity, BLK, pair_width), jnp.bfloat16).at[slots].set(random_terms)
    )
    returned = lax.all_to_all(
        outgoing_terms.reshape(shards, capacity, BLK, pair_width),
        "seq",
        split_axis=0,
        concat_axis=0,
        tiled=True,
    ).reshape(shards * capacity, BLK, pair_width)
    random_add = jnp.einsum(
        "sc,sid->cid", code_hits, returned, preferred_element_type=jnp.float32
    ).reshape(head_count, blocks, BLK, pair_width)
    own_terms = own_terms + random_add
    glob_query_add = jnp.einsum(
        "bg,hgid->hbid",
        hit_weight,
        glob_query_grad.reshape(head_count, globals_count, BLK, head_width),
    )
    grad_query = token_major((gradient_row_values + glob_query_add).astype(jnp.bfloat16))
    grad_key = token_major(own_terms[..., :head_width].astype(jnp.bfloat16))
    grad_value = token_major(own_terms[..., head_width:].astype(jnp.bfloat16))
    return (attn_out, grad_query, grad_key, grad_value)


MASKED = -1e30
ALIGNED = pl.DeviceIdType.MESH


NEXT, ACROSS, SKIP = 0, 1, 2
OUTER_IN = ((0, 2, ACROSS), (0, 2, SKIP), (0, 2, NEXT), (2, 2, ACROSS), (2, 2, SKIP), (2, 2, NEXT))
INNER_IN = ((0, 2, SKIP), (0, 2, NEXT), (2, 2, SKIP), (2, 2, NEXT))
TURNS = ((ACROSS, ACROSS), None, (NEXT, SKIP), (SKIP, NEXT))
OUTER_OUT = (((0, 2, ACROSS),), (), ((0, 2, NEXT),), ((2, 2, ACROSS), (2, 2, NEXT), (0, 4, SKIP)))
INNER_OUT = ((), (), ((0, 2, SKIP),), ((2, 2, SKIP), (0, 4, ACROSS), (0, 4, NEXT)))


def rows_dot(left, right):
    return lax.dot_general(left, right, (((1,), (1,)), ((), ())), preferred_element_type=jnp.float32)


def one_head_kernel(
    shards,
    blocks,
    width_in,
    global_in,
    random_in,
    k_in,
    v_in,
    q_in,
    g_in,
    out,
    width_ref,
    global_ref,
    random_ref,
    stage,
    in_all,
    bias_own,
    bias_all,
    out_all,
    dk_sum,
    dv_sum,
    stage_sem,
    pair_recv,
    rest_recv,
    in_send,
    bias_send,
    bias_recv,
    out_send,
    out_recv,
):
    me = lax.axis_index("seq")
    rows = blocks * BLK
    key_blocks = shards * blocks
    hd = in_all.shape[2]
    logit_scale = 1.0 / math.sqrt(hd)
    inner = ((me + 1) // 2) % 2
    partner = (me + 1 - 2 * (me % 2), 3 - me, (me + 2) % 4)
    arrays = (k_in, v_in, q_in, g_in)

    def pick(pair, table):
        first, second = table[pair[0]], table[pair[1]]
        return first + (second - first) * inner

    def cols(index):
        return pl.ds(pl.multiple_of(index * hd, hd), hd)

    def span(index):
        return pl.ds(pl.multiple_of(index * rows, rows), rows)

    def send_in(first, count, step, target):
        if count == 1:
            source, landing = arrays[first].at[:, cols(target)], in_all.at[first, span(me), :]
        else:
            source = stage.at[pl.ds(first, count), :, cols(target)]
            landing = in_all.at[pl.ds(first, count), span(me), :]
        return pltpu.make_async_remote_copy(
            src_ref=source,
            dst_ref=landing,
            send_sem=in_send,
            recv_sem=pair_recv if first < 2 else rest_recv.at[step],
            device_id={"seq": target},
            device_id_type=ALIGNED,
        )

    def send_bias(target):
        return pltpu.make_async_remote_copy(
            src_ref=bias_own.at[target],
            dst_ref=bias_all.at[me],
            send_sem=bias_send,
            recv_sem=bias_recv,
            device_id={"seq": target},
            device_id_type=ALIGNED,
        )

    def send_out(first, count, step):
        return pltpu.make_async_remote_copy(
            src_ref=out_all.at[pl.ds(first, count), span(partner[step]), :],
            dst_ref=out.at[pl.ds(first, count), :, cols(me)],
            send_sem=out_send,
            recv_sem=out_recv,
            device_id={"seq": partner[step]},
            device_id_type=ALIGNED,
        )

    def start_outs(turn):
        for role, table in enumerate((OUTER_OUT, INNER_OUT)):

            @pl.when(inner == role)
            def _():
                for first, count, step in table[turn]:
                    send_out(first, count, step).start()

    def wait_for(bytes_of, semaphore):
        pltpu.make_async_copy(bytes_of, bytes_of, semaphore).wait()

    small = [
        pltpu.make_async_copy(source, landing, semaphore)
        for source, landing, semaphore in (
            (width_in, width_ref, bias_send),
            (global_in, global_ref, out_send),
            (random_in, random_ref, out_recv),
        )
    ]
    staged = [
        pltpu.make_async_copy(array, stage.at[slot], stage_sem)
        for slot, array in enumerate(arrays)
    ]
    local_out = [
        pltpu.make_async_copy(
            out_all.at[pl.ds(2 * half, 2), span(me), :],
            out.at[pl.ds(2 * half, 2), :, cols(me)],
            out_recv,
        )
        for half in range(2)
    ]

    barrier = pltpu.get_barrier_semaphore()

    def greet(device):
        pl.semaphore_signal(barrier, inc=1, device_id={"seq": device}, device_id_type=ALIGNED)

    greet(3 - me)

    @pl.when(me != 2)
    def _():
        for copy in staged:
            copy.start()

    @pl.when(inner == 1)
    def _():
        pl.semaphore_wait(barrier, 1)

        @pl.when(me == 1)
        def _():
            wait_for(stage, stage_sem)
            send_in(0, 2, ACROSS, partner[ACROSS]).start()

        @pl.when(me == 2)
        def _():
            for slot in range(4):
                send_in(slot, 1, ACROSS, partner[ACROSS]).start()

        greet(0)
        greet(3)

    for copy in small:
        copy.start()

    @pl.when(me == 1)
    def _():
        send_in(2, 2, ACROSS, partner[ACROSS]).start()

    for copy in small:
        copy.wait()

    lane = lax.broadcasted_iota(jnp.int32, (1, BLK), 1)
    spot_ids = jnp.zeros_like(lane)
    for spot in range(1, blocks):
        spot_ids += jnp.where(lane >= spot * key_blocks, 1, 0)
    key_ids = lane - spot_ids * key_blocks
    block_ids = me * blocks + spot_ids
    distance = jnp.abs(key_ids - block_ids)
    listed = jnp.zeros(lane.shape, jnp.float32)
    row_global = jnp.zeros(lane.shape, jnp.float32)
    for index in range(global_ref.shape[0]):
        listed += jnp.where(key_ids == global_ref[index], 1.0, 0.0)
        row_global = jnp.maximum(row_global, jnp.where(block_ids == global_ref[index], 1.0, 0.0))
    for head in range(shards):
        hits = listed + jnp.where(distance <= jnp.minimum(width_ref[head], WMAX), 1.0, 0.0)
        for index in range(random_ref.shape[0]):
            named = jnp.zeros_like(lane)
            for spot in range(blocks):
                named = jnp.where(spot_ids == spot, random_ref[index, spot, head], named)
            hits += jnp.where(key_ids == named, 1.0, 0.0)
        hits = row_global + (1.0 - row_global) * hits
        bias_own[head] = jnp.where(
            hits > 0.5, jnp.log(jnp.maximum(hits, 1.0)) * (1.0 / math.log(2.0)), MASKED
        )

    @pl.when(me == 2)
    def _():
        for copy in staged:
            copy.start()

    @pl.when(me != 1)
    def _():
        wait_for(stage, stage_sem)

    @pl.when(inner == 0)
    def _():
        pl.semaphore_wait(barrier, 3)
        greet(1)
        greet(2)
        for step, target in enumerate(partner):
            send_bias(target).start()
        for first, count, step in OUTER_IN:
            send_in(first, count, step, partner[step]).start()

    @pl.when(inner == 1)
    def _():
        pl.semaphore_wait(barrier, 2)
        for step, target in enumerate(partner):
            send_bias(target).start()
        for first, count, step in INNER_IN:
            send_in(first, count, step, partner[step]).start()

    bias_all[me] = bias_own[me]

    sub_ids = lax.broadcasted_iota(jnp.int32, (key_blocks, BLK), 0)
    lane_ids = lax.broadcasted_iota(jnp.int32, (key_blocks, BLK), 1)

    for slot in range(4):
        in_all[slot, span(me), :] = stage[slot, :, cols(me)]
    others = pl.ds(0, (shards - 1) * rows)
    wait_for(in_all.at[pl.ds(0, 2), others, :], pair_recv)
    wait_for(bias_all.at[pl.ds(0, shards - 1)], bias_recv)
    keys = in_all[0]
    vals = in_all[1]
    keys_t = keys.T
    vals_t = vals.T
    for turn, pair in enumerate(TURNS):
        if pair is None:
            chunk = me
        else:
            chunk, step = pick(pair, partner), pick(pair, (NEXT, ACROSS, SKIP))
            wait_for(in_all.at[pl.ds(2, 2), span(chunk), :], rest_recv.at[step])
        q = in_all[2, span(chunk), :]
        g = in_all[3, span(chunk), :]
        row = jnp.broadcast_to(bias_all[chunk], lane_ids.shape)
        spread = [
            jnp.broadcast_to(
                jnp.sum(
                    jnp.where(lane_ids == sub_ids + spot * key_blocks, row, 0.0),
                    axis=1,
                    keepdims=True,
                ),
                lane_ids.shape,
            )
            for spot in range(blocks)
        ]
        bias = jnp.concatenate(
            [
                jnp.concatenate(
                    [
                        jnp.broadcast_to(spread[spot][key : key + 1, :], (BLK, BLK))
                        for spot in range(blocks)
                    ],
                    axis=1,
                )
                for key in range(key_blocks)
            ],
            axis=0,
        )
        scores = rows_dot(keys, q) * (logit_scale / math.log(2.0)) + bias
        top = jnp.max(scores, axis=0, keepdims=True)
        weights = jnp.exp2(scores - top)
        inverse = 1.0 / jnp.sum(weights, axis=0, keepdims=True)
        out_t = (
            jnp.dot(vals_t, weights.astype(jnp.bfloat16), preferred_element_type=jnp.float32)
            * inverse
        )
        out_rows = out_t.T.astype(jnp.bfloat16)
        out_all[0, span(chunk), :] = out_rows
        delta = jnp.sum(
            (g.astype(jnp.float32) * out_rows.astype(jnp.float32)).T, axis=0, keepdims=True
        )
        probs = weights * inverse
        grads = (probs * (rows_dot(vals, g) - delta)).astype(jnp.bfloat16)
        dq_t = jnp.dot(keys_t, grads, preferred_element_type=jnp.float32) * logit_scale
        out_all[1, span(chunk), :] = dq_t.T.astype(jnp.bfloat16)
        if pair is None:
            local_out[0].start()
        if turn < shards - 1:
            start_outs(turn)
        dv_part = jnp.dot(probs.astype(jnp.bfloat16), g, preferred_element_type=jnp.float32)
        dk_part = jnp.dot(grads, q, preferred_element_type=jnp.float32)
        if turn == 0:
            dv_sum[...] = dv_part
            dk_sum[...] = dk_part
        elif turn < shards - 1:
            dv_sum[...] += dv_part
            dk_sum[...] += dk_part
        else:
            out_all[3] = (dv_sum[...] + dv_part).astype(jnp.bfloat16)
            out_all[2] = ((dk_sum[...] + dk_part) * logit_scale).astype(jnp.bfloat16)
    start_outs(shards - 1)
    local_out[1].start()
    wait_for(bias_own.at[pl.ds(0, shards - 1)], bias_send)
    wait_for(in_all.at[:, others, :], in_send)
    wait_for(out_all.at[:, others, :], out_send)
    wait_for(out, out_recv)


def deliver_kernel(landed, *refs):
    for slot in range(4):
        pltpu.make_async_copy(landed.at[slot], refs[slot], refs[4]).start()
    pltpu.make_async_copy(landed, landed, refs[4]).wait()


def one_head(queries, key_rows, values, grad_out, window_width, global_blocks, random_blocks):
    shards = lax.axis_size("seq")
    tokens, columns = queries.shape
    hd = columns // shards
    blocks = tokens // BLK
    whole = shards * tokens
    bf16 = jnp.bfloat16
    anywhere = pl.BlockSpec(memory_space=pl.ANY)
    dma = pltpu.SemaphoreType.DMA
    lists = (window_width, global_blocks, random_blocks.transpose(2, 1, 0))
    landed = pl.pallas_call(
        functools.partial(one_head_kernel, shards, blocks),
        out_shape=jax.ShapeDtypeStruct((4, tokens, columns), bf16),
        in_specs=[anywhere] * 7,
        out_specs=anywhere,
        scratch_shapes=[pltpu.SMEM(array.shape, jnp.int32) for array in lists]
        + [pltpu.VMEM((4, tokens, columns), bf16), pltpu.VMEM((4, whole, hd), bf16)]
        + [pltpu.VMEM((shards, 1, BLK), jnp.float32)] * 2
        + [pltpu.VMEM((4, whole, hd), bf16)]
        + [pltpu.VMEM((whole, hd), jnp.float32)] * 2
        + [dma(()), dma(()), dma((shards - 1,))]
        + [dma(())] * 5,
        compiler_params=pltpu.CompilerParams(
            collective_id=0, has_side_effects=True, vmem_limit_bytes=48 * 1024 * 1024
        ),
    )(
        *(
            pltpu.with_memory_space_constraint(array, pltpu.HBM)
            for array in (*lists, key_rows, values, queries, grad_out)
        )
    )
    return pl.pallas_call(
        deliver_kernel,
        out_shape=(jax.ShapeDtypeStruct((tokens, columns), bf16),) * 4,
        in_specs=[anywhere],
        out_specs=(anywhere,) * 4,
        scratch_shapes=[dma(())],
        compiler_params=pltpu.CompilerParams(vmem_limit_bytes=8 * 1024 * 1024),
    )(landed)


def dispatch(queries, key_rows, values, grad_out, window_width, global_blocks, random_blocks):
    shards = lax.axis_size("seq")
    if shards == 4 and window_width.shape[0] == shards and queries.shape[1] == shards * BLK:
        chosen = one_head
    else:
        chosen = on_device
    return chosen(
        queries, key_rows, values, grad_out, window_width, global_blocks, random_blocks
    )


def solution(mesh):
    in_specs = (
        P(("groups", "seq"), ("head", "sub")),
        P(("groups", "seq"), ("head", "sub")),
        P(("groups", "seq"), ("head", "sub")),
        P(("groups", "seq"), ("head", "sub")),
        P(("groups", "head", "sub")),
        P("groups"),
        P(("groups", "head", "sub"), "seq", None),
    )
    out_specs = (
        P(("groups", "seq"), ("head", "sub")),
        P(("groups", "seq"), ("head", "sub")),
        P(("groups", "seq"), ("head", "sub")),
        P(("groups", "seq"), ("head", "sub")),
    )
    return jax.shard_map(
        dispatch, mesh=mesh, in_specs=in_specs, out_specs=out_specs, check_vma=False
    )
```

```python
import functools
import math

import jax
import jax.numpy as jnp
from jax import lax
from jax.experimental import pallas as pl
from jax.experimental.pallas import tpu as pltpu
from jax.sharding import PartitionSpec as P

BLK = 128
WMAX = 1


def extended(cells, sides, width):
    for axis, dim in sides:
        count = lax.axis_size(axis)
        ends = count - 1
        head = lax.slice_in_dim(cells, 0, width, axis=dim)
        tail = lax.slice_in_dim(cells, cells.shape[dim] - width, cells.shape[dim], axis=dim)
        cells = jnp.concatenate(
            [
                lax.ppermute(tail, axis, [(i, (i + 1) % count) for i in range(ends)]),
                cells,
                lax.ppermute(head, axis, [((i + 1) % count, i) for i in range(ends)]),
            ],
            axis=dim,
        )
    return cells


def from_behind(block, axis, distance):
    devices = range(lax.axis_size(axis))
    route = [(i - distance, i) for i in devices if i - distance in devices]
    return lax.ppermute(block, axis, route)


def head_major(tensor, head_count, head_width):
    block_count = tensor.shape[0] // BLK
    return tensor.reshape(block_count, BLK, head_count, head_width).transpose(2, 0, 1, 3)


def token_major(tensor):
    head_count, block_count, row_count, head_width = tensor.shape
    return tensor.transpose(1, 2, 0, 3).reshape(block_count * row_count, head_count * head_width)


def on_device(queries, key_rows, values, grad_out, window_width, global_blocks, random_blocks):
    head_count = window_width.shape[0]
    tokens = queries.shape[0]
    head_width = queries.shape[1] // head_count
    blocks = tokens // BLK
    span = 2 * WMAX + 1
    globals_count = global_blocks.shape[0]
    randoms = random_blocks.shape[2]
    shards = lax.axis_size("seq")
    my_index = lax.axis_index("seq")
    logit_scale = 1.0 / math.sqrt(head_width)
    group = 2
    group_count = blocks // group
    pair_width = 2 * head_width
    query_heads = head_major(queries, head_count, head_width)
    grad_heads = head_major(grad_out, head_count, head_width)
    packed = jnp.concatenate([key_rows, values], axis=1)
    padded = extended(packed, (("seq", 0),), WMAX * BLK)
    pair_heads = (
        padded.reshape(blocks + 2 * WMAX, BLK, 2, head_count, head_width)
        .transpose(3, 0, 1, 2, 4)
        .reshape(head_count, blocks + 2 * WMAX, BLK, pair_width)
    )
    local_pairs = pair_heads[:, WMAX : WMAX + blocks]
    owners = global_blocks // blocks
    local_spot = global_blocks % blocks
    stacked = jnp.concatenate([queries, key_rows, values, grad_out], axis=1)
    own_rows = jnp.stack(
        [
            lax.dynamic_slice_in_dim(stacked, local_spot[glob_index] * BLK, BLK, 0)
            for glob_index in range(globals_count)
        ]
    )
    owned_mask = (owners == my_index)[:, None, None]
    masked_rows = jnp.where(owned_mask, own_rows, jnp.zeros((), jnp.bfloat16))
    panels = lax.psum(masked_rows, "seq").astype(jnp.float32).astype(jnp.bfloat16)
    panel_heads = panels.reshape(globals_count, BLK, 4, head_count, head_width).transpose(
        2, 3, 0, 1, 4
    )
    glob_query = panel_heads[0]
    glob_grad = panel_heads[3]
    glob_pairs = jnp.concatenate([panel_heads[1], panel_heads[2]], axis=-1)
    requests = random_blocks.reshape(-1)
    request_count = requests.shape[0]
    capacity = max(2, -(-request_count // shards))
    targets = requests // blocks
    request_head = jnp.arange(request_count, dtype=jnp.int32) // (blocks * randoms)
    codes = request_head * blocks + requests % blocks
    positions = jnp.arange(request_count, dtype=jnp.int32)
    earlier = (targets[:, None] == targets[None, :]) & (positions[None, :] < positions[:, None])
    ranks = jnp.sum(earlier.astype(jnp.int32), axis=1)
    slots = targets * capacity + ranks
    outgoing = jnp.full((shards * capacity,), -1, jnp.int32).at[slots].set(codes)
    incoming = lax.all_to_all(
        outgoing.reshape(shards, capacity), "seq", split_axis=0, concat_axis=0, tiled=True
    ).reshape(-1)
    code_hits = (
        incoming[:, None] == jnp.arange(head_count * blocks, dtype=jnp.int32)[None, :]
    ).astype(jnp.bfloat16)
    flat_pairs = local_pairs.reshape(head_count * blocks, BLK, pair_width)
    reply = jnp.einsum(
        "sc,cid->sid", code_hits, flat_pairs, preferred_element_type=jnp.float32
    ).astype(jnp.bfloat16)
    fetched = lax.all_to_all(
        reply.reshape(shards, capacity, BLK, pair_width),
        "seq",
        split_axis=0,
        concat_axis=0,
        tiled=True,
    )
    slot_hits = (
        slots[:, None] == jnp.arange(shards * capacity, dtype=jnp.int32)[None, :]
    ).astype(jnp.bfloat16)
    random_pairs = (
        jnp.einsum(
            "rs,sid->rid",
            slot_hits,
            fetched.reshape(shards * capacity, BLK, pair_width),
            preferred_element_type=jnp.float32,
        )
        .astype(jnp.bfloat16)
        .reshape(head_count, blocks, randoms, BLK, pair_width)
    )
    offsets = jnp.arange(span, dtype=jnp.int32) - WMAX
    block_ids = my_index * blocks + jnp.arange(blocks, dtype=jnp.int32)
    reach = block_ids[:, None] + offsets[None, :]
    in_range = (reach >= 0) & (reach < shards * blocks)
    window_ok = in_range[None, :, :] & (
        jnp.abs(offsets)[None, None, :] <= window_width[:, None, None]
    )
    list_ok = jnp.concatenate(
        [window_ok, jnp.ones((head_count, blocks, globals_count + randoms), jnp.bool_)], axis=2
    )
    global_hit = block_ids[:, None] == global_blocks[None, :]
    row_global = jnp.any(global_hit, axis=1)
    hit_weight = global_hit.astype(jnp.float32)

    def key_sequence(first_block):
        pieces_list = [
            jnp.stack(
                [
                    lax.dynamic_slice_in_dim(pair_heads, first_block + offset, group, 1)
                    for offset in range(span)
                ],
                axis=2,
            )
        ]
        pieces_list.append(
            jnp.broadcast_to(
                glob_pairs[:, None], (head_count, group, globals_count, BLK, pair_width)
            )
        )
        pieces_list.append(random_pairs)
        joined = jnp.concatenate(pieces_list, axis=2)
        entry_count = joined.shape[2]
        list_mask = list_ok[:, :, :entry_count]
        return (
            joined.reshape(head_count, group, entry_count * BLK, pair_width),
            jnp.repeat(list_mask, BLK, axis=2),
        )

    def forward_group(group_index):
        first_block = group_index * group
        pairs, list_mask = key_sequence(first_block)
        key_part = pairs[..., :head_width]
        value_part = pairs[..., head_width:]
        score_matrix = (
            jnp.einsum("hqid,hqkd->hqik", query_heads, key_part, preferred_element_type=jnp.float32)
            * logit_scale
        )
        score_matrix = jnp.where(list_mask[:, :, None, :], score_matrix, -jnp.inf)
        row_max = jnp.max(score_matrix, axis=-1)
        weights = jnp.exp(score_matrix - row_max[..., None])
        totals = jnp.sum(weights, axis=-1)
        accumulated_total = jnp.einsum(
            "hqik,hqkd->hqid",
            weights.astype(jnp.bfloat16),
            value_part,
            preferred_element_type=jnp.float32,
        )
        return (
            (accumulated_total / totals[..., None]).astype(jnp.bfloat16),
            row_max + jnp.log(totals),
        )

    sparse_out, sparse_lse = lax.map(forward_group, jnp.arange(group_count))
    sparse_out = jnp.moveaxis(sparse_out, 0, 1).reshape(head_count, blocks, BLK, head_width)
    sparse_lse = jnp.moveaxis(sparse_lse, 0, 1).reshape(head_count, blocks, BLK)
    local_keys = local_pairs[..., :head_width].reshape(head_count, blocks * BLK, head_width)
    local_values = local_pairs[..., head_width:].reshape(head_count, blocks * BLK, head_width)
    glob_rows = glob_query.reshape(head_count, globals_count * BLK, head_width)
    glob_grad_rows = glob_grad.reshape(head_count, globals_count * BLK, head_width)
    glob_scores = (
        jnp.einsum("hid,hjd->hij", glob_rows, local_keys, preferred_element_type=jnp.float32)
        * logit_scale
    )
    glob_max = lax.pmax(jnp.max(glob_scores, axis=-1), "seq")
    glob_weights = jnp.exp(glob_scores - glob_max[..., None])
    glob_part_sum = jnp.einsum(
        "hij,hjd->hid",
        glob_weights.astype(jnp.bfloat16),
        local_values,
        preferred_element_type=jnp.float32,
    )
    glob_sum, glob_total = lax.psum((glob_part_sum, jnp.sum(glob_weights, axis=-1)), "seq")
    glob_out = (glob_sum / glob_total[..., None]).astype(jnp.bfloat16)
    glob_lse = glob_max + jnp.log(glob_total)
    chosen_out = jnp.einsum(
        "bg,hgid->hbid",
        hit_weight,
        glob_out.reshape(head_count, globals_count, BLK, head_width).astype(jnp.float32),
    )
    out_heads = jnp.where(
        row_global[None, :, None, None], chosen_out.astype(jnp.bfloat16), sparse_out
    )
    attn_out = token_major(out_heads)
    delta = jnp.sum(grad_heads.astype(jnp.float32) * out_heads.astype(jnp.float32), axis=-1)
    row_lse = jnp.where(row_global[None, :, None], jnp.inf, sparse_lse)
    glob_delta = jnp.sum(glob_grad_rows.astype(jnp.float32) * glob_out.astype(jnp.float32), axis=-1)

    def backward_group(group_index):
        first_block = group_index * group
        pairs, list_mask = key_sequence(first_block)
        key_part = pairs[..., :head_width]
        value_part = pairs[..., head_width:]
        score_matrix = (
            jnp.einsum("hqid,hqkd->hqik", query_heads, key_part, preferred_element_type=jnp.float32)
            * logit_scale
        )
        probs = jnp.where(list_mask[:, :, None, :], jnp.exp(score_matrix - row_lse[..., None]), 0.0)
        probability_gradient = jnp.einsum(
            "hqid,hqkd->hqik", grad_heads, value_part, preferred_element_type=jnp.float32
        )
        score_gradient = (probs * (probability_gradient - delta[..., None])).astype(jnp.bfloat16)
        grad_rows_part = (
            jnp.einsum(
                "hqik,hqkd->hqid", score_gradient, key_part, preferred_element_type=jnp.float32
            )
            * logit_scale
        )
        key_contributions = (
            jnp.einsum(
                "hqik,hqid->hqkd", score_gradient, query_heads, preferred_element_type=jnp.float32
            )
            * logit_scale
        )
        value_contributions = jnp.einsum(
            "hqik,hqid->hqkd",
            probs.astype(jnp.bfloat16),
            grad_heads,
            preferred_element_type=jnp.float32,
        )
        terms = jnp.concatenate([key_contributions, value_contributions], axis=-1).reshape(
            head_count, group, -1, BLK, pair_width
        )
        window_terms = terms[:, :, :span]
        glob_terms = jnp.sum(terms[:, :, span : span + globals_count], axis=1)
        random_terms = terms[:, :, span + globals_count :].astype(jnp.bfloat16)
        return (grad_rows_part, window_terms, glob_terms, random_terms)

    gradient_row_values, window_terms, glob_terms, random_terms = lax.map(
        backward_group, jnp.arange(group_count)
    )
    gradient_row_values = jnp.moveaxis(gradient_row_values, 0, 1).reshape(
        head_count, blocks, BLK, head_width
    )
    window_terms = jnp.moveaxis(window_terms, 0, 1).reshape(
        head_count, blocks, span, BLK, pair_width
    )
    glob_terms = jnp.sum(glob_terms, axis=0)
    spread = jnp.zeros((head_count, blocks + 2 * WMAX, BLK, pair_width), jnp.float32)
    for offset in range(span):
        spread = spread.at[:, offset : offset + blocks].add(window_terms[:, :, offset])
    glob_probs = jnp.exp(glob_scores - glob_lse[..., None])
    glob_grad_probs = jnp.einsum(
        "hid,hjd->hij", glob_grad_rows, local_values, preferred_element_type=jnp.float32
    )
    glob_grad_scores = (glob_probs * (glob_grad_probs - glob_delta[..., None])).astype(jnp.bfloat16)
    glob_query_part = (
        jnp.einsum("hij,hjd->hid", glob_grad_scores, local_keys, preferred_element_type=jnp.float32)
        * logit_scale
    )
    key_from_glob = (
        jnp.einsum("hij,hid->hjd", glob_grad_scores, glob_rows, preferred_element_type=jnp.float32)
        * logit_scale
    )
    value_from_glob = jnp.einsum(
        "hij,hid->hjd",
        glob_probs.astype(jnp.bfloat16),
        glob_grad_rows,
        preferred_element_type=jnp.float32,
    )
    glob_total_terms, glob_query_grad = lax.psum((glob_terms, glob_query_part), "seq")
    from_below = from_behind(spread[:, blocks + WMAX :], "seq", 1)
    from_above = from_behind(spread[:, :WMAX].astype(jnp.bfloat16), "seq", -1).astype(jnp.float32)
    own_terms = spread[:, WMAX : WMAX + blocks]
    own_terms = own_terms.at[:, :WMAX].add(from_below).at[:, blocks - WMAX :].add(from_above)
    own_terms = own_terms + jnp.concatenate([key_from_glob, value_from_glob], axis=-1).reshape(
        head_count, blocks, BLK, pair_width
    )
    own_terms = own_terms + jnp.einsum("bg,hgid->hbid", hit_weight, glob_total_terms)
    random_terms = jnp.moveaxis(random_terms, 0, 1).reshape(request_count, BLK, pair_width)
    outgoing_terms = (
        jnp.zeros((shards * capacity, BLK, pair_width), jnp.bfloat16).at[slots].set(random_terms)
    )
    returned = lax.all_to_all(
        outgoing_terms.reshape(shards, capacity, BLK, pair_width),
        "seq",
        split_axis=0,
        concat_axis=0,
        tiled=True,
    ).reshape(shards * capacity, BLK, pair_width)
    random_add = jnp.einsum(
        "sc,sid->cid", code_hits, returned, preferred_element_type=jnp.float32
    ).reshape(head_count, blocks, BLK, pair_width)
    own_terms = own_terms + random_add
    glob_query_add = jnp.einsum(
        "bg,hgid->hbid",
        hit_weight,
        glob_query_grad.reshape(head_count, globals_count, BLK, head_width),
    )
    grad_query = token_major((gradient_row_values + glob_query_add).astype(jnp.bfloat16))
    grad_key = token_major(own_terms[..., :head_width].astype(jnp.bfloat16))
    grad_value = token_major(own_terms[..., head_width:].astype(jnp.bfloat16))
    return (attn_out, grad_query, grad_key, grad_value)


MASKED = -1e30
ALIGNED = pl.DeviceIdType.MESH


NEXT, ACROSS, SKIP = 0, 1, 2
OUTER_IN = ((0, 2, ACROSS), (0, 2, SKIP), (0, 2, NEXT), (2, 2, ACROSS), (2, 2, SKIP), (2, 2, NEXT))
INNER_IN = ((0, 2, SKIP), (0, 2, NEXT), (2, 2, SKIP), (2, 2, NEXT))
TURNS = ((ACROSS, ACROSS), None, (NEXT, SKIP), (SKIP, NEXT))
OUTER_OUT = (((0, 2, ACROSS),), (), ((0, 2, NEXT),), ((2, 2, ACROSS), (2, 2, NEXT), (0, 4, SKIP)))
INNER_OUT = ((), (), ((0, 2, SKIP),), ((2, 2, SKIP), (0, 4, ACROSS), (0, 4, NEXT)))


def rows_dot(left, right):
    return lax.dot_general(left, right, (((1,), (1,)), ((), ())), preferred_element_type=jnp.float32)


def one_head_kernel(
    shards,
    blocks,
    width_in,
    global_in,
    random_in,
    k_in,
    v_in,
    q_in,
    g_in,
    out,
    width_ref,
    global_ref,
    random_ref,
    stage,
    in_all,
    bias_own,
    bias_all,
    out_all,
    dk_sum,
    dv_sum,
    stage_sem,
    pair_recv,
    rest_recv,
    in_send,
    bias_send,
    bias_recv,
    out_send,
    out_recv,
):
    me = lax.axis_index("seq")
    rows = blocks * BLK
    key_blocks = shards * blocks
    hd = in_all.shape[2]
    logit_scale = 1.0 / math.sqrt(hd)
    inner = ((me + 1) // 2) % 2
    partner = (me + 1 - 2 * (me % 2), 3 - me, (me + 2) % 4)
    arrays = (k_in, v_in, q_in, g_in)

    def pick(pair, table):
        first, second = table[pair[0]], table[pair[1]]
        return first + (second - first) * inner

    def cols(index):
        return pl.ds(pl.multiple_of(index * hd, hd), hd)

    def span(index):
        return pl.ds(pl.multiple_of(index * rows, rows), rows)

    def send_in(first, count, step, target):
        if count == 1:
            source, landing = arrays[first].at[:, cols(target)], in_all.at[first, span(me), :]
        else:
            source = stage.at[pl.ds(first, count), :, cols(target)]
            landing = in_all.at[pl.ds(first, count), span(me), :]
        return pltpu.make_async_remote_copy(
            src_ref=source,
            dst_ref=landing,
            send_sem=in_send,
            recv_sem=pair_recv if first < 2 else rest_recv.at[step],
            device_id={"seq": target},
            device_id_type=ALIGNED,
        )

    def send_bias(target):
        return pltpu.make_async_remote_copy(
            src_ref=bias_own.at[target],
            dst_ref=bias_all.at[me],
            send_sem=bias_send,
            recv_sem=bias_recv,
            device_id={"seq": target},
            device_id_type=ALIGNED,
        )

    def send_out(first, count, step):
        return pltpu.make_async_remote_copy(
            src_ref=out_all.at[pl.ds(first, count), span(partner[step]), :],
            dst_ref=out.at[pl.ds(first, count), :, cols(me)],
            send_sem=out_send,
            recv_sem=out_recv,
            device_id={"seq": partner[step]},
            device_id_type=ALIGNED,
        )

    def start_outs(turn):
        for role, table in enumerate((OUTER_OUT, INNER_OUT)):

            @pl.when(inner == role)
            def _():
                for first, count, step in table[turn]:
                    send_out(first, count, step).start()

    def wait_for(bytes_of, semaphore):
        pltpu.make_async_copy(bytes_of, bytes_of, semaphore).wait()

    small = [
        pltpu.make_async_copy(source, landing, semaphore)
        for source, landing, semaphore in (
            (width_in, width_ref, bias_send),
            (global_in, global_ref, out_send),
            (random_in, random_ref, out_recv),
        )
    ]
    staged = [
        pltpu.make_async_copy(array, stage.at[slot], stage_sem.at[slot // 2])
        for slot, array in enumerate(arrays)
    ]
    local_out = [
        pltpu.make_async_copy(
            out_all.at[pl.ds(2 * half, 2), span(me), :],
            out.at[pl.ds(2 * half, 2), :, cols(me)],
            out_recv,
        )
        for half in range(2)
    ]

    barrier = pltpu.get_barrier_semaphore()

    def greet(device):
        pl.semaphore_signal(barrier, inc=1, device_id={"seq": device}, device_id_type=ALIGNED)

    greet(3 - me)

    @pl.when(me != 2)
    def _():
        for copy in staged:
            copy.start()

    @pl.when(inner == 1)
    def _():
        pl.semaphore_wait(barrier, 1)

        @pl.when(me == 1)
        def _():
            wait_for(stage.at[pl.ds(0, 2)], stage_sem.at[0])
            send_in(0, 2, ACROSS, partner[ACROSS]).start()

        @pl.when(me == 2)
        def _():
            for slot in range(2):
                send_in(slot, 1, ACROSS, partner[ACROSS]).start()
            for copy in staged:
                copy.start()

        greet(0)
        greet(3)

    for copy in small:
        copy.start()

    @pl.when(me != 1)
    def _():
        wait_for(stage.at[pl.ds(0, 2)], stage_sem.at[0])

    wait_for(stage.at[pl.ds(2, 2)], stage_sem.at[1])

    @pl.when(inner == 1)
    def _():
        send_in(2, 2, ACROSS, partner[ACROSS]).start()

    for copy in small:
        copy.wait()

    lane = lax.broadcasted_iota(jnp.int32, (1, BLK), 1)
    spot_ids = jnp.zeros_like(lane)
    for spot in range(1, blocks):
        spot_ids += jnp.where(lane >= spot * key_blocks, 1, 0)
    key_ids = lane - spot_ids * key_blocks
    block_ids = me * blocks + spot_ids
    distance = jnp.abs(key_ids - block_ids)
    listed = jnp.zeros(lane.shape, jnp.float32)
    row_global = jnp.zeros(lane.shape, jnp.float32)
    for index in range(global_ref.shape[0]):
        listed += jnp.where(key_ids == global_ref[index], 1.0, 0.0)
        row_global = jnp.maximum(row_global, jnp.where(block_ids == global_ref[index], 1.0, 0.0))
    for head in range(shards):
        hits = listed + jnp.where(distance <= jnp.minimum(width_ref[head], WMAX), 1.0, 0.0)
        for index in range(random_ref.shape[0]):
            named = jnp.zeros_like(lane)
            for spot in range(blocks):
                named = jnp.where(spot_ids == spot, random_ref[index, spot, head], named)
            hits += jnp.where(key_ids == named, 1.0, 0.0)
        hits = row_global + (1.0 - row_global) * hits
        bias_own[head] = jnp.where(
            hits > 0.5, jnp.log(jnp.maximum(hits, 1.0)) * (1.0 / math.log(2.0)), MASKED
        )

    @pl.when(inner == 0)
    def _():
        pl.semaphore_wait(barrier, 3)
        greet(1)
        greet(2)
        for step, target in enumerate(partner):
            send_bias(target).start()
        for first, count, step in OUTER_IN:
            send_in(first, count, step, partner[step]).start()

    @pl.when(inner == 1)
    def _():
        pl.semaphore_wait(barrier, 2)
        for step, target in enumerate(partner):
            send_bias(target).start()
        for first, count, step in INNER_IN:
            send_in(first, count, step, partner[step]).start()

    bias_all[me] = bias_own[me]

    sub_ids = lax.broadcasted_iota(jnp.int32, (key_blocks, BLK), 0)
    lane_ids = lax.broadcasted_iota(jnp.int32, (key_blocks, BLK), 1)

    for slot in range(4):
        in_all[slot, span(me), :] = stage[slot, :, cols(me)]
    others = pl.ds(0, (shards - 1) * rows)
    wait_for(in_all.at[pl.ds(0, 2), others, :], pair_recv)
    wait_for(bias_all.at[pl.ds(0, shards - 1)], bias_recv)
    keys = in_all[0]
    vals = in_all[1]
    keys_t = keys.T
    vals_t = vals.T
    for turn, pair in enumerate(TURNS):
        if pair is None:
            chunk = me
        else:
            chunk, step = pick(pair, partner), pick(pair, (NEXT, ACROSS, SKIP))
            wait_for(in_all.at[pl.ds(2, 2), span(chunk), :], rest_recv.at[step])
        q = in_all[2, span(chunk), :]
        g = in_all[3, span(chunk), :]
        row = jnp.broadcast_to(bias_all[chunk], lane_ids.shape)
        spread = [
            jnp.broadcast_to(
                jnp.sum(
                    jnp.where(lane_ids == sub_ids + spot * key_blocks, row, 0.0),
                    axis=1,
                    keepdims=True,
                ),
                lane_ids.shape,
            )
            for spot in range(blocks)
        ]
        bias = jnp.concatenate(
            [
                jnp.concatenate(
                    [
                        jnp.broadcast_to(spread[spot][key : key + 1, :], (BLK, BLK))
                        for spot in range(blocks)
                    ],
                    axis=1,
                )
                for key in range(key_blocks)
            ],
            axis=0,
        )
        scores = rows_dot(keys, q) * (logit_scale / math.log(2.0)) + bias
        top = jnp.max(scores, axis=0, keepdims=True)
        weights = jnp.exp2(scores - top)
        inverse = 1.0 / jnp.sum(weights, axis=0, keepdims=True)
        out_t = (
            jnp.dot(vals_t, weights.astype(jnp.bfloat16), preferred_element_type=jnp.float32)
            * inverse
        )
        out_rows = out_t.T.astype(jnp.bfloat16)
        out_all[0, span(chunk), :] = out_rows
        delta = jnp.sum(
            (g.astype(jnp.float32) * out_rows.astype(jnp.float32)).T, axis=0, keepdims=True
        )
        probs = weights * inverse
        grads = (probs * (rows_dot(vals, g) - delta)).astype(jnp.bfloat16)
        dq_t = jnp.dot(keys_t, grads, preferred_element_type=jnp.float32) * logit_scale
        out_all[1, span(chunk), :] = dq_t.T.astype(jnp.bfloat16)
        if pair is None:
            local_out[0].start()
        if turn < shards - 1:
            start_outs(turn)
        dv_part = jnp.dot(probs.astype(jnp.bfloat16), g, preferred_element_type=jnp.float32)
        dk_part = jnp.dot(grads, q, preferred_element_type=jnp.float32)
        if turn == 0:
            dv_sum[...] = dv_part
            dk_sum[...] = dk_part
        elif turn < shards - 1:
            dv_sum[...] += dv_part
            dk_sum[...] += dk_part
        else:
            out_all[3] = (dv_sum[...] + dv_part).astype(jnp.bfloat16)
            out_all[2] = ((dk_sum[...] + dk_part) * logit_scale).astype(jnp.bfloat16)
    start_outs(shards - 1)
    local_out[1].start()
    wait_for(bias_own.at[pl.ds(0, shards - 1)], bias_send)
    wait_for(in_all.at[:, others, :], in_send)
    wait_for(out_all.at[:, others, :], out_send)
    wait_for(out, out_recv)


def deliver_kernel(landed, *refs):
    for slot in range(4):
        pltpu.make_async_copy(landed.at[slot], refs[slot], refs[4]).start()
    pltpu.make_async_copy(landed, landed, refs[4]).wait()


def one_head(queries, key_rows, values, grad_out, window_width, global_blocks, random_blocks):
    shards = lax.axis_size("seq")
    tokens, columns = queries.shape
    hd = columns // shards
    blocks = tokens // BLK
    whole = shards * tokens
    bf16 = jnp.bfloat16
    anywhere = pl.BlockSpec(memory_space=pl.ANY)
    dma = pltpu.SemaphoreType.DMA
    lists = (window_width, global_blocks, random_blocks.transpose(2, 1, 0))
    landed = pl.pallas_call(
        functools.partial(one_head_kernel, shards, blocks),
        out_shape=jax.ShapeDtypeStruct((4, tokens, columns), bf16),
        in_specs=[anywhere] * 7,
        out_specs=anywhere,
        scratch_shapes=[pltpu.SMEM(array.shape, jnp.int32) for array in lists]
        + [pltpu.VMEM((4, tokens, columns), bf16), pltpu.VMEM((4, whole, hd), bf16)]
        + [pltpu.VMEM((shards, 1, BLK), jnp.float32)] * 2
        + [pltpu.VMEM((4, whole, hd), bf16)]
        + [pltpu.VMEM((whole, hd), jnp.float32)] * 2
        + [dma((2,)), dma(()), dma((shards - 1,))]
        + [dma(())] * 5,
        compiler_params=pltpu.CompilerParams(
            collective_id=0, has_side_effects=True, vmem_limit_bytes=48 * 1024 * 1024
        ),
    )(
        *(
            pltpu.with_memory_space_constraint(array, pltpu.HBM)
            for array in (*lists, key_rows, values, queries, grad_out)
        )
    )
    return pl.pallas_call(
        deliver_kernel,
        out_shape=(jax.ShapeDtypeStruct((tokens, columns), bf16),) * 4,
        in_specs=[anywhere],
        out_specs=(anywhere,) * 4,
        scratch_shapes=[dma(())],
        compiler_params=pltpu.CompilerParams(vmem_limit_bytes=8 * 1024 * 1024),
    )(landed)


def dispatch(queries, key_rows, values, grad_out, window_width, global_blocks, random_blocks):
    shards = lax.axis_size("seq")
    if shards == 4 and window_width.shape[0] == shards and queries.shape[1] == shards * BLK:
        chosen = one_head
    else:
        chosen = on_device
    return chosen(
        queries, key_rows, values, grad_out, window_width, global_blocks, random_blocks
    )


def solution(mesh):
    in_specs = (
        P(("groups", "seq"), ("head", "sub")),
        P(("groups", "seq"), ("head", "sub")),
        P(("groups", "seq"), ("head", "sub")),
        P(("groups", "seq"), ("head", "sub")),
        P(("groups", "head", "sub")),
        P("groups"),
        P(("groups", "head", "sub"), "seq", None),
    )
    out_specs = (
        P(("groups", "seq"), ("head", "sub")),
        P(("groups", "seq"), ("head", "sub")),
        P(("groups", "seq"), ("head", "sub")),
        P(("groups", "seq"), ("head", "sub")),
    )
    return jax.shard_map(
        dispatch, mesh=mesh, in_specs=in_specs, out_specs=out_specs, check_vma=False
    )
```

```python
import functools
import math

import jax
import jax.numpy as jnp
from jax import lax
from jax.experimental import pallas as pl
from jax.experimental.pallas import tpu as pltpu
from jax.sharding import PartitionSpec as P

BLK = 128
WMAX = 1


def extended(cells, sides, width):
    for axis, dim in sides:
        count = lax.axis_size(axis)
        ends = count - 1
        head = lax.slice_in_dim(cells, 0, width, axis=dim)
        tail = lax.slice_in_dim(cells, cells.shape[dim] - width, cells.shape[dim], axis=dim)
        cells = jnp.concatenate(
            [
                lax.ppermute(tail, axis, [(i, (i + 1) % count) for i in range(ends)]),
                cells,
                lax.ppermute(head, axis, [((i + 1) % count, i) for i in range(ends)]),
            ],
            axis=dim,
        )
    return cells


def from_behind(block, axis, distance):
    devices = range(lax.axis_size(axis))
    route = [(i - distance, i) for i in devices if i - distance in devices]
    return lax.ppermute(block, axis, route)


def head_major(tensor, head_count, head_width):
    block_count = tensor.shape[0] // BLK
    return tensor.reshape(block_count, BLK, head_count, head_width).transpose(2, 0, 1, 3)


def token_major(tensor):
    head_count, block_count, row_count, head_width = tensor.shape
    return tensor.transpose(1, 2, 0, 3).reshape(block_count * row_count, head_count * head_width)


def on_device(queries, key_rows, values, grad_out, window_width, global_blocks, random_blocks):
    head_count = window_width.shape[0]
    tokens = queries.shape[0]
    head_width = queries.shape[1] // head_count
    blocks = tokens // BLK
    span = 2 * WMAX + 1
    globals_count = global_blocks.shape[0]
    randoms = random_blocks.shape[2]
    shards = lax.axis_size("seq")
    my_index = lax.axis_index("seq")
    logit_scale = 1.0 / math.sqrt(head_width)
    group = 2
    group_count = blocks // group
    pair_width = 2 * head_width
    query_heads = head_major(queries, head_count, head_width)
    grad_heads = head_major(grad_out, head_count, head_width)
    packed = jnp.concatenate([key_rows, values], axis=1)
    padded = extended(packed, (("seq", 0),), WMAX * BLK)
    pair_heads = (
        padded.reshape(blocks + 2 * WMAX, BLK, 2, head_count, head_width)
        .transpose(3, 0, 1, 2, 4)
        .reshape(head_count, blocks + 2 * WMAX, BLK, pair_width)
    )
    local_pairs = pair_heads[:, WMAX : WMAX + blocks]
    owners = global_blocks // blocks
    local_spot = global_blocks % blocks
    stacked = jnp.concatenate([queries, key_rows, values, grad_out], axis=1)
    own_rows = jnp.stack(
        [
            lax.dynamic_slice_in_dim(stacked, local_spot[glob_index] * BLK, BLK, 0)
            for glob_index in range(globals_count)
        ]
    )
    owned_mask = (owners == my_index)[:, None, None]
    masked_rows = jnp.where(owned_mask, own_rows, jnp.zeros((), jnp.bfloat16))
    panels = lax.psum(masked_rows, "seq").astype(jnp.float32).astype(jnp.bfloat16)
    panel_heads = panels.reshape(globals_count, BLK, 4, head_count, head_width).transpose(
        2, 3, 0, 1, 4
    )
    glob_query = panel_heads[0]
    glob_grad = panel_heads[3]
    glob_pairs = jnp.concatenate([panel_heads[1], panel_heads[2]], axis=-1)
    requests = random_blocks.reshape(-1)
    request_count = requests.shape[0]
    capacity = max(2, -(-request_count // shards))
    targets = requests // blocks
    request_head = jnp.arange(request_count, dtype=jnp.int32) // (blocks * randoms)
    codes = request_head * blocks + requests % blocks
    positions = jnp.arange(request_count, dtype=jnp.int32)
    earlier = (targets[:, None] == targets[None, :]) & (positions[None, :] < positions[:, None])
    ranks = jnp.sum(earlier.astype(jnp.int32), axis=1)
    slots = targets * capacity + ranks
    outgoing = jnp.full((shards * capacity,), -1, jnp.int32).at[slots].set(codes)
    incoming = lax.all_to_all(
        outgoing.reshape(shards, capacity), "seq", split_axis=0, concat_axis=0, tiled=True
    ).reshape(-1)
    code_hits = (
        incoming[:, None] == jnp.arange(head_count * blocks, dtype=jnp.int32)[None, :]
    ).astype(jnp.bfloat16)
    flat_pairs = local_pairs.reshape(head_count * blocks, BLK, pair_width)
    reply = jnp.einsum(
        "sc,cid->sid", code_hits, flat_pairs, preferred_element_type=jnp.float32
    ).astype(jnp.bfloat16)
    fetched = lax.all_to_all(
        reply.reshape(shards, capacity, BLK, pair_width),
        "seq",
        split_axis=0,
        concat_axis=0,
        tiled=True,
    )
    slot_hits = (
        slots[:, None] == jnp.arange(shards * capacity, dtype=jnp.int32)[None, :]
    ).astype(jnp.bfloat16)
    random_pairs = (
        jnp.einsum(
            "rs,sid->rid",
            slot_hits,
            fetched.reshape(shards * capacity, BLK, pair_width),
            preferred_element_type=jnp.float32,
        )
        .astype(jnp.bfloat16)
        .reshape(head_count, blocks, randoms, BLK, pair_width)
    )
    offsets = jnp.arange(span, dtype=jnp.int32) - WMAX
    block_ids = my_index * blocks + jnp.arange(blocks, dtype=jnp.int32)
    reach = block_ids[:, None] + offsets[None, :]
    in_range = (reach >= 0) & (reach < shards * blocks)
    window_ok = in_range[None, :, :] & (
        jnp.abs(offsets)[None, None, :] <= window_width[:, None, None]
    )
    list_ok = jnp.concatenate(
        [window_ok, jnp.ones((head_count, blocks, globals_count + randoms), jnp.bool_)], axis=2
    )
    global_hit = block_ids[:, None] == global_blocks[None, :]
    row_global = jnp.any(global_hit, axis=1)
    hit_weight = global_hit.astype(jnp.float32)

    def key_sequence(first_block):
        pieces_list = [
            jnp.stack(
                [
                    lax.dynamic_slice_in_dim(pair_heads, first_block + offset, group, 1)
                    for offset in range(span)
                ],
                axis=2,
            )
        ]
        pieces_list.append(
            jnp.broadcast_to(
                glob_pairs[:, None], (head_count, group, globals_count, BLK, pair_width)
            )
        )
        pieces_list.append(random_pairs)
        joined = jnp.concatenate(pieces_list, axis=2)
        entry_count = joined.shape[2]
        list_mask = list_ok[:, :, :entry_count]
        return (
            joined.reshape(head_count, group, entry_count * BLK, pair_width),
            jnp.repeat(list_mask, BLK, axis=2),
        )

    def forward_group(group_index):
        first_block = group_index * group
        pairs, list_mask = key_sequence(first_block)
        key_part = pairs[..., :head_width]
        value_part = pairs[..., head_width:]
        score_matrix = (
            jnp.einsum("hqid,hqkd->hqik", query_heads, key_part, preferred_element_type=jnp.float32)
            * logit_scale
        )
        score_matrix = jnp.where(list_mask[:, :, None, :], score_matrix, -jnp.inf)
        row_max = jnp.max(score_matrix, axis=-1)
        weights = jnp.exp(score_matrix - row_max[..., None])
        totals = jnp.sum(weights, axis=-1)
        accumulated_total = jnp.einsum(
            "hqik,hqkd->hqid",
            weights.astype(jnp.bfloat16),
            value_part,
            preferred_element_type=jnp.float32,
        )
        return (
            (accumulated_total / totals[..., None]).astype(jnp.bfloat16),
            row_max + jnp.log(totals),
        )

    sparse_out, sparse_lse = lax.map(forward_group, jnp.arange(group_count))
    sparse_out = jnp.moveaxis(sparse_out, 0, 1).reshape(head_count, blocks, BLK, head_width)
    sparse_lse = jnp.moveaxis(sparse_lse, 0, 1).reshape(head_count, blocks, BLK)
    local_keys = local_pairs[..., :head_width].reshape(head_count, blocks * BLK, head_width)
    local_values = local_pairs[..., head_width:].reshape(head_count, blocks * BLK, head_width)
    glob_rows = glob_query.reshape(head_count, globals_count * BLK, head_width)
    glob_grad_rows = glob_grad.reshape(head_count, globals_count * BLK, head_width)
    glob_scores = (
        jnp.einsum("hid,hjd->hij", glob_rows, local_keys, preferred_element_type=jnp.float32)
        * logit_scale
    )
    glob_max = lax.pmax(jnp.max(glob_scores, axis=-1), "seq")
    glob_weights = jnp.exp(glob_scores - glob_max[..., None])
    glob_part_sum = jnp.einsum(
        "hij,hjd->hid",
        glob_weights.astype(jnp.bfloat16),
        local_values,
        preferred_element_type=jnp.float32,
    )
    glob_sum, glob_total = lax.psum((glob_part_sum, jnp.sum(glob_weights, axis=-1)), "seq")
    glob_out = (glob_sum / glob_total[..., None]).astype(jnp.bfloat16)
    glob_lse = glob_max + jnp.log(glob_total)
    chosen_out = jnp.einsum(
        "bg,hgid->hbid",
        hit_weight,
        glob_out.reshape(head_count, globals_count, BLK, head_width).astype(jnp.float32),
    )
    out_heads = jnp.where(
        row_global[None, :, None, None], chosen_out.astype(jnp.bfloat16), sparse_out
    )
    attn_out = token_major(out_heads)
    delta = jnp.sum(grad_heads.astype(jnp.float32) * out_heads.astype(jnp.float32), axis=-1)
    row_lse = jnp.where(row_global[None, :, None], jnp.inf, sparse_lse)
    glob_delta = jnp.sum(glob_grad_rows.astype(jnp.float32) * glob_out.astype(jnp.float32), axis=-1)

    def backward_group(group_index):
        first_block = group_index * group
        pairs, list_mask = key_sequence(first_block)
        key_part = pairs[..., :head_width]
        value_part = pairs[..., head_width:]
        score_matrix = (
            jnp.einsum("hqid,hqkd->hqik", query_heads, key_part, preferred_element_type=jnp.float32)
            * logit_scale
        )
        probs = jnp.where(list_mask[:, :, None, :], jnp.exp(score_matrix - row_lse[..., None]), 0.0)
        probability_gradient = jnp.einsum(
            "hqid,hqkd->hqik", grad_heads, value_part, preferred_element_type=jnp.float32
        )
        score_gradient = (probs * (probability_gradient - delta[..., None])).astype(jnp.bfloat16)
        grad_rows_part = (
            jnp.einsum(
                "hqik,hqkd->hqid", score_gradient, key_part, preferred_element_type=jnp.float32
            )
            * logit_scale
        )
        key_contributions = (
            jnp.einsum(
                "hqik,hqid->hqkd", score_gradient, query_heads, preferred_element_type=jnp.float32
            )
            * logit_scale
        )
        value_contributions = jnp.einsum(
            "hqik,hqid->hqkd",
            probs.astype(jnp.bfloat16),
            grad_heads,
            preferred_element_type=jnp.float32,
        )
        terms = jnp.concatenate([key_contributions, value_contributions], axis=-1).reshape(
            head_count, group, -1, BLK, pair_width
        )
        window_terms = terms[:, :, :span]
        glob_terms = jnp.sum(terms[:, :, span : span + globals_count], axis=1)
        random_terms = terms[:, :, span + globals_count :].astype(jnp.bfloat16)
        return (grad_rows_part, window_terms, glob_terms, random_terms)

    gradient_row_values, window_terms, glob_terms, random_terms = lax.map(
        backward_group, jnp.arange(group_count)
    )
    gradient_row_values = jnp.moveaxis(gradient_row_values, 0, 1).reshape(
        head_count, blocks, BLK, head_width
    )
    window_terms = jnp.moveaxis(window_terms, 0, 1).reshape(
        head_count, blocks, span, BLK, pair_width
    )
    glob_terms = jnp.sum(glob_terms, axis=0)
    spread = jnp.zeros((head_count, blocks + 2 * WMAX, BLK, pair_width), jnp.float32)
    for offset in range(span):
        spread = spread.at[:, offset : offset + blocks].add(window_terms[:, :, offset])
    glob_probs = jnp.exp(glob_scores - glob_lse[..., None])
    glob_grad_probs = jnp.einsum(
        "hid,hjd->hij", glob_grad_rows, local_values, preferred_element_type=jnp.float32
    )
    glob_grad_scores = (glob_probs * (glob_grad_probs - glob_delta[..., None])).astype(jnp.bfloat16)
    glob_query_part = (
        jnp.einsum("hij,hjd->hid", glob_grad_scores, local_keys, preferred_element_type=jnp.float32)
        * logit_scale
    )
    key_from_glob = (
        jnp.einsum("hij,hid->hjd", glob_grad_scores, glob_rows, preferred_element_type=jnp.float32)
        * logit_scale
    )
    value_from_glob = jnp.einsum(
        "hij,hid->hjd",
        glob_probs.astype(jnp.bfloat16),
        glob_grad_rows,
        preferred_element_type=jnp.float32,
    )
    glob_total_terms, glob_query_grad = lax.psum((glob_terms, glob_query_part), "seq")
    from_below = from_behind(spread[:, blocks + WMAX :], "seq", 1)
    from_above = from_behind(spread[:, :WMAX].astype(jnp.bfloat16), "seq", -1).astype(jnp.float32)
    own_terms = spread[:, WMAX : WMAX + blocks]
    own_terms = own_terms.at[:, :WMAX].add(from_below).at[:, blocks - WMAX :].add(from_above)
    own_terms = own_terms + jnp.concatenate([key_from_glob, value_from_glob], axis=-1).reshape(
        head_count, blocks, BLK, pair_width
    )
    own_terms = own_terms + jnp.einsum("bg,hgid->hbid", hit_weight, glob_total_terms)
    random_terms = jnp.moveaxis(random_terms, 0, 1).reshape(request_count, BLK, pair_width)
    outgoing_terms = (
        jnp.zeros((shards * capacity, BLK, pair_width), jnp.bfloat16).at[slots].set(random_terms)
    )
    returned = lax.all_to_all(
        outgoing_terms.reshape(shards, capacity, BLK, pair_width),
        "seq",
        split_axis=0,
        concat_axis=0,
        tiled=True,
    ).reshape(shards * capacity, BLK, pair_width)
    random_add = jnp.einsum(
        "sc,sid->cid", code_hits, returned, preferred_element_type=jnp.float32
    ).reshape(head_count, blocks, BLK, pair_width)
    own_terms = own_terms + random_add
    glob_query_add = jnp.einsum(
        "bg,hgid->hbid",
        hit_weight,
        glob_query_grad.reshape(head_count, globals_count, BLK, head_width),
    )
    grad_query = token_major((gradient_row_values + glob_query_add).astype(jnp.bfloat16))
    grad_key = token_major(own_terms[..., :head_width].astype(jnp.bfloat16))
    grad_value = token_major(own_terms[..., head_width:].astype(jnp.bfloat16))
    return (attn_out, grad_query, grad_key, grad_value)


MASKED = -1e30
ALIGNED = pl.DeviceIdType.MESH


NEXT, ACROSS, SKIP = 0, 1, 2
OUTER_IN = ((0, 2, ACROSS), (0, 2, SKIP), (0, 2, NEXT), (2, 2, ACROSS), (2, 2, SKIP), (2, 2, NEXT))
INNER_IN = ((0, 2, SKIP), (0, 2, NEXT), (2, 2, SKIP), (2, 2, NEXT))
TURNS = ((ACROSS, ACROSS), None, (NEXT, SKIP), (SKIP, NEXT))
OUTER_OUT = (((0, 2, ACROSS),), (), ((0, 2, NEXT),), ((0, 4, SKIP), (2, 2, ACROSS), (2, 2, NEXT)))
INNER_OUT = ((), (), ((0, 2, SKIP),), ((2, 2, SKIP), (0, 4, ACROSS), (0, 4, NEXT)))


def rows_dot(left, right):
    return lax.dot_general(left, right, (((1,), (1,)), ((), ())), preferred_element_type=jnp.float32)


def one_head_kernel(
    shards,
    blocks,
    width_in,
    global_in,
    random_in,
    k_in,
    v_in,
    q_in,
    g_in,
    out,
    width_ref,
    global_ref,
    random_ref,
    stage,
    in_all,
    bias_own,
    bias_all,
    out_all,
    dk_sum,
    dv_sum,
    stage_sem,
    pair_recv,
    rest_recv,
    in_send,
    bias_send,
    bias_recv,
    out_send,
    out_recv,
):
    me = lax.axis_index("seq")
    rows = blocks * BLK
    key_blocks = shards * blocks
    hd = in_all.shape[2]
    logit_scale = 1.0 / math.sqrt(hd)
    inner = ((me + 1) // 2) % 2
    partner = (me + 1 - 2 * (me % 2), 3 - me, (me + 2) % 4)
    arrays = (k_in, v_in, q_in, g_in)

    def pick(pair, table):
        first, second = table[pair[0]], table[pair[1]]
        return first + (second - first) * inner

    def cols(index):
        return pl.ds(pl.multiple_of(index * hd, hd), hd)

    def span(index):
        return pl.ds(pl.multiple_of(index * rows, rows), rows)

    def send_in(first, count, step, target):
        if count == 1:
            source, landing = arrays[first].at[:, cols(target)], in_all.at[first, span(me), :]
        else:
            source = stage.at[pl.ds(first, count), :, cols(target)]
            landing = in_all.at[pl.ds(first, count), span(me), :]
        return pltpu.make_async_remote_copy(
            src_ref=source,
            dst_ref=landing,
            send_sem=in_send,
            recv_sem=pair_recv if first < 2 else rest_recv.at[step],
            device_id={"seq": target},
            device_id_type=ALIGNED,
        )

    def send_bias(target):
        return pltpu.make_async_remote_copy(
            src_ref=bias_own.at[target],
            dst_ref=bias_all.at[me],
            send_sem=bias_send,
            recv_sem=bias_recv,
            device_id={"seq": target},
            device_id_type=ALIGNED,
        )

    def send_out(first, count, step):
        return pltpu.make_async_remote_copy(
            src_ref=out_all.at[pl.ds(first, count), span(partner[step]), :],
            dst_ref=out.at[pl.ds(first, count), :, cols(me)],
            send_sem=out_send,
            recv_sem=out_recv,
            device_id={"seq": partner[step]},
            device_id_type=ALIGNED,
        )

    def start_outs(turn):
        for role, table in enumerate((OUTER_OUT, INNER_OUT)):

            @pl.when(inner == role)
            def _():
                for first, count, step in table[turn]:
                    send_out(first, count, step).start()

    def wait_for(bytes_of, semaphore):
        pltpu.make_async_copy(bytes_of, bytes_of, semaphore).wait()

    small = [
        pltpu.make_async_copy(source, landing, semaphore)
        for source, landing, semaphore in (
            (width_in, width_ref, bias_send),
            (global_in, global_ref, out_send),
            (random_in, random_ref, out_recv),
        )
    ]
    staged = [
        pltpu.make_async_copy(array, stage.at[slot], stage_sem.at[slot // 2])
        for slot, array in enumerate(arrays)
    ]
    local_out = [
        pltpu.make_async_copy(
            out_all.at[pl.ds(2 * half, 2), span(me), :],
            out.at[pl.ds(2 * half, 2), :, cols(me)],
            out_recv,
        )
        for half in range(2)
    ]

    barrier = pltpu.get_barrier_semaphore()

    def greet(device):
        pl.semaphore_signal(barrier, inc=1, device_id={"seq": device}, device_id_type=ALIGNED)

    greet(3 - me)

    @pl.when(me != 2)
    def _():
        for copy in staged:
            copy.start()

    @pl.when(inner == 1)
    def _():
        pl.semaphore_wait(barrier, 1)

        @pl.when(me == 1)
        def _():
            wait_for(stage.at[pl.ds(0, 2)], stage_sem.at[0])
            send_in(0, 2, ACROSS, partner[ACROSS]).start()

        @pl.when(me == 2)
        def _():
            for slot in range(2):
                send_in(slot, 1, ACROSS, partner[ACROSS]).start()
            for copy in staged:
                copy.start()

        greet(0)
        greet(3)

    for copy in small:
        copy.start()

    @pl.when(me != 1)
    def _():
        wait_for(stage.at[pl.ds(0, 2)], stage_sem.at[0])

    wait_for(stage.at[pl.ds(2, 2)], stage_sem.at[1])

    @pl.when(inner == 1)
    def _():
        send_in(2, 2, ACROSS, partner[ACROSS]).start()

    for copy in small:
        copy.wait()

    lane = lax.broadcasted_iota(jnp.int32, (1, BLK), 1)
    spot_ids = jnp.zeros_like(lane)
    for spot in range(1, blocks):
        spot_ids += jnp.where(lane >= spot * key_blocks, 1, 0)
    key_ids = lane - spot_ids * key_blocks
    block_ids = me * blocks + spot_ids
    distance = jnp.abs(key_ids - block_ids)
    listed = jnp.zeros(lane.shape, jnp.float32)
    row_global = jnp.zeros(lane.shape, jnp.float32)
    for index in range(global_ref.shape[0]):
        listed += jnp.where(key_ids == global_ref[index], 1.0, 0.0)
        row_global = jnp.maximum(row_global, jnp.where(block_ids == global_ref[index], 1.0, 0.0))
    for head in range(shards):
        hits = listed + jnp.where(distance <= jnp.minimum(width_ref[head], WMAX), 1.0, 0.0)
        for index in range(random_ref.shape[0]):
            named = jnp.zeros_like(lane)
            for spot in range(blocks):
                named = jnp.where(spot_ids == spot, random_ref[index, spot, head], named)
            hits += jnp.where(key_ids == named, 1.0, 0.0)
        hits = row_global + (1.0 - row_global) * hits
        bias_own[head] = jnp.where(
            hits > 0.5, jnp.log(jnp.maximum(hits, 1.0)) * (1.0 / math.log(2.0)), MASKED
        )

    @pl.when(inner == 0)
    def _():
        pl.semaphore_wait(barrier, 3)
        greet(1)
        greet(2)
        for step, target in enumerate(partner):
            send_bias(target).start()
        for first, count, step in OUTER_IN:
            send_in(first, count, step, partner[step]).start()

    @pl.when(inner == 1)
    def _():
        pl.semaphore_wait(barrier, 2)
        for step, target in enumerate(partner):
            send_bias(target).start()
        for first, count, step in INNER_IN:
            send_in(first, count, step, partner[step]).start()

    bias_all[me] = bias_own[me]

    sub_ids = lax.broadcasted_iota(jnp.int32, (key_blocks, BLK), 0)
    lane_ids = lax.broadcasted_iota(jnp.int32, (key_blocks, BLK), 1)

    for slot in range(4):
        in_all[slot, span(me), :] = stage[slot, :, cols(me)]
    others = pl.ds(0, (shards - 1) * rows)
    wait_for(in_all.at[pl.ds(0, 2), others, :], pair_recv)
    wait_for(bias_all.at[pl.ds(0, shards - 1)], bias_recv)
    keys = in_all[0]
    vals = in_all[1]
    keys_t = keys.T
    vals_t = vals.T
    for turn, pair in enumerate(TURNS):
        if pair is None:
            chunk = me
        else:
            chunk, step = pick(pair, partner), pick(pair, (NEXT, ACROSS, SKIP))
            wait_for(in_all.at[pl.ds(2, 2), span(chunk), :], rest_recv.at[step])
        q = in_all[2, span(chunk), :]
        g = in_all[3, span(chunk), :]
        row = jnp.broadcast_to(bias_all[chunk], lane_ids.shape)
        spread = [
            jnp.broadcast_to(
                jnp.sum(
                    jnp.where(lane_ids == sub_ids + spot * key_blocks, row, 0.0),
                    axis=1,
                    keepdims=True,
                ),
                lane_ids.shape,
            )
            for spot in range(blocks)
        ]
        bias = jnp.concatenate(
            [
                jnp.concatenate(
                    [
                        jnp.broadcast_to(spread[spot][key : key + 1, :], (BLK, BLK))
                        for spot in range(blocks)
                    ],
                    axis=1,
                )
                for key in range(key_blocks)
            ],
            axis=0,
        )
        scores = rows_dot(keys, q) * (logit_scale / math.log(2.0)) + bias
        top = jnp.max(scores, axis=0, keepdims=True)
        weights = jnp.exp2(scores - top)
        inverse = 1.0 / jnp.sum(weights, axis=0, keepdims=True)
        out_t = (
            jnp.dot(vals_t, weights.astype(jnp.bfloat16), preferred_element_type=jnp.float32)
            * inverse
        )
        out_rows = out_t.T.astype(jnp.bfloat16)
        out_all[0, span(chunk), :] = out_rows
        delta = jnp.sum(
            (g.astype(jnp.float32) * out_rows.astype(jnp.float32)).T, axis=0, keepdims=True
        )
        probs = weights * inverse
        grads = (probs * (rows_dot(vals, g) - delta)).astype(jnp.bfloat16)
        dq_t = jnp.dot(keys_t, grads, preferred_element_type=jnp.float32) * logit_scale
        out_all[1, span(chunk), :] = dq_t.T.astype(jnp.bfloat16)
        if pair is None:
            local_out[0].start()
        if turn < shards - 1:
            start_outs(turn)
        dv_part = jnp.dot(probs.astype(jnp.bfloat16), g, preferred_element_type=jnp.float32)
        dk_part = jnp.dot(grads, q, preferred_element_type=jnp.float32)
        if turn == 0:
            dv_sum[...] = dv_part
            dk_sum[...] = dk_part
        elif turn < shards - 1:
            dv_sum[...] += dv_part
            dk_sum[...] += dk_part
        else:
            out_all[3] = (dv_sum[...] + dv_part).astype(jnp.bfloat16)
            out_all[2] = ((dk_sum[...] + dk_part) * logit_scale).astype(jnp.bfloat16)
    start_outs(shards - 1)
    local_out[1].start()
    wait_for(bias_own.at[pl.ds(0, shards - 1)], bias_send)
    wait_for(in_all.at[:, others, :], in_send)
    wait_for(out_all.at[:, others, :], out_send)
    wait_for(out, out_recv)


def deliver_kernel(landed, *refs):
    for slot in range(4):
        pltpu.make_async_copy(landed.at[slot], refs[slot], refs[4]).start()
    pltpu.make_async_copy(landed, landed, refs[4]).wait()


def one_head(queries, key_rows, values, grad_out, window_width, global_blocks, random_blocks):
    shards = lax.axis_size("seq")
    tokens, columns = queries.shape
    hd = columns // shards
    blocks = tokens // BLK
    whole = shards * tokens
    bf16 = jnp.bfloat16
    anywhere = pl.BlockSpec(memory_space=pl.ANY)
    dma = pltpu.SemaphoreType.DMA
    lists = (window_width, global_blocks, random_blocks.transpose(2, 1, 0))
    landed = pl.pallas_call(
        functools.partial(one_head_kernel, shards, blocks),
        out_shape=jax.ShapeDtypeStruct((4, tokens, columns), bf16),
        in_specs=[anywhere] * 7,
        out_specs=anywhere,
        scratch_shapes=[pltpu.SMEM(array.shape, jnp.int32) for array in lists]
        + [pltpu.VMEM((4, tokens, columns), bf16), pltpu.VMEM((4, whole, hd), bf16)]
        + [pltpu.VMEM((shards, 1, BLK), jnp.float32)] * 2
        + [pltpu.VMEM((4, whole, hd), bf16)]
        + [pltpu.VMEM((whole, hd), jnp.float32)] * 2
        + [dma((2,)), dma(()), dma((shards - 1,))]
        + [dma(())] * 5,
        compiler_params=pltpu.CompilerParams(
            collective_id=0, has_side_effects=True, vmem_limit_bytes=48 * 1024 * 1024
        ),
    )(
        *(
            pltpu.with_memory_space_constraint(array, pltpu.HBM)
            for array in (*lists, key_rows, values, queries, grad_out)
        )
    )
    return pl.pallas_call(
        deliver_kernel,
        out_shape=(jax.ShapeDtypeStruct((tokens, columns), bf16),) * 4,
        in_specs=[anywhere],
        out_specs=(anywhere,) * 4,
        scratch_shapes=[dma(())],
        compiler_params=pltpu.CompilerParams(vmem_limit_bytes=8 * 1024 * 1024),
    )(landed)


def dispatch(queries, key_rows, values, grad_out, window_width, global_blocks, random_blocks):
    shards = lax.axis_size("seq")
    if shards == 4 and window_width.shape[0] == shards and queries.shape[1] == shards * BLK:
        chosen = one_head
    else:
        chosen = on_device
    return chosen(
        queries, key_rows, values, grad_out, window_width, global_blocks, random_blocks
    )


def solution(mesh):
    in_specs = (
        P(("groups", "seq"), ("head", "sub")),
        P(("groups", "seq"), ("head", "sub")),
        P(("groups", "seq"), ("head", "sub")),
        P(("groups", "seq"), ("head", "sub")),
        P(("groups", "head", "sub")),
        P("groups"),
        P(("groups", "head", "sub"), "seq", None),
    )
    out_specs = (
        P(("groups", "seq"), ("head", "sub")),
        P(("groups", "seq"), ("head", "sub")),
        P(("groups", "seq"), ("head", "sub")),
        P(("groups", "seq"), ("head", "sub")),
    )
    return jax.shard_map(
        dispatch, mesh=mesh, in_specs=in_specs, out_specs=out_specs, check_vma=False
    )
```
